256 devices in a mesh: wide: 64 (over x, z, core), narrow: 4 (over y).
Axes of the slice: x: 4, y: 4, z: 8, core: 2. Of those that a mesh axis runs over, the one named last changes fastest.
Arguments:
- block: float32 [4, 8192, 512], P(None, 'wide', 'narrow'), may hold values from -6 to 6
- east_weight: float32 [8192, 512], P('wide', 'narrow'), may hold values from 0.2 to 5
- north_weight: float32 [8192, 512], P('wide', 'narrow'), may hold values from 0.2 to 5
- fine_groups: int32 [8192, 512], P('wide', 'narrow'), may hold values from 0 to 2047
- tiles_one: float32 [4096, 4, 128, 128], P(('wide', 'narrow')), as said below
- columns_one: int32 [4096, 3], P(('wide', 'narrow')), may hold values from 0 to 79
- live_one: int32 [4096, 3], P(('wide', 'narrow')), may hold values 0 or 1
- coarse_groups: int32 [524288], P(('wide', 'narrow')), may hold values from 0 to 255
- tiles_two: float32 [1024, 4, 64, 64], P(('wide', 'narrow')), as said below
- columns_two: int32 [1024, 3], P(('wide', 'narrow')), may hold values from 0 to 19
- live_two: int32 [1024, 3], P(('wide', 'narrow')), may hold values 0 or 1
- coarser_groups: int32 [65536], P(('wide', 'narrow')), may hold values from 0 to 31
- chain_forward: float32 [64, 128, 128], P('wide')
- chain_gain: float32 [64, 128, 128], P('wide')
- chain_backward: float32 [64, 128, 128], P('wide')
Outputs:
- corrected: float32 [4, 8192, 512], P(None, 'wide', 'narrow')
The draws below stay inside these ranges and needn't reach their ends.
Inputs may be any that keep to these rules, and one draw needn't show every extreme that they name: `tiles_one`: in every row tile, slot 0 is the tile of that row tile with itself, and its diagonal entries lie in 1 to 2. `tiles_two`: in every row tile, slot 0 is the tile of that row tile with itself, and its diagonal entries lie in 1 to 2.
All inputs are finite; a program needn't handle non-finite values. No bound on the sum of `live_one` or of `live_two` on one device may be relied on, other than what follows from the above.
Results may differ from the reference program's by a relative error of at most 0.0001.
Values sent between devices are 32-bit elements; how exact they have to be, the bound alone decides.
A program may use at most 128 MiB of HBM per device.

```python
import math
import jax
import jax.numpy as jnp
from jax import lax

GX = 128
GY = 128
COLS = 4
SLOTS = 4
TB1 = 128
TB2 = 64
NX0 = 8192
NY0 = 512
C1 = 2048
C2 = 256
C3L = 32
NT1 = 16
NT2 = 4
M3 = 128
CHAIN = 64
ROWS1 = 524288
ROWS2 = 65536
ROWS3 = 8192
TILES1 = 4096
TILES2 = 1024
N_WIDE = 64
N_NARROW = 4


def build_tiles(key, noise, tile_rows, tile_size):
    diagonal = jax.random.uniform(jax.random.fold_in(key, 7), (tile_rows, tile_size), jnp.float32, 1.0, 2.0)
    identity = jnp.eye(tile_size, dtype=jnp.float32)
    first_slot = (lax.broadcasted_iota(jnp.int32, (1, SLOTS, 1, 1), 1) == 0).astype(jnp.float32)
    marker = first_slot * identity
    return noise * (1.0 - marker) + marker * diagonal[:, None, :, None]


def draw_tiles_one(key, part):
    spread = 0.35 / math.sqrt(SLOTS * TB1)
    shape = (TILES1, SLOTS, TB1, TB1)
    noise = jax.random.normal(key, shape, jnp.float32) * spread
    return build_tiles(key, noise, TILES1, TB1)


def draw_tiles_two(key, part):
    spread = 0.35 / math.sqrt(SLOTS * TB2)
    shape = (TILES2, SLOTS, TB2, TB2)
    noise = jax.random.normal(key, shape, jnp.float32) * spread
    return build_tiles(key, noise, TILES2, TB2)


def coupling_draw(key):
    decay = 0.3 ** (1.0 / CHAIN)
    shape = (CHAIN, M3, M3)
    noise = jax.random.normal(key, shape, jnp.float32)
    return decay * noise / math.sqrt(M3)


def draw_chain_forward(key, part):
    return coupling_draw(jax.random.fold_in(key, 11))


def draw_chain_backward(key, part):
    return coupling_draw(jax.random.fold_in(key, 13))


def draw_chain_gain(key, part):
    shape = (CHAIN, M3, M3)
    noise = jax.random.normal(key, shape, jnp.float32)
    diagonal = jax.random.uniform(jax.random.fold_in(key, 5), (CHAIN, M3), jnp.float32, 0.5, 1.5)
    identity = jnp.eye(M3, dtype=jnp.float32)
    return identity[None] * diagonal[:, :, None] + 0.5 * noise / math.sqrt(M3)


def plant(values, rng, low, top_value):
    dims = values.shape
    spot = [jax.random.randint(jax.random.fold_in(rng, axis), (), 0, dims[axis]) for axis in range(len(dims))]
    values = values.at[tuple(spot)].set(low)
    longest = dims.index(max(dims))
    spot[longest] = (spot[longest] + 1) % dims[longest]
    return values.at[tuple(spot)].set(top_value)


def block_scale(key, extent, split, low, largest):
    gain, own = 1.0, jax.random.fold_in(key, 6)
    for position, shards_of in split:
        steps = jnp.exp(jax.random.uniform(jax.random.fold_in(own, position), (shards_of,), jnp.float32, low / len(split), largest / len(split)))
        gain = gain * jnp.repeat(steps, extent[position] // shards_of).reshape([-1 if axis == position else 1 for axis in range(len(extent))])
    return gain


def scatter_about(stream_key, extent, deviation, reach, split=(), kind=jnp.bfloat16):
    loudness = block_scale(stream_key, extent, split, -0.22, 0.18) if split else 1.0
    entries = jax.random.normal(stream_key, extent, jnp.float32) * deviation * loudness
    return jnp.minimum(jnp.maximum(entries, -reach), reach).astype(kind)


def setup_inputs(seed: int = 0) -> dict:
    arg_keys = jax.random.split(jax.random.key(seed), 16)
    block = scatter_about(arg_keys[0], (COLS, NX0, NY0), 1.0, 6.0, ((1, 64), (2, 4)), jnp.float32)
    east_weight = jnp.clip(jnp.exp(math.log(5.0) - 3.218876 * jax.random.uniform(arg_keys[1], (NX0, NY0), jnp.float32) ** block_scale(arg_keys[1], (NX0, NY0), ((0, 64), (1, 4)), -0.2, 0.2)), 0.2, 5.0)
    north_weight = jnp.clip(jnp.exp(math.log(5.0) - 3.218876 * jax.random.uniform(arg_keys[2], (NX0, NY0), jnp.float32) ** block_scale(arg_keys[2], (NX0, NY0), ((0, 64), (1, 4)), -0.2, 0.2)), 0.2, 5.0)
    fine_groups = plant(jax.random.randint(arg_keys[3], (NX0, NY0), 0, C1), jax.random.fold_in(arg_keys[3], 1), 0, C1 - 1).astype(jnp.int32)
    tiles_one = draw_tiles_one(jax.random.fold_in(arg_keys[15], 71), 0)
    columns_one = plant(jax.random.randint(arg_keys[5], (TILES1, SLOTS - 1), 0, 5 * NT1), jax.random.fold_in(arg_keys[5], 1), 0, (5 * NT1) - 1).astype(jnp.int32)
    live_one = plant((jax.random.randint(arg_keys[6], (TILES1, SLOTS - 1), 0, 3) < 2).astype(jnp.int32), jax.random.fold_in(arg_keys[6], 1), 0, 1)
    coarse_groups = plant(jax.random.randint(arg_keys[7], (ROWS1,), 0, C2), jax.random.fold_in(arg_keys[7], 1), 0, C2 - 1).astype(jnp.int32)
    tiles_two = draw_tiles_two(jax.random.fold_in(arg_keys[15], 71), 0)
    columns_two = plant(jax.random.randint(arg_keys[9], (TILES2, SLOTS - 1), 0, 5 * NT2), jax.random.fold_in(arg_keys[9], 1), 0, (5 * NT2) - 1).astype(jnp.int32)
    live_two = plant((jax.random.randint(arg_keys[10], (TILES2, SLOTS - 1), 0, 3) < 2).astype(jnp.int32), jax.random.fold_in(arg_keys[10], 1), 0, 1)
    coarser_groups = plant(jax.random.randint(arg_keys[11], (ROWS2,), 0, C3L), jax.random.fold_in(arg_keys[11], 1), 0, C3L - 1).astype(jnp.int32)
    chain_forward = draw_chain_forward(jax.random.fold_in(arg_keys[15], 71), 0)
    chain_gain = draw_chain_gain(jax.random.fold_in(arg_keys[15], 71), 0)
    chain_backward = draw_chain_backward(jax.random.fold_in(arg_keys[15], 71), 0)
    return dict(block=block, east_weight=east_weight, north_weight=north_weight, fine_groups=fine_groups, tiles_one=tiles_one, columns_one=columns_one, live_one=live_one, coarse_groups=coarse_groups, tiles_two=tiles_two, columns_two=columns_two, live_two=live_two, coarser_groups=coarser_groups, chain_forward=chain_forward, chain_gain=chain_gain, chain_backward=chain_backward)


shift_value = 0.1
jacobi_weight = 0.6
smooth_weight = 0.5


def fine_weights(east_weight, north_weight):
    row_index = lax.broadcasted_iota(jnp.int32, east_weight.shape, 0)
    column_index = lax.broadcasted_iota(jnp.int32, east_weight.shape, 1)
    east_live = jnp.where(row_index < NX0 - 1, east_weight, 0.0)
    north_live = jnp.where(column_index < NY0 - 1, north_weight, 0.0)
    west_live = jnp.pad(east_live, ((1, 0), (0, 0)))[:-1]
    south_live = jnp.pad(north_live, ((0, 0), (1, 0)))[:, :-1]
    diagonal = shift_value + east_live + west_live + north_live + south_live
    return east_live, west_live, north_live, south_live, diagonal


def combine_fine(field, padded, east_live, west_live, north_live, south_live):
    east_side = padded[:, 2:, 1:-1]
    west_side = padded[:, :-2, 1:-1]
    north_side = padded[:, 1:-1, 2:]
    south_side = padded[:, 1:-1, :-2]
    result = shift_value * field + east_live * (field - east_side) + west_live * (field - west_side)
    return result + north_live * (field - north_side) + south_live * (field - south_side)


def tile_product(tiles, blocks, picked):
    own_part = jnp.einsum("rab,crb->cra", tiles[:, 0], blocks, precision=lax.Precision.HIGHEST)
    other_part = jnp.einsum("rkab,crkb->cra", tiles[:, 1:], picked, precision=lax.Precision.HIGHEST)
    return (own_part + other_part).reshape(blocks.shape[0], -1)


def neighbour_targets(columns, tile_count):
    owner = lax.broadcasted_iota(jnp.int32, columns.shape, 0) // tile_count
    wide_pos = owner // N_NARROW
    narrow_pos = owner % N_NARROW
    slot_code = columns // tile_count
    local_tile = columns % tile_count
    step_wide = jnp.where(slot_code == 1, -1, jnp.where(slot_code == 2, 1, 0))
    step_narrow = jnp.where(slot_code == 3, -1, jnp.where(slot_code == 4, 1, 0))
    wide_to = wide_pos + step_wide
    narrow_to = narrow_pos + step_narrow
    inside = (wide_to >= 0) & (wide_to < N_WIDE) & (narrow_to >= 0) & (narrow_to < N_NARROW)
    target = (wide_to * N_NARROW + narrow_to) * tile_count + local_tile
    target = jnp.where(inside, target, 0).astype(jnp.int32)
    return target, inside


def coarse_apply(field, tiles, columns, live, tile_count):
    tile_size = tiles.shape[2]
    blocks = field.reshape(COLS, -1, tile_size)
    target, inside = neighbour_targets(columns, tile_count)
    picked = jnp.take(blocks, target.reshape(-1), axis=1)
    picked = picked.reshape(COLS, columns.shape[0], columns.shape[1], tile_size)
    usable = (inside & (live == 1)).astype(jnp.float32)
    picked = picked * usable[None, :, :, None]
    return tile_product(tiles, blocks, picked)


def segment_total(values, indices, segment_count):
    return jax.ops.segment_sum(values.T, indices, num_segments=segment_count).T


def smooth_cycle(level, right, levels, coarsest):
    if level == len(levels):
        return coarsest(right)
    apply_op, diagonal, restrict_op, prolong_op = levels[level]
    first_iter = jacobi_weight * right / diagonal
    second_iter = first_iter + jacobi_weight * (right - apply_op(first_iter)) / diagonal
    leftover = right - apply_op(second_iter)
    scaled = leftover / diagonal
    coarse_right = restrict_op(leftover - smooth_weight * apply_op(scaled))
    coarse_answer = smooth_cycle(level + 1, coarse_right, levels, coarsest)
    spread = prolong_op(coarse_answer)
    third_iter = second_iter + (spread - smooth_weight * apply_op(spread) / diagonal)
    fourth_iter = third_iter + jacobi_weight * (right - apply_op(third_iter)) / diagonal
    return fourth_iter + jacobi_weight * (right - apply_op(fourth_iter)) / diagonal


def reference(block, east_weight, north_weight, fine_groups, tiles_one, columns_one, live_one, coarse_groups, tiles_two, columns_two, live_two, coarser_groups, chain_forward, chain_gain, chain_backward):
    weights = fine_weights(east_weight, north_weight)
    row_index = lax.broadcasted_iota(jnp.int32, (NX0, NY0), 0)
    column_index = lax.broadcasted_iota(jnp.int32, (NX0, NY0), 1)
    owner = (row_index // GX) * N_NARROW + column_index // GY
    fine_ids = (owner * C1 + fine_groups).reshape(-1).astype(jnp.int32)
    ids_one = ((jnp.arange(ROWS1, dtype=jnp.int32) // C1) * C2 + coarse_groups).astype(jnp.int32)
    ids_two = ((jnp.arange(ROWS2, dtype=jnp.int32) // C2) * C3L + coarser_groups).astype(jnp.int32)

    def apply_fine(field):
        padded = jnp.pad(field, ((0, 0), (1, 1), (1, 1)))
        return combine_fine(field, padded, weights[0], weights[1], weights[2], weights[3])

    def restrict_fine(field):
        return segment_total(field.reshape(COLS, -1), fine_ids, ROWS1)

    def prolong_fine(coarse):
        return jnp.take(coarse, fine_ids, axis=1).reshape(COLS, NX0, NY0)

    def apply_one(field):
        return coarse_apply(field, tiles_one, columns_one, live_one, NT1)

    def restrict_one(field):
        return segment_total(field, ids_one, ROWS2)

    def prolong_one(coarse):
        return jnp.take(coarse, ids_one, axis=1)

    def apply_two(field):
        return coarse_apply(field, tiles_two, columns_two, live_two, NT2)

    def restrict_two(field):
        return segment_total(field, ids_two, ROWS3)

    def prolong_two(coarse):
        return jnp.take(coarse, ids_two, axis=1)

    def chain_solve(right):
        blocks = right.reshape(COLS, N_WIDE, M3).transpose(1, 2, 0)

        def forward(carry, items):
            forward_map, gain_map, piece_now = items
            result = jnp.dot(forward_map, carry, precision=lax.Precision.HIGHEST) + jnp.dot(gain_map, piece_now, precision=lax.Precision.HIGHEST)
            return result, result

        unused, ahead_all = lax.scan(forward, jnp.zeros((M3, COLS), jnp.float32), (chain_forward, chain_gain, blocks))

        def backward(carry, items):
            back_map, piece_now = items
            result = jnp.dot(back_map, carry, precision=lax.Precision.HIGHEST) + piece_now
            return result, result

        unused_two, behind_all = lax.scan(backward, jnp.zeros((M3, COLS), jnp.float32), (chain_backward, ahead_all), reverse=True)
        return behind_all.transpose(2, 0, 1).reshape(COLS, -1)

    diag_one = jnp.diagonal(tiles_one[:, 0], axis1=1, axis2=2).reshape(-1)
    diag_two = jnp.diagonal(tiles_two[:, 0], axis1=1, axis2=2).reshape(-1)
    levels = ((apply_fine, weights[4], restrict_fine, prolong_fine), (apply_one, diag_one, restrict_one, prolong_one), (apply_two, diag_two, restrict_two, prolong_two))
    return smooth_cycle(0, block, levels, chain_solve)
```

```python
import jax
import jax.numpy as jnp
from jax import lax
from jax.experimental import pallas as pl
from jax.experimental.pallas import tpu as pltpu
from jax.sharding import PartitionSpec as P

F32 = jnp.float32
BF16 = jnp.bfloat16
MESH_ID = pl.DeviceIdType.MESH
GX = 128
GY = 128
COLS = 4
NT1 = 16
NT2 = 4
C3L = 32
CORES = 2
CHIPS_Z = 8
TOP = 16
EXT_ROWS = 160
EXT_LANES = 256
WEST, EAST, SOUTH, NORTH = 0, 1, 2, 3
STEPS = ((-1, 0), (1, 0), (0, -1), (0, 1), (-1, -1), (-1, 1), (1, -1), (1, 1))
FACING = (1, 0, 3, 2, 7, 6, 5, 4)
shift_value = 0.1
jacobi_weight = 0.6
smooth_weight = 0.5


def iota(shape, dim):
    return lax.broadcasted_iota(jnp.int32, shape, dim)


def dot_nt(a, b):
    return lax.dot_general(a, b, (((1,), (1,)), ((), ())), preferred_element_type=F32)


def dot_nn(a, b):
    return lax.dot_general(a, b, (((1,), (0,)), ((), ())), preferred_element_type=F32)


def matmul(a, b):
    return jnp.dot(a, b, precision=lax.Precision.HIGHEST, preferred_element_type=F32)


def upper():
    return iota((8, 128), 0) < 4


def left():
    return iota((8, 128), 1) < 64


def rounded(v):
    return v.astype(BF16).astype(F32)


def fold(o):
    return o + pltpu.roll(o, 4, 0)


def split_twin(v):
    hi = rounded(v)
    return jnp.where(upper(), hi, v - hi)


def split_pair(v):
    hi = rounded(v)
    lo = v - hi
    first = jnp.where(upper(), hi, pltpu.roll(lo, 4, 0))
    second = jnp.where(upper(), pltpu.roll(hi, 4, 0), lo)
    return first, second


def store_split(ref, m):
    hi = m.astype(BF16)
    ref[:, 0:128] = hi
    ref[:, 128:256] = (m - hi.astype(F32)).astype(BF16)


def times(v, split_map):
    a = split_twin(v).astype(BF16)
    return fold(dot_nt(jnp.concatenate([a, a], axis=1), split_map))


def kernel(
    wide_size,
    narrow_size,
    block,
    east,
    north,
    fine_groups,
    tiles_one,
    columns_one,
    live_one,
    coarse_groups,
    tiles_two,
    columns_two,
    live_two,
    coarser_groups,
    chain_forward,
    chain_gain,
    chain_backward,
    out,
    ext,
    groups_hi,
    groups_lo,
    held_one,
    held_two,
    slabs,
    packs,
    fine_box,
    weight_e,
    weight_w,
    weight_n,
    weight_s,
    inverse,
    diagonal,
    field_a,
    field_b,
    field_c,
    second,
    high_rows,
    low_rows,
    segment,
    table,
    w_one,
    w_two,
    picks_one,
    picks_two,
    spots_one,
    spots_two,
    hot_one,
    hot_two,
    sent_one,
    sent_two,
    box_one,
    box_two,
    pair_maps,
    pair_split,
    own_split,
    z_maps,
    z_split,
    prefix_u,
    suffix_v,
    x_maps,
    x_split,
    last_split,
    box_rhs,
    box_z,
    box_x,
    enter_y,
    enter_x,
    local_sem,
    fine_send,
    fine_recv,
    send_one,
    recv_one,
    send_two,
    recv_two,
    core_send,
    core_recv,
    rhs_send,
    rhs_recv,
    zmap_send,
    zmap_recv,
    xmap_send,
    xmap_recv,
    z_send,
    z_recv,
    x_send,
    x_recv,
):
    w = lax.axis_index("wide")
    q = lax.axis_index("narrow")
    seg_size = CORES * CHIPS_Z
    segs = wide_size // seg_size
    xs = w // seg_size
    zs = lax.rem(w, seg_size) // CORES
    core = lax.rem(w, CORES)

    def place(step):
        return w + step[0], q + step[1]

    def exists(step):
        a, b = place(step)
        return (a >= 0) & (a < wide_size) & (b >= 0) & (b < narrow_size)

    loads = (
        (block, ext.at[pl.ds(0, 4), pl.ds(TOP, GX), pl.ds(0, GY)]),
        (east, ext.at[4, pl.ds(TOP, GX), pl.ds(0, GY)]),
        (north, ext.at[5, pl.ds(TOP, GX), pl.ds(0, GY)]),
        (chain_forward.at[0], pair_maps.at[core, 0]),
        (chain_gain.at[0], pair_maps.at[core, 1]),
        (chain_backward.at[0], pair_maps.at[core, 2]),
        (fine_groups, groups_lo),
        (tiles_two, held_two),
        (tiles_one, held_one),
    )
    local = [pltpu.make_async_copy(a, b, local_sem.at[i]) for i, (a, b) in enumerate(loads)]
    for c in local:
        c.start()

    barrier = pltpu.get_barrier_semaphore()
    awaited = jnp.int32(0)
    for step in STEPS:
        there = exists(step)
        a, b = place(step)

        @pl.when(there)
        def _():
            pl.semaphore_signal(barrier, inc=1, device_id=(a, b), device_id_type=MESH_ID)

        awaited = awaited + jnp.where(there, 1, 0)
    group = [(i, j) for i in range(CORES) for j in range(narrow_size)]
    for i, j in group[1:]:
        mate = (w - core + lax.rem(core + i, CORES), lax.rem(q + j, narrow_size))
        pl.semaphore_signal(barrier, inc=1, device_id=mate, device_id_type=MESH_ID)
    for i in range(1, CHIPS_Z):
        mate = (xs * seg_size + lax.rem(zs + i, CHIPS_Z) * CORES + core, q)
        pl.semaphore_signal(barrier, inc=1, device_id=mate, device_id_type=MESH_ID)
    for i in range(1, segs):
        mate = (lax.rem(xs + i, segs) * seg_size + zs * CORES + core, q)
        pl.semaphore_signal(barrier, inc=1, device_id=mate, device_id_type=MESH_ID)
    awaited = awaited + len(group) - 1 + CHIPS_Z - 1 + segs - 1

    def fine_start(turn, source, arrays):
        lane = iota((8, 128), 1) // 4
        for a in range(arrays):
            slabs[turn, 0, a] = source[a, TOP : TOP + 8, 0:128]
            slabs[turn, 1, a] = source[a, TOP + GX - 8 : TOP + GX, 0:128]
            packed = jnp.zeros((8, 128), F32)
            for g in range(GX // 8):
                v = source[a, TOP + 8 * g : TOP + 8 * g + 8, 0:128]
                packed = jnp.where(lane == g, v if g == 0 else pltpu.roll(v, 4 * g, 1), packed)
                packed = jnp.where(lane == 16 + g, pltpu.roll(v, (68 + 4 * g) % 128, 1), packed)
            packs[turn, a] = packed

    def fine_copy(turn, arrays, d, landing):
        span = pl.ds(0, arrays)
        source = slabs.at[turn, d, span] if d < 2 else packs.at[turn, span]
        return pltpu.make_async_remote_copy(
            src_ref=source,
            dst_ref=fine_box.at[turn, landing, span],
            send_sem=fine_send.at[turn, d],
            recv_sem=fine_recv.at[turn, landing],
            device_id=place(STEPS[d]),
            device_id_type=MESH_ID,
        )

    def fine_send_all(turn, arrays):
        for d, step in enumerate(STEPS):

            @pl.when(exists(step))
            def _():
                fine_copy(turn, arrays, d, FACING[d]).start()

    def fine_wait(turn, arrays):
        for d, step in enumerate(STEPS):

            @pl.when(exists(step))
            def _():
                fine_copy(turn, arrays, d, d).wait_recv()
                fine_copy(turn, arrays, d, FACING[d]).wait_send()

    def fine_fill(turn, target, arrays):
        lane = iota((8, 128), 1)
        there = [exists(step) for step in STEPS]

        def got(d, a):
            return jnp.where(there[d], fine_box[turn, d, a], 0.0)

        def beside(south_pack, south_group, north_pack, north_group):
            low = pltpu.roll(south_pack, (124 - 64 - 4 * south_group) % 128, 1)
            high = pltpu.roll(north_pack, (128 - 4 * north_group) % 128, 1)
            return jnp.where(lane < 4, high, jnp.where(lane >= 124, low, 0.0))

        for a in range(arrays):
            target[a, TOP - 8 : TOP, 0:128] = got(0, a)
            target[a, TOP + GX : TOP + GX + 8, 0:128] = got(1, a)
            south_pack, north_pack = got(2, a), got(3, a)
            for g in range(GX // 8):
                target[a, TOP + 8 * g : TOP + 8 * g + 8, 128:256] = beside(south_pack, g, north_pack, g)
            target[a, TOP - 8 : TOP, 128:256] = beside(got(4, a), 15, got(5, a), 15)
            target[a, TOP + GX : TOP + GX + 8, 128:256] = beside(got(6, a), 0, got(7, a), 0)

    local[0].wait()
    local[1].wait()
    local[2].wait()
    fine_start(0, ext, 6)
    pl.semaphore_wait(barrier, awaited)
    fine_send_all(0, 6)

    local[3].wait()
    local[4].wait()
    local[5].wait()

    def core_copy(landing):
        return pltpu.make_async_remote_copy(
            src_ref=pair_maps.at[core],
            dst_ref=pair_maps.at[landing],
            send_sem=core_send,
            recv_sem=core_recv,
            device_id=(w - core + (1 - core), q),
            device_id_type=MESH_ID,
        )

    core_copy(core).start()

    local[6].wait()
    groups = groups_lo[...]
    groups_hi[...] = groups // 128
    groups_lo[...] = lax.rem(groups, 128)
    for r in range(NT1):
        for k in range(3):
            spots_one[3 * r + k] = jnp.where(live_one[r, k] == 1, columns_one[r, k], 5 * NT1)
    for r in range(NT2):
        for k in range(3):
            spots_two[3 * r + k] = jnp.where(live_two[r, k] == 1, columns_two[r, k], 5 * NT2)
    picks_one[5 * NT1] = jnp.zeros((8, 128), F32)
    picks_two[5 * NT2] = jnp.zeros((8, 128), F32)
    local[7].wait()
    lane_two = iota((64, 128), 1)
    eye_two = iota((64, 128), 0) == lax.rem(lane_two, 64)
    diag_two = []
    for r in range(NT2):
        for k in range(4):
            m = held_two[r, k]
            m = jnp.concatenate([m, m], axis=1)
            if k == 0:
                diag_two.append(jnp.sum(jnp.where(eye_two, m, 0.0), axis=0, keepdims=True))
            hi = rounded(m)
            m = jnp.where(lane_two < 64, hi, m - hi).astype(BF16)
            w_two[r, 0:64, 128 * k : 128 * k + 128] = m
            w_two[r, 64:128, 128 * k : 128 * k + 128] = m
    wide_two = [jnp.broadcast_to(d, (8, 128)) for d in diag_two]
    inverse_two = 1.0 / jnp.where(
        upper(),
        jnp.where(left(), wide_two[0], wide_two[1]),
        jnp.where(left(), wide_two[2], wide_two[3]),
    )
    for t in range(NT1):
        hot = iota((256, 128), 0) == coarse_groups[t : t + 1, :]
        hot_one[:, 128 * t : 128 * t + 128] = jnp.where(hot, 1.0, 0.0).astype(BF16)
    for h in range(2):
        hot = iota((128, 128), 0) == coarser_groups[h : h + 1, :] + C3L * q
        hot_two[:, 128 * h : 128 * h + 128] = jnp.where(hot, 1.0, 0.0).astype(BF16)
    local[8].wait()

    eye_one = iota((128, 128), 0) == iota((128, 128), 1)

    def split_tiles(t, carry):
        diags = []
        for r in (t, t + 8):
            for k in range(4):
                m = held_one[r, k]
                if k == 0:
                    diags.append(jnp.sum(jnp.where(eye_one, m, 0.0), axis=0, keepdims=True))
                store_split(w_one.at[r, :, pl.ds(256 * k, 256)], m)
        low, high = (jnp.broadcast_to(d, (8, 128)) for d in diags)
        table[t] = 1.0 / jnp.where(upper(), low, high)
        return carry

    lax.fori_loop(0, 8, split_tiles, 0)
    inverse_one = table[...]

    fine_wait(0, 6)
    fine_fill(0, ext, 6)
    rows_all = range(8, EXT_ROWS - 8, 8)
    last_row = wide_size * GX - 1
    last_column = narrow_size * GY - 1
    lane_ext = iota((8, EXT_LANES), 1)
    column = q * GY + jnp.where(lane_ext < 192, lane_ext, lane_ext - EXT_LANES)
    for o in rows_all:
        row = w * GX + (o - TOP) + iota((8, EXT_LANES), 0)
        ext[4, o : o + 8, :] = jnp.where(row < last_row, ext[4, o : o + 8, :], 0.0)
        ext[5, o : o + 8, :] = jnp.where(column < last_column, ext[5, o : o + 8, :], 0.0)
    for o in rows_all:
        e = ext[4, o : o + 8, :]
        b = ext[4, o - 1 : o + 7, :]
        n = ext[5, o : o + 8, :]
        s = pltpu.roll(n, 1, 1)
        d = shift_value + e + b + n + s
        inv = 1.0 / d
        weight_e[o - 8 : o, :] = e * inv
        weight_w[o - 8 : o, :] = b * inv
        weight_n[o - 8 : o, :] = n * inv
        weight_s[o - 8 : o, :] = s * inv
        if TOP <= o < TOP + GX:
            diagonal[o - TOP : o - TOP + 8, :] = d[:, 0:128]
        for c in range(COLS):
            field_a[c, o : o + 8, :] = ext[c, o : o + 8, :] * inv

    def mixed(source, c, o):
        v = source[c, o : o + 8, :]
        a = weight_e[o - 8 : o, :] * source[c, o + 1 : o + 9, :]
        b = weight_w[o - 8 : o, :] * source[c, o - 1 : o + 7, :]
        n = weight_n[o - 8 : o, :] * pltpu.roll(v, EXT_LANES - 1, 1)
        s = weight_s[o - 8 : o, :] * pltpu.roll(v, 1, 1)
        return v, (a + b) + (n + s)

    rows_in = range(TOP, TOP + GX, 8)
    rest = 1.0 - jacobi_weight
    for o in rows_all:
        for c in range(COLS):
            v, m = mixed(field_a, c, o)
            field_b[c, o : o + 8, :] = rest * v + jacobi_weight * m
    for o in rows_all:
        for c in range(COLS):
            v, m = mixed(field_b, c, o)
            field_c[c, o : o + 8, :] = rest * v + jacobi_weight * m
    for o in rows_in:
        i = o - TOP
        for c in range(COLS):
            v, m = mixed(field_c, c, o)
            r = ((1.0 - smooth_weight) * v + smooth_weight * m)[:, 0:128] * diagonal[i : i + 8, :]
            both = field_a[c, o : o + 8, 0:128] + field_b[c, o : o + 8, 0:128]
            second[c, i : i + 8, :] = jacobi_weight * both
            hi = rounded(r)
            lo = r - hi
            for h in range(2):
                high_rows[pl.ds(8 * i + 4 * h + c, 8, stride=8), :] = hi
                low_rows[pl.ds(8 * i + 4 * h + c, 8, stride=8), :] = lo

    segment[...] = jnp.zeros((128, 128), F32)
    half = jnp.where(upper(), 0, 8)
    tall = iota((128, 128), 0)
    chunk = 8

    def gather_up(step, carry):
        lhs, rhs = [], []
        for j in range(chunk):
            i = step * chunk + j
            hi_index = jnp.broadcast_to(groups_hi[pl.ds(i, 1), :], (8, 128))
            lo_index = groups_lo[pl.ds(i, 1), :]
            at = pl.multiple_of(8 * i, 8)
            v_hi = high_rows[pl.ds(at, 8), :]
            v_lo = low_rows[pl.ds(at, 8), :]
            masks = [hi_index == half + t for t in range(8)]
            rows = [jnp.where(m, v_hi, 0.0) for m in masks] + [jnp.where(m, v_lo, 0.0) for m in masks]
            lhs.append(jnp.concatenate(rows, axis=0).astype(BF16))
            rhs.append(jnp.where(tall == lo_index, 1.0, 0.0).astype(BF16))
        segment[...] += dot_nt(jnp.concatenate(lhs, axis=1), jnp.concatenate(rhs, axis=1))
        return carry

    lax.fori_loop(0, GX // chunk, gather_up, 0)
    right_one = (segment[0:64, :] + segment[64:128, :]).reshape(8, 8, 128)

    def coarse_copy(sent, box, sends, receives, k, d, landing):
        return pltpu.make_async_remote_copy(
            src_ref=sent.at[k],
            dst_ref=box.at[k, landing],
            send_sem=sends.at[k, d],
            recv_sem=receives.at[k, landing],
            device_id=place(STEPS[d]),
            device_id_type=MESH_ID,
        )

    def coarse_send(bufs, k):
        for d in range(4):

            @pl.when(exists(STEPS[d]))
            def _():
                coarse_copy(*bufs, k, d, FACING[d]).start()

    def coarse_wait(bufs, k):
        for d in range(4):

            @pl.when(exists(STEPS[d]))
            def _():
                coarse_copy(*bufs, k, d, d).wait_recv()
                coarse_copy(*bufs, k, d, FACING[d]).wait_send()

    bufs_one = (sent_one, box_one, send_one, recv_one)
    bufs_two = (sent_two, box_two, send_two, recv_two)

    def put_one(p, t, v):
        a, b = split_pair(v)
        picks_one[NT1 * p + t] = a
        picks_one[NT1 * p + t + 8] = b

    def apply_one(k, field, meanwhile=None):
        sent_one[k] = field
        coarse_send(bufs_one, k)
        for t in range(8):
            put_one(0, t, field[t])
        own = []
        for r in range(NT1):
            a = picks_one[r].astype(BF16)
            own.append(dot_nt(jnp.concatenate([a, a], axis=1), w_one[r, :, 0:256]))
        own = [jnp.where(upper(), fold(own[t]), fold(own[t + 8])) for t in range(8)]
        if meanwhile is not None:
            meanwhile()
        coarse_wait(bufs_one, k)
        for d in range(4):
            there = exists(STEPS[d])
            for t in range(8):
                put_one(d + 1, t, jnp.where(there, box_one[k, d, t], 0.0))
        outs = []
        for r in range(NT1):
            parts = []
            for j in range(3):
                a = picks_one[spots_one[3 * r + j]].astype(BF16)
                parts += [a, a]
            outs.append(dot_nt(jnp.concatenate(parts, axis=1), w_one[r, :, 256:1024]))
        return jnp.stack(
            [own[t] + jnp.where(upper(), fold(outs[t]), fold(outs[t + 8])) for t in range(8)]
        )

    def put_two(p, v):
        for h, a in enumerate(split_pair(v)):
            turned = pltpu.roll(a, 64, 1)
            picks_two[NT2 * p + 2 * h] = jnp.where(left(), a, turned)
            picks_two[NT2 * p + 2 * h + 1] = jnp.where(left(), turned, a)

    def apply_two(k, field, meanwhile=None):
        sent_two[k] = field
        coarse_send(bufs_two, k)
        put_two(0, field)
        if meanwhile is not None:
            meanwhile()
        coarse_wait(bufs_two, k)
        for d in range(4):
            put_two(d + 1, jnp.where(exists(STEPS[d]), box_two[k, d], 0.0))
        outs = []
        for r in range(NT2):
            parts = [picks_two[r]] + [picks_two[spots_two[3 * r + j]] for j in range(3)]
            lhs = jnp.concatenate([a.astype(BF16) for a in parts], axis=1)
            outs.append(fold(dot_nt(lhs, w_two[r])))
        return jnp.where(
            upper(), jnp.where(left(), outs[0], outs[1]), jnp.where(left(), outs[2], outs[3])
        )

    def down(apply_op, inv, right, windows):
        s0 = inv * right
        r1 = right - jacobi_weight * apply_op(0, s0, windows[0])
        s1 = inv * r1
        r2 = r1 - jacobi_weight * apply_op(1, s1, windows[1])
        s2 = inv * r2
        r3 = r2 - smooth_weight * apply_op(2, s2, windows[2])
        return r3, r2, jacobi_weight * (s0 + s1)

    def up(apply_op, inv, spread, r2, x2):
        fix = spread - smooth_weight * (inv * apply_op(3, spread))
        r3 = r2 - apply_op(4, fix)
        s3 = inv * r3
        r4 = r3 - jacobi_weight * apply_op(5, s3)
        return x2 + fix + jacobi_weight * s3 + jacobi_weight * (inv * r4)

    def peer_copy(source, target, sends, receives, slot, landing, mate):
        return pltpu.make_async_remote_copy(
            src_ref=source,
            dst_ref=target.at[landing],
            send_sem=sends.at[slot],
            recv_sem=receives.at[landing],
            device_id=mate,
            device_id_type=MESH_ID,
        )

    def z_mate(i):
        z = lax.rem(zs + i, CHIPS_Z)
        return z, (xs * seg_size + z * CORES + core, q)

    def x_mate(i):
        x = lax.rem(xs + i, segs)
        return x, (x * seg_size + zs * CORES + core, q)

    def along(mates, count, box, sends, receives, mine):
        def start():
            for i in range(1, count):
                _, mate = mates(i)
                peer_copy(box.at[mine], box, sends, receives, i, mine, mate).start()

        def finish():
            for i in range(1, count):
                other, mate = mates(i)
                peer_copy(box.at[mine], box, sends, receives, i, other, mate).wait_recv()
                peer_copy(box.at[mine], box, sends, receives, i, mine, mate).wait_send()

        return start, finish

    zmap_start, zmap_finish = along(z_mate, CHIPS_Z, z_maps, zmap_send, zmap_recv, zs)
    xmap_start, xmap_finish = along(x_mate, segs, x_maps, xmap_send, xmap_recv, xs)
    z_start, z_finish = along(z_mate, CHIPS_Z, box_z, z_send, z_recv, zs)
    x_start, x_finish = along(x_mate, segs, box_x, x_send, x_recv, xs)

    def pair_products():
        core_copy(1 - core).wait_recv()
        core_copy(core).wait_send()
        f0, g0, b0 = pair_maps[0, 0], pair_maps[0, 1], pair_maps[0, 2]
        f1, g1, b1 = pair_maps[1, 0], pair_maps[1, 1], pair_maps[1, 2]
        both = matmul(f1, f0)
        z_maps[zs, 0] = both
        z_maps[zs, 1] = f0 + matmul(b0, both)
        z_maps[zs, 2] = matmul(b0, b1)
        zmap_start()

    def pair_gains():
        g0, b0 = pair_maps[0, 1], pair_maps[0, 2]
        f1, g1 = pair_maps[1, 0], pair_maps[1, 1]
        across = matmul(f1, g0)
        store_split(pair_split.at[0:128, 0:256], across)
        store_split(pair_split.at[0:128, 256:512], g1)
        store_split(pair_split.at[128:256, 0:256], g0 + matmul(b0, across))
        store_split(pair_split.at[128:256, 256:512], matmul(b0, g1))

    def z_prefix():
        zmap_finish()
        prefix_u[0] = jnp.where(eye_one, 1.0, 0.0)
        prefix_u[1] = z_maps[0, 0]

        def one(p, carry):
            prefix_u[p + 1] = matmul(z_maps[p, 0], prefix_u[p])
            return carry

        lax.fori_loop(1, CHIPS_Z, one, 0)
        x_maps[xs, 0] = prefix_u[CHIPS_Z]

    def z_suffix():
        suffix_v[CHIPS_Z, :, 0:128] = jnp.zeros((128, 128), F32)
        suffix_v[CHIPS_Z, :, 128:256] = jnp.where(eye_one, 1.0, 0.0)

        def one(i, carry):
            p = CHIPS_Z - 1 - i
            both = matmul(z_maps[p, 2], suffix_v[p + 1])
            suffix_v[p, :, 0:128] = both[:, 0:128] + matmul(z_maps[p, 1], prefix_u[p])
            suffix_v[p, :, 128:256] = both[:, 128:256]
            return carry

        lax.fori_loop(0, CHIPS_Z, one, 0)
        x_maps[xs, 1] = suffix_v[0, :, 0:128]
        x_maps[xs, 2] = suffix_v[0, :, 128:256]
        xmap_start()

    def z_splits():
        def one(p, carry):
            for j in range(3):
                store_split(z_split.at[p, j], z_maps[p, j])
            return carry

        lax.fori_loop(0, CHIPS_Z, one, 0)
        inner = core == 0
        first = jnp.where(inner, z_maps[zs, 1], z_maps[zs, 0])
        last = jnp.where(inner, z_maps[zs, 2], pair_maps[1, 2])
        store_split(own_split.at[:, 0:256], first)
        store_split(own_split.at[:, 256:512], last)
        both = matmul(last, suffix_v[zs + 1])
        store_split(last_split.at[:, 0:256], matmul(first, prefix_u[zs]) + both[:, 0:128])
        store_split(last_split.at[:, 256:512], both[:, 128:256])

    def x_splits():
        xmap_finish()
        for p in range(segs):
            for j in range(3):
                store_split(x_split.at[p, j], x_maps[p, j])

    def joined(a, b):
        a, b = split_twin(a).astype(BF16), split_twin(b).astype(BF16)
        return jnp.concatenate([a, a, b, b], axis=1)

    def sweep(count, maps, box):
        y = box[0, 0]
        enter_y[0] = jnp.zeros((8, 128), F32)
        lifted = [box[0, 1]]
        for p in range(1, count):
            enter_y[p] = y
            lifted.append(box[p, 1] + times(y, maps[p, 1]))
            y = box[p, 0] + times(y, maps[p, 0])
        x = lifted[count - 1]
        enter_x[count - 1] = jnp.zeros((8, 128), F32)
        for p in reversed(range(count - 1)):
            enter_x[p] = x
            x = lifted[p] + times(x, maps[p, 2])
        return y, x

    def chain_solve(piece):
        slot = core * narrow_size + q
        box_rhs[slot] = piece

        def rhs_copy(i, j, landing):
            mate = (w - core + lax.rem(core + i, CORES), lax.rem(q + j, narrow_size))
            return peer_copy(
                box_rhs.at[slot], box_rhs, rhs_send, rhs_recv, i * narrow_size + j, landing, mate
            )

        for i, j in group[1:]:
            rhs_copy(i, j, slot).start()
        for i, j in group[1:]:
            other = lax.rem(core + i, CORES) * narrow_size + lax.rem(q + j, narrow_size)
            rhs_copy(i, j, other).wait_recv()
            rhs_copy(i, j, slot).wait_send()
        sums = []
        for i in range(CORES):
            total = box_rhs[i * narrow_size]
            for j in range(1, narrow_size):
                total = total + box_rhs[i * narrow_size + j]
            sums.append(total)
        both = fold(dot_nt(joined(*sums), pair_split[...]))
        ahead, behind = both[:, 0:128], both[:, 128:256]
        box_z[zs, 0] = ahead
        box_z[zs, 1] = behind
        z_start()
        z_finish()
        y, x = sweep(CHIPS_Z, z_split, box_z)
        box_x[xs, 0] = y
        box_x[xs, 1] = x
        x_start()
        base = jnp.where(core == 0, behind, ahead)
        base = base + fold(dot_nt(joined(enter_y[zs], enter_x[zs]), own_split[...]))
        x_finish()
        sweep(segs, x_split, box_x)
        return base + fold(dot_nt(joined(enter_y[xs], enter_x[xs]), last_split[...]))

    def halves(pair):
        return jnp.concatenate([a.astype(BF16) for a in pair], axis=1)

    def pack_two(o):
        o = fold(o)
        return jnp.where(upper(), o[:, 0:128], o[:, 128:256])

    def restrict_one(field):
        pairs = [split_pair(field[t]) for t in range(8)]
        tiles = [p[0] for p in pairs] + [p[1] for p in pairs]
        return pack_two(dot_nt(halves(tiles), hot_one[...]))

    def prolong_one(coarse):
        o = fold(dot_nn(halves(split_pair(coarse)), hot_one[...]))
        parts = [o[:, 128 * t : 128 * t + 128] for t in range(NT1)]
        return jnp.stack([jnp.where(upper(), parts[t], parts[t + 8]) for t in range(8)])

    r_one, r2_one, x2_one = down(apply_one, inverse_one, right_one, (pair_products, pair_gains, None))
    right_two = restrict_one(r_one)
    r_two, r2_two, x2_two = down(apply_two, inverse_two, right_two, (z_prefix, z_suffix, z_splits))
    piece = fold(dot_nt(halves(split_pair(r_two)), hot_two[...]))
    x_splits()
    answer = chain_solve(piece)
    spread_two = pack_two(dot_nn(split_twin(answer).astype(BF16), hot_two[...]))
    answer_two = up(apply_two, inverse_two, spread_two, r2_two, x2_two)
    answer_one = up(apply_one, inverse_one, prolong_one(answer_two), r2_one, x2_one)
    table[...] = answer_one

    def spread_rows(k, carry):
        at = pl.multiple_of(8 * k, 8)
        hi_index = groups_hi[pl.ds(at, 8), :]
        lo_index = groups_lo[pl.ds(at, 8), :]
        for c in range(COLS):
            total = jnp.zeros((8, 128), F32)
            for t in range(NT1):
                j = 4 * (t // 8) + c
                row = jnp.broadcast_to(table[t % 8, j : j + 1, :], (8, 128))
                value = jnp.take_along_axis(row, lo_index, axis=1, mode="promise_in_bounds")
                total = jnp.where(hi_index == t, value, total)
            field_a[c, pl.ds(pl.multiple_of(TOP + at, 8), 8), 0:128] = total
        return carry

    lax.fori_loop(0, GX // 8, spread_rows, 0)
    fine_start(1, field_a, 4)
    fine_send_all(1, 4)
    fine_wait(1, 4)
    fine_fill(1, field_a, 4)
    for o in rows_all:
        for c in range(COLS):
            v, m = mixed(field_a, c, o)
            field_b[c, o : o + 8, :] = (1.0 - smooth_weight) * v + smooth_weight * m
    for o in rows_all:
        for c in range(COLS):
            v, m = mixed(field_b, c, o)
            field_a[c, o : o + 8, :] = field_c[c, o : o + 8, :] - v + m
    for o in rows_in:
        i = o - TOP
        for c in range(COLS):
            v, m = mixed(field_a, c, o)
            x3 = second[c, i : i + 8, :] + field_b[c, o : o + 8, 0:128]
            s4 = rest * v + jacobi_weight * m
            out[c, i : i + 8, :] = x3 + jacobi_weight * (v + s4)[:, 0:128]


def solution(mesh):
    wide_size, narrow_size = mesh.shape["wide"], mesh.shape["narrow"]
    segs = wide_size // (CORES * CHIPS_Z)

    def body(
        block,
        east,
        north,
        fine_groups,
        tiles_one,
        columns_one,
        live_one,
        coarse_groups,
        tiles_two,
        columns_two,
        live_two,
        coarser_groups,
        chain_forward,
        chain_gain,
        chain_backward,
    ):
        hbm = pl.BlockSpec(memory_space=pl.ANY)
        vmem = pl.BlockSpec(memory_space=pltpu.VMEM)
        smem = pl.BlockSpec(memory_space=pltpu.SMEM)
        dma = pltpu.SemaphoreType.DMA
        big = pltpu.VMEM((COLS, EXT_ROWS, EXT_LANES), F32)
        weight = pltpu.VMEM((EXT_ROWS - 16, EXT_LANES), F32)
        square = pltpu.VMEM((GX, GY), F32)
        indices = pltpu.VMEM((GX, GY), jnp.int32)

        def kernel_fn(*refs):
            kernel(wide_size, narrow_size, *refs)

        return pl.pallas_call(
            kernel_fn,
            out_shape=jax.ShapeDtypeStruct((COLS, GX, GY), F32),
            in_specs=[hbm] * 5 + [smem] * 2 + [vmem, hbm] + [smem] * 2 + [vmem] + [hbm] * 3,
            out_specs=vmem,
            scratch_shapes=[
                pltpu.VMEM((6, EXT_ROWS, EXT_LANES), F32),
                indices,
                indices,
                pltpu.VMEM((NT1, 4, 128, 128), F32),
                pltpu.VMEM((NT2, 4, 64, 64), F32),
                pltpu.VMEM((2, 2, 6, 8, 128), F32),
                pltpu.VMEM((2, 6, 8, 128), F32),
                pltpu.VMEM((2, 8, 6, 8, 128), F32),
                weight,
                weight,
                weight,
                weight,
                weight,
                square,
                big,
                big,
                big,
                pltpu.VMEM((COLS, GX, GY), F32),
                pltpu.VMEM((8 * GX, GY), F32),
                pltpu.VMEM((8 * GX, GY), F32),
                square,
                pltpu.VMEM((8, 8, 128), F32),
                pltpu.VMEM((NT1, 128, 1024), BF16),
                pltpu.VMEM((NT2, 128, 512), BF16),
                pltpu.VMEM((5 * NT1 + 1, 8, 128), F32),
                pltpu.VMEM((5 * NT2 + 1, 8, 128), F32),
                pltpu.SMEM((3 * NT1,), jnp.int32),
                pltpu.SMEM((3 * NT2,), jnp.int32),
                pltpu.VMEM((256, 2048), BF16),
                pltpu.VMEM((128, 256), BF16),
                pltpu.VMEM((6, 8, 8, 128), F32),
                pltpu.VMEM((6, 8, 128), F32),
                pltpu.VMEM((6, 4, 8, 8, 128), F32),
                pltpu.VMEM((6, 4, 8, 128), F32),
                pltpu.VMEM((CORES, 3, 128, 128), F32),
                pltpu.VMEM((256, 512), BF16),
                pltpu.VMEM((128, 512), BF16),
                pltpu.VMEM((CHIPS_Z, 3, 128, 128), F32),
                pltpu.VMEM((CHIPS_Z, 3, 128, 256), BF16),
                pltpu.VMEM((CHIPS_Z + 1, 128, 128), F32),
                pltpu.VMEM((CHIPS_Z + 1, 128, 256), F32),
                pltpu.VMEM((segs, 3, 128, 128), F32),
                pltpu.VMEM((segs, 3, 128, 256), BF16),
                pltpu.VMEM((128, 512), BF16),
                pltpu.VMEM((CORES * narrow_size, 8, 128), F32),
                pltpu.VMEM((CHIPS_Z, 2, 8, 128), F32),
                pltpu.VMEM((segs, 2, 8, 128), F32),
                pltpu.VMEM((CHIPS_Z, 8, 128), F32),
                pltpu.VMEM((CHIPS_Z, 8, 128), F32),
                dma((9,)),
                dma((2, 8)),
                dma((2, 8)),
                dma((6, 4)),
                dma((6, 4)),
                dma((6, 4)),
                dma((6, 4)),
                dma,
                dma,
                dma((CORES * narrow_size,)),
                dma((CORES * narrow_size,)),
                dma((CHIPS_Z,)),
                dma((CHIPS_Z,)),
                dma((segs,)),
                dma((segs,)),
                dma((CHIPS_Z,)),
                dma((CHIPS_Z,)),
                dma((segs,)),
                dma((segs,)),
            ],
            compiler_params=pltpu.CompilerParams(
                collective_id=0, has_side_effects=True, vmem_limit_bytes=56 * 1024 * 1024
            ),
            name="cycle",
        )(
            block,
            east,
            north,
            fine_groups,
            tiles_one,
            columns_one,
            live_one,
            coarse_groups.reshape(16, 128),
            tiles_two,
            columns_two,
            live_two,
            coarser_groups.reshape(2, 128),
            chain_forward,
            chain_gain,
            chain_backward,
        )

    both = ("wide", "narrow")
    placed = (
        P(None, "wide", "narrow"),
        P("wide", "narrow"),
        P("wide", "narrow"),
        P("wide", "narrow"),
        P(both, None, None, None),
        P(both, None),
        P(both, None),
        P(both),
        P(both, None, None, None),
        P(both, None),
        P(both, None),
        P(both),
        P("wide", None, None),
        P("wide", None, None),
        P("wide", None, None),
    )
    return jax.shard_map(
        body, mesh=mesh, in_specs=placed, out_specs=P(None, "wide", "narrow"), check_vma=False
    )
```

```python
import jax
import jax.numpy as jnp
from jax import lax
from jax.experimental import pallas as pl
from jax.experimental.pallas import tpu as pltpu
from jax.sharding import PartitionSpec as P

F32 = jnp.float32
BF16 = jnp.bfloat16
MESH_ID = pl.DeviceIdType.MESH
GX = 128
GY = 128
COLS = 4
NT1 = 16
NT2 = 4
C3L = 32
CORES = 2
CHIPS_Z = 8
TOP = 16
EXT_ROWS = 160
EXT_LANES = 256
WEST, EAST, SOUTH, NORTH = 0, 1, 2, 3
STEPS = ((-1, 0), (1, 0), (0, -1), (0, 1), (-1, -1), (-1, 1), (1, -1), (1, 1))
FACING = (1, 0, 3, 2, 7, 6, 5, 4)
shift_value = 0.1
jacobi_weight = 0.6
smooth_weight = 0.5


def iota(shape, dim):
    return lax.broadcasted_iota(jnp.int32, shape, dim)


def dot_nt(a, b):
    return lax.dot_general(a, b, (((1,), (1,)), ((), ())), preferred_element_type=F32)


def dot_nn(a, b):
    return lax.dot_general(a, b, (((1,), (0,)), ((), ())), preferred_element_type=F32)


def matmul(a, b):
    return jnp.dot(a, b, precision=lax.Precision.HIGHEST, preferred_element_type=F32)


def upper():
    return iota((8, 128), 0) < 4


def left():
    return iota((8, 128), 1) < 64


def rounded(v):
    return v.astype(BF16).astype(F32)


def fold(o):
    return o + pltpu.roll(o, 4, 0)


def split_twin(v):
    hi = rounded(v)
    return jnp.where(upper(), hi, v - hi)


def split_pair(v):
    hi = rounded(v)
    lo = v - hi
    first = jnp.where(upper(), hi, pltpu.roll(lo, 4, 0))
    second = jnp.where(upper(), pltpu.roll(hi, 4, 0), lo)
    return first, second


def store_split(ref, m):
    hi = m.astype(BF16)
    ref[:, 0:128] = hi
    ref[:, 128:256] = (m - hi.astype(F32)).astype(BF16)


def times(v, split_map):
    a = split_twin(v).astype(BF16)
    return fold(dot_nt(jnp.concatenate([a, a], axis=1), split_map))


def kernel(
    wide_size,
    narrow_size,
    block,
    east,
    north,
    fine_groups,
    tiles_one,
    columns_one,
    live_one,
    coarse_groups,
    tiles_two,
    columns_two,
    live_two,
    coarser_groups,
    chain_forward,
    chain_gain,
    chain_backward,
    out,
    ext,
    groups_hi,
    groups_lo,
    held_one,
    held_two,
    slabs,
    packs,
    fine_box,
    weight_e,
    weight_w,
    weight_n,
    weight_s,
    inverse,
    diagonal,
    field_a,
    field_b,
    field_c,
    second,
    high_rows,
    low_rows,
    segment,
    table,
    w_one,
    w_two,
    picks_one,
    picks_two,
    spots_one,
    spots_two,
    hot_one,
    hot_two,
    sent_one,
    sent_two,
    box_one,
    box_two,
    pair_maps,
    pair_split,
    pair_out,
    west_map,
    west_split,
    group_box,
    z_maps,
    z_split,
    prefix_u,
    suffix_v,
    suffix_w,
    x_maps,
    x_split,
    enter_split,
    box_rhs,
    box_z,
    box_x,
    enter_y,
    enter_x,
    local_sem,
    fine_send,
    fine_recv,
    send_one,
    recv_one,
    send_two,
    recv_two,
    core_send,
    core_recv,
    west_send,
    west_recv,
    group_send,
    group_recv,
    relay_send,
    relay_recv,
    rhs_send,
    rhs_recv,
    zmap_send,
    zmap_recv,
    xmap_send,
    xmap_recv,
    z_send,
    z_recv,
    x_send,
    x_recv,
):
    w = lax.axis_index("wide")
    q = lax.axis_index("narrow")
    seg_size = CORES * CHIPS_Z
    segs = wide_size // seg_size
    xs = w // seg_size
    zs = lax.rem(w, seg_size) // CORES
    core = lax.rem(w, CORES)

    def place(step):
        return w + step[0], q + step[1]

    def exists(step):
        a, b = place(step)
        return (a >= 0) & (a < wide_size) & (b >= 0) & (b < narrow_size)

    loads = (
        (block, ext.at[pl.ds(0, 4), pl.ds(TOP, GX), pl.ds(0, GY)]),
        (east, ext.at[4, pl.ds(TOP, GX), pl.ds(0, GY)]),
        (north, ext.at[5, pl.ds(TOP, GX), pl.ds(0, GY)]),
        (chain_forward.at[0], pair_maps.at[core, 0]),
        (chain_gain.at[0], pair_maps.at[core, 1]),
        (chain_backward.at[0], pair_maps.at[core, 2]),
        (fine_groups, groups_lo),
        (tiles_two, held_two),
        (tiles_one, held_one),
    )
    local = [pltpu.make_async_copy(a, b, local_sem.at[i]) for i, (a, b) in enumerate(loads)]
    for c in local:
        c.start()

    barrier = pltpu.get_barrier_semaphore()
    awaited = jnp.int32(0)
    for step in STEPS:
        there = exists(step)
        a, b = place(step)

        @pl.when(there)
        def _():
            pl.semaphore_signal(barrier, inc=1, device_id=(a, b), device_id_type=MESH_ID)

        awaited = awaited + jnp.where(there, 1, 0)
    group = [(i, j) for i in range(CORES) for j in range(narrow_size)]
    for i, j in group[1:]:
        mate = (w - core + lax.rem(core + i, CORES), lax.rem(q + j, narrow_size))
        pl.semaphore_signal(barrier, inc=1, device_id=mate, device_id_type=MESH_ID)
    for i in range(1, CHIPS_Z):
        mate = (xs * seg_size + lax.rem(zs + i, CHIPS_Z) * CORES + core, q)
        pl.semaphore_signal(barrier, inc=1, device_id=mate, device_id_type=MESH_ID)
    for i in range(1, segs):
        mate = (lax.rem(xs + i, segs) * seg_size + zs * CORES + core, q)
        pl.semaphore_signal(barrier, inc=1, device_id=mate, device_id_type=MESH_ID)
    awaited = awaited + len(group) - 1 + CHIPS_Z - 1 + segs - 1

    def fine_start(turn, source, arrays):
        lane = iota((8, 128), 1) // 4
        for a in range(arrays):
            slabs[turn, 0, a] = source[a, TOP : TOP + 8, 0:128]
            slabs[turn, 1, a] = source[a, TOP + GX - 8 : TOP + GX, 0:128]
            packed = jnp.zeros((8, 128), F32)
            for g in range(GX // 8):
                v = source[a, TOP + 8 * g : TOP + 8 * g + 8, 0:128]
                packed = jnp.where(lane == g, v if g == 0 else pltpu.roll(v, 4 * g, 1), packed)
                packed = jnp.where(lane == 16 + g, pltpu.roll(v, (68 + 4 * g) % 128, 1), packed)
            packs[turn, a] = packed

    def fine_copy(turn, arrays, d, landing):
        span = pl.ds(0, arrays)
        source = slabs.at[turn, d, span] if d < 2 else packs.at[turn, span]
        return pltpu.make_async_remote_copy(
            src_ref=source,
            dst_ref=fine_box.at[turn, landing, span],
            send_sem=fine_send.at[turn, d],
            recv_sem=fine_recv.at[turn, landing],
            device_id=place(STEPS[d]),
            device_id_type=MESH_ID,
        )

    def fine_send_all(turn, arrays):
        for d, step in enumerate(STEPS):

            @pl.when(exists(step))
            def _():
                fine_copy(turn, arrays, d, FACING[d]).start()

    def fine_wait(turn, arrays):
        for d, step in enumerate(STEPS):

            @pl.when(exists(step))
            def _():
                fine_copy(turn, arrays, d, d).wait_recv()
                fine_copy(turn, arrays, d, FACING[d]).wait_send()

    def fine_fill(turn, target, arrays):
        lane = iota((8, 128), 1)
        there = [exists(step) for step in STEPS]

        def got(d, a):
            return jnp.where(there[d], fine_box[turn, d, a], 0.0)

        def beside(south_pack, south_group, north_pack, north_group):
            low = pltpu.roll(south_pack, (124 - 64 - 4 * south_group) % 128, 1)
            high = pltpu.roll(north_pack, (128 - 4 * north_group) % 128, 1)
            return jnp.where(lane < 4, high, jnp.where(lane >= 124, low, 0.0))

        for a in range(arrays):
            target[a, TOP - 8 : TOP, 0:128] = got(0, a)
            target[a, TOP + GX : TOP + GX + 8, 0:128] = got(1, a)
            south_pack, north_pack = got(2, a), got(3, a)
            for g in range(GX // 8):
                target[a, TOP + 8 * g : TOP + 8 * g + 8, 128:256] = beside(south_pack, g, north_pack, g)
            target[a, TOP - 8 : TOP, 128:256] = beside(got(4, a), 15, got(5, a), 15)
            target[a, TOP + GX : TOP + GX + 8, 128:256] = beside(got(6, a), 0, got(7, a), 0)

    local[0].wait()
    local[1].wait()
    local[2].wait()
    fine_start(0, ext, 6)
    pl.semaphore_wait(barrier, awaited)
    fine_send_all(0, 6)

    local[3].wait()
    local[4].wait()
    local[5].wait()

    def core_copy(landing):
        return pltpu.make_async_remote_copy(
            src_ref=pair_maps.at[core],
            dst_ref=pair_maps.at[landing],
            send_sem=core_send,
            recv_sem=core_recv,
            device_id=(w - core + (1 - core), q),
            device_id_type=MESH_ID,
        )

    def west_copy():
        return pltpu.make_async_remote_copy(
            src_ref=pair_maps.at[core, 2],
            dst_ref=west_map,
            send_sem=west_send,
            recv_sem=west_recv,
            device_id=(w + 1, q),
            device_id_type=MESH_ID,
        )

    def group_copy(d, landing):
        return pltpu.make_async_remote_copy(
            src_ref=coarser_groups,
            dst_ref=group_box.at[landing],
            send_sem=group_send.at[d],
            recv_sem=group_recv.at[landing],
            device_id=place(STEPS[d]),
            device_id_type=MESH_ID,
        )

    feeds_east = (core == CORES - 1) & (w < wide_size - 1)
    fed_from_west = (core == 0) & (w > 0)
    core_copy(core).start()

    @pl.when(feeds_east)
    def _():
        west_copy().start()

    for d in range(4):

        @pl.when(exists(STEPS[d]))
        def _():
            group_copy(d, FACING[d]).start()


    eye_one = iota((128, 128), 0) == iota((128, 128), 1)

    def peer_copy(source, target, sends, receives, slot, landing, mate):
        return pltpu.make_async_remote_copy(
            src_ref=source,
            dst_ref=target.at[landing],
            send_sem=sends.at[slot],
            recv_sem=receives.at[landing],
            device_id=mate,
            device_id_type=MESH_ID,
        )

    def z_mate(i):
        z = lax.rem(zs + i, CHIPS_Z)
        return z, (xs * seg_size + z * CORES + core, q)

    def x_mate(i):
        x = lax.rem(xs + i, segs)
        return x, (x * seg_size + zs * CORES + core, q)

    def along(mates, count, box, sends, receives, mine):
        def start():
            for i in range(1, count):
                _, mate = mates(i)
                peer_copy(box.at[mine], box, sends, receives, i, mine, mate).start()

        def finish():
            for i in range(1, count):
                other, mate = mates(i)
                peer_copy(box.at[mine], box, sends, receives, i, other, mate).wait_recv()
                peer_copy(box.at[mine], box, sends, receives, i, mine, mate).wait_send()

        return start, finish

    z_start, z_finish = along(z_mate, CHIPS_Z, box_z, z_send, z_recv, zs)
    x_start, x_finish = along(x_mate, segs, box_x, x_send, x_recv, xs)
    z_order = (1, 7, 2, 6, 3, 5, 4)

    def zmap_copy(i, landing, mate):
        half = pl.ds(pl.multiple_of(192 * core, 64), 192)
        return pltpu.make_async_remote_copy(
            src_ref=z_maps.at[zs, half],
            dst_ref=z_maps.at[landing, half],
            send_sem=zmap_send.at[i],
            recv_sem=zmap_recv.at[landing],
            device_id=mate,
            device_id_type=MESH_ID,
        )

    def relay_copy(z, side):
        half = pl.ds(pl.multiple_of(192 * side, 64), 192)
        return pltpu.make_async_remote_copy(
            src_ref=z_maps.at[z, half],
            dst_ref=z_maps.at[z, half],
            send_sem=relay_send.at[z],
            recv_sem=relay_recv.at[z],
            device_id=(w - core + (1 - core), q),
            device_id_type=MESH_ID,
        )

    def pair_products():
        core_copy(1 - core).wait_recv()
        core_copy(core).wait_send()
        f0, b0 = pair_maps[0, 0], pair_maps[0, 2]
        f1, b1 = pair_maps[1, 0], pair_maps[1, 2]
        both = matmul(f1, f0)
        z_maps[zs, 0:128] = both
        z_maps[zs, 128:256] = matmul(b0, b1)
        z_maps[zs, 256:384] = f0 + matmul(b0, both)
        for i in z_order:
            _, mate = z_mate(i)
            zmap_copy(i, zs, mate).start()

    def pair_gains():
        g0, b0 = pair_maps[0, 1], pair_maps[0, 2]
        f1, g1 = pair_maps[1, 0], pair_maps[1, 1]
        across = matmul(f1, g0)
        store_split(pair_split.at[0:128, 0:256], across)
        store_split(pair_split.at[0:128, 256:512], g1)
        store_split(pair_split.at[128:256, 0:256], g0 + matmul(b0, across))
        store_split(pair_split.at[128:256, 256:512], matmul(b0, g1))

    def zmap_relay():
        for i in z_order:
            other, mate = z_mate(i)
            zmap_copy(i, other, mate).wait_recv()
            relay_copy(other, core).start()

    def times_map(split_map, m):
        hi = m.astype(BF16)
        lo = (m - hi.astype(F32)).astype(BF16)
        lhs = jnp.concatenate([split_map, split_map[:, 0:128]], axis=1)
        return dot_nn(lhs, jnp.concatenate([hi, hi, lo], axis=0))

    def z_prefix():
        for i in z_order:
            other, mate = z_mate(i)
            zmap_copy(i, zs, mate).wait_send()
            relay_copy(other, 1 - core).wait_recv()
            relay_copy(other, core).wait_send()

        def split_one(p, carry):
            for j in range(3):
                store_split(z_split.at[p, j], z_maps[p, 128 * j : 128 * j + 128])
            return carry

        lax.fori_loop(0, CHIPS_Z, split_one, 0)
        one_map = jnp.where(eye_one, 1.0, 0.0)
        prefix_u[0] = one_map
        suffix_w[CHIPS_Z] = one_map

        def one(p, carry):
            prefix_u[p + 1] = times_map(z_split[p, 0], prefix_u[p])
            r = CHIPS_Z - 1 - p
            suffix_w[r] = times_map(z_split[r, 1], suffix_w[r + 1])
            return carry

        lax.fori_loop(0, CHIPS_Z, one, 0)
        x_maps[xs, 0] = prefix_u[CHIPS_Z]
        x_maps[xs, 1] = suffix_w[0]

    def xmap_copy(part, i, landing, mate):
        span = pl.ds(0, 2) if part == 0 else pl.ds(2, 1)
        return pltpu.make_async_remote_copy(
            src_ref=x_maps.at[xs, span],
            dst_ref=x_maps.at[landing, span],
            send_sem=xmap_send.at[part, i],
            recv_sem=xmap_recv.at[part, landing],
            device_id=mate,
            device_id_type=MESH_ID,
        )

    def has_map(part, x):
        return (x > 0) & (x < segs - 1) if part == 0 else x > 0

    def z_suffix():
        suffix_v[CHIPS_Z] = jnp.zeros((128, 128), F32)

        def one(i, carry):
            p = CHIPS_Z - 1 - i
            suffix_v[p] = times_map(z_split[p, 1], suffix_v[p + 1]) + times_map(
                z_split[p, 2], prefix_u[p]
            )
            return carry

        lax.fori_loop(0, CHIPS_Z, one, 0)
        x_maps[xs, 2] = suffix_v[0]
        for part in range(2):
            for i in range(1, segs):
                _, mate = x_mate(i)

                @pl.when(has_map(part, xs))
                def _():
                    xmap_copy(part, i, xs, mate).start()

    def z_splits():
        store_split(enter_split.at[0], prefix_u[zs])
        store_split(enter_split.at[1], suffix_v[zs + 1])
        store_split(enter_split.at[2], suffix_w[zs + 1])
        pair_out[0:128, 0:256] = z_split[zs, 2]
        pair_out[0:128, 256:512] = z_split[zs, 1]
        pair_out[128:256, 0:256] = z_split[zs, 0]
        store_split(pair_out.at[128:256, 256:512], pair_maps[1, 2])

        @pl.when(fed_from_west)
        def _():
            west_copy().wait_recv()

        @pl.when(feeds_east)
        def _():
            west_copy().wait_send()

        store_split(west_split, west_map[...])
        for d in range(4):

            @pl.when(exists(STEPS[d]))
            def _():
                group_copy(d, d).wait_recv()
                group_copy(d, FACING[d]).wait_send()

            mark_two(d + 1, group_box[d], q + STEPS[d][1])

    def x_splits():
        for part in range(2):
            for i in range(1, segs):
                other, mate = x_mate(i)

                @pl.when(has_map(part, other))
                def _():
                    xmap_copy(part, i, other, mate).wait_recv()

                @pl.when(has_map(part, xs))
                def _():
                    xmap_copy(part, i, xs, mate).wait_send()

        for p in range(1, segs):
            for j in range(3):
                if j == 2 or p < segs - 1:
                    store_split(x_split.at[p, j], x_maps[p, j])

    local[6].wait()
    groups = groups_lo[...]
    groups_hi[...] = groups // 128
    groups_lo[...] = lax.rem(groups, 128)
    for r in range(NT1):
        for k in range(3):
            spots_one[3 * r + k] = jnp.where(live_one[k, r] == 1, columns_one[k, r], 5 * NT1)
    for r in range(NT2):
        for k in range(3):
            spots_two[3 * r + k] = jnp.where(live_two[r, k] == 1, columns_two[r, k], 5 * NT2)
    picks_one[5 * NT1] = jnp.zeros((8, 128), F32)
    picks_two[5 * NT2] = jnp.zeros((8, 128), F32)
    local[7].wait()
    lane_two = iota((64, 128), 1)
    eye_two = iota((64, 128), 0) == lax.rem(lane_two, 64)
    diag_two = []
    for r in range(NT2):
        for k in range(4):
            m = held_two[r, k]
            m = jnp.concatenate([m, m], axis=1)
            if k == 0:
                diag_two.append(jnp.sum(jnp.where(eye_two, m, 0.0), axis=0, keepdims=True))
            hi = rounded(m)
            m = jnp.where(lane_two < 64, hi, m - hi).astype(BF16)
            w_two[r, 0:64, 128 * k : 128 * k + 128] = m
            w_two[r, 64:128, 128 * k : 128 * k + 128] = m
    wide_two = [jnp.broadcast_to(d, (8, 128)) for d in diag_two]
    inverse_two = 1.0 / jnp.where(
        upper(),
        jnp.where(left(), wide_two[0], wide_two[1]),
        jnp.where(left(), wide_two[2], wide_two[3]),
    )
    for t in range(NT1):
        hot = iota((256, 128), 0) == coarse_groups[t : t + 1, :]
        hot_one[:, 128 * t : 128 * t + 128] = jnp.where(hot, 1.0, 0.0).astype(BF16)

    def mark_two(p, groups, owner):
        for h in range(2):
            hot = iota((128, 128), 0) == groups[h : h + 1, :] + C3L * owner
            hot_two[p, :, 128 * h : 128 * h + 128] = jnp.where(hot, 1.0, 0.0).astype(BF16)

    mark_two(0, coarser_groups[...], q)
    pair_products()
    local[8].wait()

    def split_tiles(t, carry):
        diags = []
        for r in (t, t + 8):
            for k in range(4):
                m = held_one[r, k]
                if k == 0:
                    diags.append(jnp.sum(jnp.where(eye_one, m, 0.0), axis=0, keepdims=True))
                store_split(w_one.at[r, :, pl.ds(256 * k, 256)], m)
        low, high = (jnp.broadcast_to(d, (8, 128)) for d in diags)
        table[t] = 1.0 / jnp.where(upper(), low, high)
        return carry

    lax.fori_loop(0, 8, split_tiles, 0)
    inverse_one = table[...]
    pair_gains()

    fine_wait(0, 6)
    fine_fill(0, ext, 6)
    rows_all = range(8, EXT_ROWS - 8, 8)
    last_row = wide_size * GX - 1
    last_column = narrow_size * GY - 1
    lane_ext = iota((8, EXT_LANES), 1)
    column = q * GY + jnp.where(lane_ext < 192, lane_ext, lane_ext - EXT_LANES)
    for o in rows_all:
        row = w * GX + (o - TOP) + iota((8, EXT_LANES), 0)
        ext[4, o : o + 8, :] = jnp.where(row < last_row, ext[4, o : o + 8, :], 0.0)
        ext[5, o : o + 8, :] = jnp.where(column < last_column, ext[5, o : o + 8, :], 0.0)
    for o in rows_all:
        e = ext[4, o : o + 8, :]
        b = ext[4, o - 1 : o + 7, :]
        n = ext[5, o : o + 8, :]
        s = pltpu.roll(n, 1, 1)
        d = shift_value + e + b + n + s
        inv = 1.0 / d
        weight_e[o - 8 : o, :] = e * inv
        weight_w[o - 8 : o, :] = b * inv
        weight_n[o - 8 : o, :] = n * inv
        weight_s[o - 8 : o, :] = s * inv
        if TOP <= o < TOP + GX:
            diagonal[o - TOP : o - TOP + 8, :] = d[:, 0:128]
        for c in range(COLS):
            field_a[c, o : o + 8, :] = ext[c, o : o + 8, :] * inv

    def mixed(source, c, o):
        v = source[c, o : o + 8, :]
        a = weight_e[o - 8 : o, :] * source[c, o + 1 : o + 9, :]
        b = weight_w[o - 8 : o, :] * source[c, o - 1 : o + 7, :]
        n = weight_n[o - 8 : o, :] * pltpu.roll(v, EXT_LANES - 1, 1)
        s = weight_s[o - 8 : o, :] * pltpu.roll(v, 1, 1)
        return v, (a + b) + (n + s)

    rows_in = range(TOP, TOP + GX, 8)
    rest = 1.0 - jacobi_weight
    for o in rows_all:
        for c in range(COLS):
            v, m = mixed(field_a, c, o)
            field_b[c, o : o + 8, :] = rest * v + jacobi_weight * m
    for o in rows_all:
        for c in range(COLS):
            v, m = mixed(field_b, c, o)
            field_c[c, o : o + 8, :] = rest * v + jacobi_weight * m
    for o in rows_in:
        i = o - TOP
        for c in range(COLS):
            v, m = mixed(field_c, c, o)
            r = ((1.0 - smooth_weight) * v + smooth_weight * m)[:, 0:128] * diagonal[i : i + 8, :]
            both = field_a[c, o : o + 8, 0:128] + field_b[c, o : o + 8, 0:128]
            second[c, i : i + 8, :] = jacobi_weight * both
            hi = rounded(r)
            lo = r - hi
            for h in range(2):
                high_rows[pl.ds(8 * i + 4 * h + c, 8, stride=8), :] = hi
                low_rows[pl.ds(8 * i + 4 * h + c, 8, stride=8), :] = lo

    segment[...] = jnp.zeros((128, 128), F32)
    half = jnp.where(upper(), 0, 8)
    tall = iota((128, 128), 0)
    chunk = 8

    def gather_up(step, carry):
        lhs, rhs = [], []
        for j in range(chunk):
            i = step * chunk + j
            hi_index = jnp.broadcast_to(groups_hi[pl.ds(i, 1), :], (8, 128))
            lo_index = groups_lo[pl.ds(i, 1), :]
            at = pl.multiple_of(8 * i, 8)
            v_hi = high_rows[pl.ds(at, 8), :]
            v_lo = low_rows[pl.ds(at, 8), :]
            masks = [hi_index == half + t for t in range(8)]
            rows = [jnp.where(m, v_hi, 0.0) for m in masks] + [jnp.where(m, v_lo, 0.0) for m in masks]
            lhs.append(jnp.concatenate(rows, axis=0).astype(BF16))
            rhs.append(jnp.where(tall == lo_index, 1.0, 0.0).astype(BF16))
        segment[...] += dot_nt(jnp.concatenate(lhs, axis=1), jnp.concatenate(rhs, axis=1))
        return carry

    lax.fori_loop(0, GX // chunk, gather_up, 0)
    right_one = (segment[0:64, :] + segment[64:128, :]).reshape(8, 8, 128)

    def coarse_copy(sent, box, sends, receives, k, d, landing):
        return pltpu.make_async_remote_copy(
            src_ref=sent.at[k],
            dst_ref=box.at[k, landing],
            send_sem=sends.at[k, d],
            recv_sem=receives.at[k, landing],
            device_id=place(STEPS[d]),
            device_id_type=MESH_ID,
        )

    def coarse_send(bufs, k):
        for d in range(4):

            @pl.when(exists(STEPS[d]))
            def _():
                coarse_copy(*bufs, k, d, FACING[d]).start()

    def coarse_wait(bufs, k, sides=range(4)):
        for d in sides:

            @pl.when(exists(STEPS[d]))
            def _():
                coarse_copy(*bufs, k, d, d).wait_recv()
                coarse_copy(*bufs, k, d, FACING[d]).wait_send()

    bufs_one = (sent_one, box_one, send_one, recv_one)
    bufs_two = (sent_two, box_two, send_two, recv_two)

    def put_one(p, t, v):
        a, b = split_pair(v)
        picks_one[NT1 * p + t] = a
        picks_one[NT1 * p + t + 8] = b

    def apply_one(k, field, meanwhile=None):
        sent_one[k] = field
        coarse_send(bufs_one, k)
        for t in range(8):
            put_one(0, t, field[t])
        own = []
        for r in range(NT1):
            a = picks_one[r].astype(BF16)
            own.append(dot_nt(jnp.concatenate([a, a], axis=1), w_one[r, :, 0:256]))
        own = [jnp.where(upper(), fold(own[t]), fold(own[t + 8])) for t in range(8)]
        if meanwhile is not None:
            meanwhile()
        for d in (SOUTH, NORTH, WEST, EAST):
            coarse_wait(bufs_one, k, (d,))
            there = exists(STEPS[d])
            for t in range(8):
                put_one(d + 1, t, jnp.where(there, box_one[k, d, t], 0.0))
        outs = []
        for r in range(NT1):
            parts = []
            for j in range(3):
                a = picks_one[spots_one[3 * r + j]].astype(BF16)
                parts += [a, a]
            outs.append(dot_nt(jnp.concatenate(parts, axis=1), w_one[r, :, 256:1024]))
        return jnp.stack(
            [own[t] + jnp.where(upper(), fold(outs[t]), fold(outs[t + 8])) for t in range(8)]
        )

    def put_two(p, v):
        for h, a in enumerate(split_pair(v)):
            turned = pltpu.roll(a, 64, 1)
            picks_two[NT2 * p + 2 * h] = jnp.where(left(), a, turned)
            picks_two[NT2 * p + 2 * h + 1] = jnp.where(left(), turned, a)

    def apply_two(k, field, meanwhile=None):
        sent_two[k] = field
        coarse_send(bufs_two, k)
        put_two(0, field)
        if meanwhile is not None:
            meanwhile()
        coarse_wait(bufs_two, k)
        for d in range(4):
            put_two(d + 1, jnp.where(exists(STEPS[d]), box_two[k, d], 0.0))
        return product_two()

    def product_two():
        outs = []
        for r in range(NT2):
            parts = [picks_two[r]] + [picks_two[spots_two[3 * r + j]] for j in range(3)]
            lhs = jnp.concatenate([a.astype(BF16) for a in parts], axis=1)
            outs.append(fold(dot_nt(lhs, w_two[r])))
        return jnp.where(
            upper(), jnp.where(left(), outs[0], outs[1]), jnp.where(left(), outs[2], outs[3])
        )

    def down(apply_op, inv, right, windows):
        s0 = inv * right
        r1 = right - jacobi_weight * apply_op(0, s0, windows[0])
        s1 = inv * r1
        r2 = r1 - jacobi_weight * apply_op(1, s1, windows[1])
        s2 = inv * r2
        r3 = r2 - smooth_weight * apply_op(2, s2, windows[2])
        return r3, r2, jacobi_weight * (s0 + s1)

    def up(apply_op, inv, spread, applied, r2, x2):
        fix = spread - smooth_weight * (inv * applied)
        r3 = r2 - apply_op(4, fix)
        s3 = inv * r3
        r4 = r3 - jacobi_weight * apply_op(5, s3)
        return x2 + fix + jacobi_weight * s3 + jacobi_weight * (inv * r4)

    def joined(a, b):
        a, b = split_twin(a).astype(BF16), split_twin(b).astype(BF16)
        return jnp.concatenate([a, a, b, b], axis=1)

    def sweep(count, maps, box, total):
        y = box[0, 0]
        enter_y[0] = jnp.zeros((8, 128), F32)
        lifted = [box[0, 1]]
        for p in range(1, count):
            enter_y[p] = y
            lifted.append(box[p, 1] + times(y, maps[p, 2]))
            if total or p < count - 1:
                y = box[p, 0] + times(y, maps[p, 0])
        x = lifted[count - 1]
        enter_x[count - 1] = jnp.zeros((8, 128), F32)
        for p in reversed(range(count - 1)):
            enter_x[p] = x
            if total or p > 0:
                x = lifted[p] + times(x, maps[p, 1])
        return y, x

    def chain_solve(piece):
        slot = core * narrow_size + q
        box_rhs[slot] = piece

        def rhs_copy(i, j, landing):
            mate = (w - core + lax.rem(core + i, CORES), lax.rem(q + j, narrow_size))
            return peer_copy(
                box_rhs.at[slot], box_rhs, rhs_send, rhs_recv, i * narrow_size + j, landing, mate
            )

        for i, j in group[1:]:
            rhs_copy(i, j, slot).start()
        for i, j in group[1:]:
            other = lax.rem(core + i, CORES) * narrow_size + lax.rem(q + j, narrow_size)
            rhs_copy(i, j, other).wait_recv()
            rhs_copy(i, j, slot).wait_send()
        sums = []
        for i in range(CORES):
            total = box_rhs[i * narrow_size]
            for j in range(1, narrow_size):
                total = total + box_rhs[i * narrow_size + j]
            sums.append(total)
        both = fold(dot_nt(joined(*sums), pair_split[...]))
        ahead, behind = both[:, 0:128], both[:, 128:256]
        box_z[zs, 0] = ahead
        box_z[zs, 1] = behind
        z_start()
        z_finish()
        y, x = sweep(CHIPS_Z, z_split, box_z, True)
        box_x[xs, 0] = y
        box_x[xs, 1] = x
        x_start()
        y_in, x_in = enter_y[zs], enter_x[zs]
        x_splits()
        x_finish()
        sweep(segs, x_split, box_x, False)
        y_far, x_far = enter_y[xs], enter_x[xs]
        y_in = y_in + times(y_far, enter_split[0])
        x_in = x_in + times(y_far, enter_split[1]) + times(x_far, enter_split[2])
        both = fold(dot_nt(joined(y_in, x_in), pair_out[...]))
        x_first, x_last = behind + both[:, 0:128], ahead + both[:, 128:256]
        x_before = y_in + times(x_first, west_split[...])
        inner = core == 0
        return (
            jnp.where(inner, x_first, x_last),
            jnp.where(inner, x_before, x_first),
            jnp.where(inner, x_last, x_in),
        )

    def halves(pair):
        return jnp.concatenate([a.astype(BF16) for a in pair], axis=1)

    def pack_two(o):
        o = fold(o)
        return jnp.where(upper(), o[:, 0:128], o[:, 128:256])

    def restrict_one(field):
        pairs = [split_pair(field[t]) for t in range(8)]
        tiles = [p[0] for p in pairs] + [p[1] for p in pairs]
        return pack_two(dot_nt(halves(tiles), hot_one[...]))

    def prolong_one(coarse):
        o = fold(dot_nn(halves(split_pair(coarse)), hot_one[...]))
        parts = [o[:, 128 * t : 128 * t + 128] for t in range(NT1)]
        return jnp.stack([jnp.where(upper(), parts[t], parts[t + 8]) for t in range(8)])

    r_one, r2_one, x2_one = down(apply_one, inverse_one, right_one, (None, None, zmap_relay))
    right_two = restrict_one(r_one)
    r_two, r2_two, x2_two = down(apply_two, inverse_two, right_two, (z_prefix, z_suffix, z_splits))
    piece = fold(dot_nt(halves(split_pair(r_two)), hot_two[0]))
    answers = chain_solve(piece)

    def spread_two(p, answer):
        return pack_two(dot_nn(split_twin(answer).astype(BF16), hot_two[p]))

    spread = spread_two(0, answers[0])
    put_two(0, spread)
    for d, answer in enumerate((answers[1], answers[2], answers[0], answers[0])):
        put_two(d + 1, jnp.where(exists(STEPS[d]), spread_two(d + 1, answer), 0.0))
    answer_two = up(apply_two, inverse_two, spread, product_two(), r2_two, x2_two)
    spread = prolong_one(answer_two)
    answer_one = up(apply_one, inverse_one, spread, apply_one(3, spread), r2_one, x2_one)
    table[...] = answer_one

    def spread_rows(k, carry):
        at = pl.multiple_of(8 * k, 8)
        hi_index = groups_hi[pl.ds(at, 8), :]
        lo_index = groups_lo[pl.ds(at, 8), :]
        for c in range(COLS):
            total = jnp.zeros((8, 128), F32)
            for t in range(NT1):
                j = 4 * (t // 8) + c
                row = jnp.broadcast_to(table[t % 8, j : j + 1, :], (8, 128))
                value = jnp.take_along_axis(row, lo_index, axis=1, mode="promise_in_bounds")
                total = jnp.where(hi_index == t, value, total)
            field_a[c, pl.ds(pl.multiple_of(TOP + at, 8), 8), 0:128] = total
        return carry

    lax.fori_loop(0, GX // 8, spread_rows, 0)
    fine_start(1, field_a, 4)
    fine_send_all(1, 4)
    fine_wait(1, 4)
    fine_fill(1, field_a, 4)
    for o in rows_all:
        for c in range(COLS):
            v, m = mixed(field_a, c, o)
            field_b[c, o : o + 8, :] = (1.0 - smooth_weight) * v + smooth_weight * m
    for o in rows_all:
        for c in range(COLS):
            v, m = mixed(field_b, c, o)
            field_a[c, o : o + 8, :] = field_c[c, o : o + 8, :] - v + m
    for o in rows_in:
        i = o - TOP
        for c in range(COLS):
            v, m = mixed(field_a, c, o)
            x3 = second[c, i : i + 8, :] + field_b[c, o : o + 8, 0:128]
            s4 = rest * v + jacobi_weight * m
            out[c, i : i + 8, :] = x3 + jacobi_weight * (v + s4)[:, 0:128]


def solution(mesh):
    wide_size, narrow_size = mesh.shape["wide"], mesh.shape["narrow"]
    segs = wide_size // (CORES * CHIPS_Z)

    def body(
        block,
        east,
        north,
        fine_groups,
        tiles_one,
        columns_one,
        live_one,
        coarse_groups,
        tiles_two,
        columns_two,
        live_two,
        coarser_groups,
        chain_forward,
        chain_gain,
        chain_backward,
    ):
        hbm = pl.BlockSpec(memory_space=pl.ANY)
        vmem = pl.BlockSpec(memory_space=pltpu.VMEM)
        smem = pl.BlockSpec(memory_space=pltpu.SMEM)
        dma = pltpu.SemaphoreType.DMA
        big = pltpu.VMEM((COLS, EXT_ROWS, EXT_LANES), F32)
        weight = pltpu.VMEM((EXT_ROWS - 16, EXT_LANES), F32)
        square = pltpu.VMEM((GX, GY), F32)
        indices = pltpu.VMEM((GX, GY), jnp.int32)

        def kernel_fn(*refs):
            kernel(wide_size, narrow_size, *refs)

        return pl.pallas_call(
            kernel_fn,
            out_shape=jax.ShapeDtypeStruct((COLS, GX, GY), F32),
            in_specs=[hbm] * 5 + [smem] * 2 + [vmem, hbm] + [smem] * 2 + [vmem] + [hbm] * 3,
            out_specs=vmem,
            scratch_shapes=[
                pltpu.VMEM((6, EXT_ROWS, EXT_LANES), F32),
                indices,
                indices,
                pltpu.VMEM((NT1, 4, 128, 128), F32),
                pltpu.VMEM((NT2, 4, 64, 64), F32),
                pltpu.VMEM((2, 2, 6, 8, 128), F32),
                pltpu.VMEM((2, 6, 8, 128), F32),
                pltpu.VMEM((2, 8, 6, 8, 128), F32),
                weight,
                weight,
                weight,
                weight,
                weight,
                square,
                big,
                big,
                big,
                pltpu.VMEM((COLS, GX, GY), F32),
                pltpu.VMEM((8 * GX, GY), F32),
                pltpu.VMEM((8 * GX, GY), F32),
                square,
                pltpu.VMEM((8, 8, 128), F32),
                pltpu.VMEM((NT1, 128, 1024), BF16),
                pltpu.VMEM((NT2, 128, 512), BF16),
                pltpu.VMEM((5 * NT1 + 1, 8, 128), F32),
                pltpu.VMEM((5 * NT2 + 1, 8, 128), F32),
                pltpu.SMEM((3 * NT1,), jnp.int32),
                pltpu.SMEM((3 * NT2,), jnp.int32),
                pltpu.VMEM((256, 2048), BF16),
                pltpu.VMEM((5, 128, 256), BF16),
                pltpu.VMEM((6, 8, 8, 128), F32),
                pltpu.VMEM((6, 8, 128), F32),
                pltpu.VMEM((6, 4, 8, 8, 128), F32),
                pltpu.VMEM((6, 4, 8, 128), F32),
                pltpu.VMEM((CORES, 3, 128, 128), F32),
                pltpu.VMEM((256, 512), BF16),
                pltpu.VMEM((256, 512), BF16),
                square,
                pltpu.VMEM((128, 256), BF16),
                pltpu.VMEM((4, 2, 128), jnp.int32),
                pltpu.VMEM((CHIPS_Z, 384, 128), F32),
                pltpu.VMEM((CHIPS_Z, 3, 128, 256), BF16),
                pltpu.VMEM((CHIPS_Z + 1, 128, 128), F32),
                pltpu.VMEM((CHIPS_Z + 1, 128, 128), F32),
                pltpu.VMEM((CHIPS_Z + 1, 128, 128), F32),
                pltpu.VMEM((segs, 3, 128, 128), F32),
                pltpu.VMEM((segs, 3, 128, 256), BF16),
                pltpu.VMEM((3, 128, 256), BF16),
                pltpu.VMEM((CORES * narrow_size, 8, 128), F32),
                pltpu.VMEM((CHIPS_Z, 2, 8, 128), F32),
                pltpu.VMEM((segs, 2, 8, 128), F32),
                pltpu.VMEM((CHIPS_Z, 8, 128), F32),
                pltpu.VMEM((CHIPS_Z, 8, 128), F32),
                dma((9,)),
                dma((2, 8)),
                dma((2, 8)),
                dma((6, 4)),
                dma((6, 4)),
                dma((6, 4)),
                dma((6, 4)),
                dma,
                dma,
                dma,
                dma,
                dma((4,)),
                dma((4,)),
                dma((CHIPS_Z,)),
                dma((CHIPS_Z,)),
                dma((CORES * narrow_size,)),
                dma((CORES * narrow_size,)),
                dma((CHIPS_Z,)),
                dma((CHIPS_Z,)),
                dma((2, segs)),
                dma((2, segs)),
                dma((CHIPS_Z,)),
                dma((CHIPS_Z,)),
                dma((segs,)),
                dma((segs,)),
            ],
            compiler_params=pltpu.CompilerParams(
                collective_id=0, has_side_effects=True, vmem_limit_bytes=56 * 1024 * 1024
            ),
            name="cycle",
        )(
            block,
            east,
            north,
            fine_groups,
            tiles_one,
            columns_one.T,
            live_one.T,
            coarse_groups.reshape(16, 128),
            tiles_two,
            columns_two,
            live_two,
            coarser_groups.reshape(2, 128),
            chain_forward,
            chain_gain,
            chain_backward,
        )

    both = ("wide", "narrow")
    placed = (
        P(None, "wide", "narrow"),
        P("wide", "narrow"),
        P("wide", "narrow"),
        P("wide", "narrow"),
        P(both, None, None, None),
        P(both, None),
        P(both, None),
        P(both),
        P(both, None, None, None),
        P(both, None),
        P(both, None),
        P(both),
        P("wide", None, None),
        P("wide", None, None),
        P("wide", None, None),
    )
    return jax.shard_map(
        body, mesh=mesh, in_specs=placed, out_specs=P(None, "wide", "narrow"), check_vma=False
    )
```

```python
import jax
import jax.numpy as jnp
from jax import lax
from jax.experimental import pallas as pl
from jax.experimental.pallas import tpu as pltpu
from jax.sharding import PartitionSpec as P

F32 = jnp.float32
BF16 = jnp.bfloat16
MESH_ID = pl.DeviceIdType.MESH
GX = 128
GY = 128
COLS = 4
NT1 = 16
NT2 = 4
C3L = 32
CORES = 2
CHIPS_Z = 8
TOP = 16
EXT_ROWS = 160
EXT_LANES = 256
WEST, EAST, SOUTH, NORTH = 0, 1, 2, 3
STEPS = ((-1, 0), (1, 0), (0, -1), (0, 1), (-1, -1), (-1, 1), (1, -1), (1, 1))
FACING = (1, 0, 3, 2, 7, 6, 5, 4)
shift_value = 0.1
jacobi_weight = 0.6
smooth_weight = 0.5


def iota(shape, dim):
    return lax.broadcasted_iota(jnp.int32, shape, dim)


def dot_nt(a, b):
    return lax.dot_general(a, b, (((1,), (1,)), ((), ())), preferred_element_type=F32)


def dot_nn(a, b):
    return lax.dot_general(a, b, (((1,), (0,)), ((), ())), preferred_element_type=F32)


def matmul(a, b):
    return jnp.dot(a, b, precision=lax.Precision.HIGHEST, preferred_element_type=F32)


def upper():
    return iota((8, 128), 0) < 4


def left():
    return iota((8, 128), 1) < 64


def rounded(v):
    return v.astype(BF16).astype(F32)


def fold(o):
    return o + pltpu.roll(o, 4, 0)


def split_twin(v):
    hi = rounded(v)
    return jnp.where(upper(), hi, v - hi)


def split_pair(v):
    hi = rounded(v)
    lo = v - hi
    first = jnp.where(upper(), hi, pltpu.roll(lo, 4, 0))
    second = jnp.where(upper(), pltpu.roll(hi, 4, 0), lo)
    return first, second


def store_split(ref, m):
    hi = m.astype(BF16)
    ref[:, 0:128] = hi
    ref[:, 128:256] = (m - hi.astype(F32)).astype(BF16)


def times(v, split_map):
    a = split_twin(v).astype(BF16)
    return fold(dot_nt(jnp.concatenate([a, a], axis=1), split_map))


def kernel(
    wide_size,
    narrow_size,
    block,
    east,
    north,
    fine_groups,
    tiles_one,
    columns_one_in,
    live_one_in,
    coarse_groups_in,
    tiles_two,
    columns_two_in,
    live_two_in,
    coarser_groups_in,
    chain_forward,
    chain_gain,
    chain_backward,
    out,
    columns_one,
    live_one,
    coarse_groups,
    columns_two,
    live_two,
    coarser_groups,
    ext,
    groups_hi,
    groups_lo,
    held_one,
    held_two,
    slabs,
    packs,
    fine_box,
    weight_e,
    weight_w,
    weight_n,
    weight_s,
    inverse,
    diagonal,
    field_a,
    field_b,
    field_c,
    second,
    high_rows,
    low_rows,
    segment,
    table,
    w_one,
    w_far,
    hot_fine,
    groups_seg,
    w_two,
    picks_one,
    picks_two,
    spots_one,
    spots_two,
    hot_one,
    hot_two,
    sent_one,
    sent_two,
    box_one,
    box_two,
    pair_maps,
    pair_split,
    pair_out,
    west_map,
    west_split,
    group_box,
    own_maps,
    z_maps,
    z_split,
    prefix_u,
    suffix_v,
    suffix_w,
    x_maps,
    x_split,
    enter_split,
    box_rhs,
    box_z,
    box_x,
    enter_y,
    enter_x,
    local_sem,
    fine_send,
    fine_recv,
    send_one,
    recv_one,
    send_two,
    recv_two,
    core_send,
    core_recv,
    west_send,
    west_recv,
    group_send,
    group_recv,
    ymap_send,
    ymap_recv,
    relay_send,
    relay_recv,
    rhs_send,
    rhs_recv,
    zmap_send,
    zmap_recv,
    xmap_send,
    xmap_recv,
    z_send,
    z_recv,
    x_send,
    x_recv,
):
    w = lax.axis_index("wide")
    q = lax.axis_index("narrow")
    seg_size = CORES * CHIPS_Z
    segs = wide_size // seg_size
    xs = w // seg_size
    zs = lax.rem(w, seg_size) // CORES
    core = lax.rem(w, CORES)

    def place(step):
        return w + step[0], q + step[1]

    def exists(step):
        a, b = place(step)
        return (a >= 0) & (a < wide_size) & (b >= 0) & (b < narrow_size)

    loads = (
        (block, ext.at[pl.ds(0, 4), pl.ds(TOP, GX), pl.ds(0, GY)]),
        (east, ext.at[4, pl.ds(TOP, GX), pl.ds(0, GY)]),
        (north, ext.at[5, pl.ds(TOP, GX), pl.ds(0, GY)]),
        (chain_forward.at[0], pair_maps.at[core, 0]),
        (chain_gain.at[0], pair_maps.at[core, 1]),
        (chain_backward.at[0], pair_maps.at[core, 2]),
        (fine_groups, groups_lo),
        (tiles_two, held_two),
        (tiles_one, held_one),
        (columns_one_in, columns_one),
        (live_one_in, live_one),
        (coarse_groups_in, coarse_groups),
        (columns_two_in, columns_two),
        (live_two_in, live_two),
        (coarser_groups_in, coarser_groups),
    )
    local = [pltpu.make_async_copy(a, b, local_sem.at[i]) for i, (a, b) in enumerate(loads)]
    barrier = pltpu.get_barrier_semaphore()
    for i in (4, 3, 5, 2, 6, 1, 7):
        mate = (xs * seg_size + lax.rem(zs + i, CHIPS_Z) * CORES + core, q)
        pl.semaphore_signal(barrier, inc=1, device_id=mate, device_id_type=MESH_ID)
    for i in range(1, segs):
        mate = (lax.rem(xs + i, segs) * seg_size + zs * CORES + core, q)
        pl.semaphore_signal(barrier, inc=1, device_id=mate, device_id_type=MESH_ID)
    awaited = jnp.int32(0)
    for step in STEPS:
        there = exists(step)
        a, b = place(step)

        @pl.when(there)
        def _():
            pl.semaphore_signal(barrier, inc=1, device_id=(a, b), device_id_type=MESH_ID)

        awaited = awaited + jnp.where(there, 1, 0)
    group = [(i, j) for i in range(CORES) for j in range(narrow_size)]
    for i, j in group[1:]:
        mate = (w - core + lax.rem(core + i, CORES), lax.rem(q + j, narrow_size))
        pl.semaphore_signal(barrier, inc=1, device_id=mate, device_id_type=MESH_ID)
    awaited = awaited + len(group) - 1 + CHIPS_Z - 1 + segs - 1

    for i in (0, 1, 2, 3, 4, 5, 14, 6, 9, 10, 11, 12, 13, 7, 8):
        local[i].start()

    def fine_start(turn, source, arrays):
        lane = iota((8, 128), 1) // 4
        for a in range(arrays):
            slabs[turn, 0, a] = source[a, TOP : TOP + 8, 0:128]
            slabs[turn, 1, a] = source[a, TOP + GX - 8 : TOP + GX, 0:128]
            packed = jnp.zeros((8, 128), F32)
            for g in range(GX // 8):
                v = source[a, TOP + 8 * g : TOP + 8 * g + 8, 0:128]
                packed = jnp.where(lane == g, v if g == 0 else pltpu.roll(v, 4 * g, 1), packed)
                packed = jnp.where(lane == 16 + g, pltpu.roll(v, (68 + 4 * g) % 128, 1), packed)
            packs[turn, a] = packed

    def fine_copy(turn, arrays, d, landing):
        span = pl.ds(0, arrays)
        source = slabs.at[turn, d, span] if d < 2 else packs.at[turn, span]
        return pltpu.make_async_remote_copy(
            src_ref=source,
            dst_ref=fine_box.at[turn, landing, span],
            send_sem=fine_send.at[turn, d],
            recv_sem=fine_recv.at[turn, landing],
            device_id=place(STEPS[d]),
            device_id_type=MESH_ID,
        )

    def fine_send_all(turn, arrays):
        for d, step in enumerate(STEPS):

            @pl.when(exists(step))
            def _():
                fine_copy(turn, arrays, d, FACING[d]).start()

    def fine_wait(turn, arrays):
        for d, step in enumerate(STEPS):

            @pl.when(exists(step))
            def _():
                fine_copy(turn, arrays, d, d).wait_recv()
                fine_copy(turn, arrays, d, FACING[d]).wait_send()

    def fine_fill(turn, target, arrays):
        lane = iota((8, 128), 1)
        there = [exists(step) for step in STEPS]

        def got(d, a):
            return jnp.where(there[d], fine_box[turn, d, a], 0.0)

        def beside(south_pack, south_group, north_pack, north_group):
            low = pltpu.roll(south_pack, (124 - 64 - 4 * south_group) % 128, 1)
            high = pltpu.roll(north_pack, (128 - 4 * north_group) % 128, 1)
            return jnp.where(lane < 4, high, jnp.where(lane >= 124, low, 0.0))

        for a in range(arrays):
            target[a, TOP - 8 : TOP, 0:128] = got(0, a)
            target[a, TOP + GX : TOP + GX + 8, 0:128] = got(1, a)
            south_pack, north_pack = got(2, a), got(3, a)
            for g in range(GX // 8):
                target[a, TOP + 8 * g : TOP + 8 * g + 8, 128:256] = beside(south_pack, g, north_pack, g)
            target[a, TOP - 8 : TOP, 128:256] = beside(got(4, a), 15, got(5, a), 15)
            target[a, TOP + GX : TOP + GX + 8, 128:256] = beside(got(6, a), 0, got(7, a), 0)

    local[0].wait()
    local[1].wait()
    local[2].wait()
    fine_start(0, ext, 6)
    pl.semaphore_wait(barrier, awaited)
    fine_send_all(0, 6)

    local[3].wait()
    local[4].wait()
    local[5].wait()

    def core_copy(landing):
        return pltpu.make_async_remote_copy(
            src_ref=pair_maps.at[core],
            dst_ref=pair_maps.at[landing],
            send_sem=core_send,
            recv_sem=core_recv,
            device_id=(w - core + (1 - core), q),
            device_id_type=MESH_ID,
        )

    def west_copy():
        return pltpu.make_async_remote_copy(
            src_ref=pair_maps.at[core, 2],
            dst_ref=west_map,
            send_sem=west_send,
            recv_sem=west_recv,
            device_id=(w + 1, q),
            device_id_type=MESH_ID,
        )

    def group_copy(d, landing):
        return pltpu.make_async_remote_copy(
            src_ref=coarser_groups,
            dst_ref=group_box.at[landing],
            send_sem=group_send.at[d],
            recv_sem=group_recv.at[landing],
            device_id=place(STEPS[d]),
            device_id_type=MESH_ID,
        )

    feeds_east = (core == CORES - 1) & (w < wide_size - 1)
    fed_from_west = (core == 0) & (w > 0)
    local[14].wait()
    core_copy(core).start()

    @pl.when(feeds_east)
    def _():
        west_copy().start()

    for d in range(4):

        @pl.when(exists(STEPS[d]))
        def _():
            group_copy(d, FACING[d]).start()


    eye_one = iota((128, 128), 0) == iota((128, 128), 1)

    def peer_copy(source, target, sends, receives, slot, landing, mate):
        return pltpu.make_async_remote_copy(
            src_ref=source,
            dst_ref=target.at[landing],
            send_sem=sends.at[slot],
            recv_sem=receives.at[landing],
            device_id=mate,
            device_id_type=MESH_ID,
        )

    def z_mate(i):
        z = lax.rem(zs + i, CHIPS_Z)
        return z, (xs * seg_size + z * CORES + core, q)

    def x_mate(i):
        x = lax.rem(xs + i, segs)
        return x, (x * seg_size + zs * CORES + core, q)

    def along(mates, count, box, sends, receives, mine):
        def start():
            for i in range(1, count):
                _, mate = mates(i)
                peer_copy(box.at[mine], box, sends, receives, i, mine, mate).start()

        def finish():
            for i in range(1, count):
                other, mate = mates(i)
                peer_copy(box.at[mine], box, sends, receives, i, other, mate).wait_recv()
                peer_copy(box.at[mine], box, sends, receives, i, mine, mate).wait_send()

        return start, finish

    z_start, z_finish = along(z_mate, CHIPS_Z, box_z, z_send, z_recv, zs)
    x_start, x_finish = along(x_mate, segs, box_x, x_send, x_recv, xs)
    z_order = (1, 7, 2, 6, 3, 5, 4)

    piece_rows = pl.ds(pl.multiple_of(192 * core + 48 * q, 16), 48)

    def zmap_copy(i, landing, mate):
        return pltpu.make_async_remote_copy(
            src_ref=own_maps.at[piece_rows],
            dst_ref=z_maps.at[landing, piece_rows],
            send_sem=zmap_send.at[i],
            recv_sem=zmap_recv.at[landing],
            device_id=mate,
            device_id_type=MESH_ID,
        )

    def ymap_copy(i, other):
        rows = pl.ds(pl.multiple_of(192 * core + 48 * other, 16), 48)
        return pltpu.make_async_remote_copy(
            src_ref=z_maps.at[:, rows],
            dst_ref=z_maps.at[:, rows],
            send_sem=ymap_send.at[i],
            recv_sem=ymap_recv.at[other],
            device_id=(w, lax.rem(q + i, narrow_size)),
            device_id_type=MESH_ID,
        )

    def relay_copy(side):
        half = pl.ds(pl.multiple_of(192 * side, 64), 192)
        return pltpu.make_async_remote_copy(
            src_ref=z_maps.at[:, half],
            dst_ref=z_maps.at[:, half],
            send_sem=relay_send,
            recv_sem=relay_recv,
            device_id=(w - core + (1 - core), q),
            device_id_type=MESH_ID,
        )

    def pair_products():
        core_copy(1 - core).wait_recv()
        core_copy(core).wait_send()
        f0, b0 = pair_maps[0, 0], pair_maps[0, 2]
        f1, b1 = pair_maps[1, 0], pair_maps[1, 2]
        both = matmul(f1, f0)
        own_maps[0:128] = both
        own_maps[128:256] = matmul(b0, b1)
        own_maps[256:384] = f0 + matmul(b0, both)
        z_maps[zs, piece_rows] = own_maps[piece_rows]
        for i in z_order:
            _, mate = z_mate(i)
            zmap_copy(i, zs, mate).start()

    def pair_gains():
        g0, b0 = pair_maps[0, 1], pair_maps[0, 2]
        f1, g1 = pair_maps[1, 0], pair_maps[1, 1]
        across = matmul(f1, g0)
        store_split(pair_split.at[0:128, 0:256], across)
        store_split(pair_split.at[0:128, 256:512], g1)
        store_split(pair_split.at[128:256, 0:256], g0 + matmul(b0, across))
        store_split(pair_split.at[128:256, 256:512], matmul(b0, g1))

    def zmap_across():
        for i in z_order:
            other, mate = z_mate(i)
            zmap_copy(i, other, mate).wait_recv()
            zmap_copy(i, zs, mate).wait_send()
        for i in range(1, narrow_size):
            ymap_copy(i, q).start()

    def zmap_relay():
        for i in range(1, narrow_size):
            ymap_copy(i, lax.rem(q + i, narrow_size)).wait_recv()
            ymap_copy(i, q).wait_send()
        relay_copy(core).start()

    def times_map(split_map, m):
        hi = m.astype(BF16)
        lo = (m - hi.astype(F32)).astype(BF16)
        lhs = jnp.concatenate([split_map, split_map[:, 0:128]], axis=1)
        return dot_nn(lhs, jnp.concatenate([hi, hi, lo], axis=0))

    def z_prefix():
        relay_copy(1 - core).wait_recv()
        relay_copy(core).wait_send()

        def split_one(p, carry):
            for j in range(3):
                store_split(z_split.at[p, j], z_maps[p, 128 * j : 128 * j + 128])
            return carry

        lax.fori_loop(0, CHIPS_Z, split_one, 0)
        one_map = jnp.where(eye_one, 1.0, 0.0)
        prefix_u[0] = one_map
        suffix_w[CHIPS_Z] = one_map

        def one(p, carry):
            prefix_u[p + 1] = times_map(z_split[p, 0], prefix_u[p])
            r = CHIPS_Z - 1 - p
            suffix_w[r] = times_map(z_split[r, 1], suffix_w[r + 1])
            return carry

        lax.fori_loop(0, CHIPS_Z, one, 0)
        x_maps[xs, 0] = prefix_u[CHIPS_Z]
        x_maps[xs, 1] = suffix_w[0]

    def xmap_copy(part, i, landing, mate):
        span = pl.ds(0, 2) if part == 0 else pl.ds(2, 1)
        return pltpu.make_async_remote_copy(
            src_ref=x_maps.at[xs, span],
            dst_ref=x_maps.at[landing, span],
            send_sem=xmap_send.at[part, i],
            recv_sem=xmap_recv.at[part, landing],
            device_id=mate,
            device_id_type=MESH_ID,
        )

    def has_map(part, x):
        return (x > 0) & (x < segs - 1) if part == 0 else x > 0

    def z_suffix():
        suffix_v[CHIPS_Z] = jnp.zeros((128, 128), F32)

        def one(i, carry):
            p = CHIPS_Z - 1 - i
            suffix_v[p] = times_map(z_split[p, 1], suffix_v[p + 1]) + times_map(
                z_split[p, 2], prefix_u[p]
            )
            return carry

        lax.fori_loop(0, CHIPS_Z, one, 0)
        x_maps[xs, 2] = suffix_v[0]
        for part in range(2):
            for i in range(1, segs):
                _, mate = x_mate(i)

                @pl.when(has_map(part, xs))
                def _():
                    xmap_copy(part, i, xs, mate).start()

    def z_composites():
        z_prefix()
        z_suffix()

    def z_splits():
        store_split(enter_split.at[0], prefix_u[zs])
        store_split(enter_split.at[1], suffix_v[zs + 1])
        store_split(enter_split.at[2], suffix_w[zs + 1])
        pair_out[0:128, 0:256] = z_split[zs, 2]
        pair_out[0:128, 256:512] = z_split[zs, 1]
        pair_out[128:256, 0:256] = z_split[zs, 0]
        store_split(pair_out.at[128:256, 256:512], pair_maps[1, 2])

        @pl.when(fed_from_west)
        def _():
            west_copy().wait_recv()

        @pl.when(feeds_east)
        def _():
            west_copy().wait_send()

        store_split(west_split, west_map[...])
        for d in range(4):

            @pl.when(exists(STEPS[d]))
            def _():
                group_copy(d, d).wait_recv()
                group_copy(d, FACING[d]).wait_send()

            mark_two(d + 1, group_box[d], q + STEPS[d][1])

    def x_splits():
        for part in range(2):
            for i in range(1, segs):
                other, mate = x_mate(i)

                @pl.when(has_map(part, other))
                def _():
                    xmap_copy(part, i, other, mate).wait_recv()

                @pl.when(has_map(part, xs))
                def _():
                    xmap_copy(part, i, xs, mate).wait_send()

        for p in range(1, segs):
            for j in range(3):
                if j == 2 or p < segs - 1:
                    store_split(x_split.at[p, j], x_maps[p, j])

    local[6].wait()
    groups = groups_lo[...]
    groups_hi[...] = groups // 128
    groups_lo[...] = lax.rem(groups, 128)
    groups_seg[...] = groups // 256
    turned = jnp.transpose(lax.rem(groups, 256).astype(F32))
    wide_lane = iota((GY, 256), 1).astype(F32)
    for i in range(GX):
        hot = turned[:, i : i + 1] == wide_lane
        hot_fine[GY * i : GY * i + GY, :] = jnp.where(hot, 1.0, 0.0).astype(BF16)
    for i in range(9, 14):
        local[i].wait()
    for r in range(NT1):
        for k in range(3):
            spots_one[3 * r + k] = jnp.where(live_one[k, r] == 1, columns_one[k, r], 5 * NT1)
    for r in range(NT2):
        for k in range(3):
            spots_two[3 * r + k] = jnp.where(live_two[r, k] == 1, columns_two[r, k], 5 * NT2)
    picks_one[5 * NT1] = jnp.zeros((8, 128), F32)
    picks_two[5 * NT2] = jnp.zeros((8, 128), F32)
    local[7].wait()
    lane_two = iota((64, 128), 1)
    eye_two = iota((64, 128), 0) == lax.rem(lane_two, 64)
    diag_two = []
    for r in range(NT2):
        for k in range(4):
            m = held_two[r, k]
            m = jnp.concatenate([m, m], axis=1)
            if k == 0:
                diag_two.append(jnp.sum(jnp.where(eye_two, m, 0.0), axis=0, keepdims=True))
            hi = rounded(m)
            m = jnp.where(lane_two < 64, hi, m - hi).astype(BF16)
            w_two[r, 0:64, 128 * k : 128 * k + 128] = m
            w_two[r, 64:128, 128 * k : 128 * k + 128] = m
    wide_two = [jnp.broadcast_to(d, (8, 128)) for d in diag_two]
    inverse_two = 1.0 / jnp.where(
        upper(),
        jnp.where(left(), wide_two[0], wide_two[1]),
        jnp.where(left(), wide_two[2], wide_two[3]),
    )
    for t in range(NT1):
        hot = iota((256, 128), 0) == coarse_groups[t : t + 1, :]
        hot_one[:, 128 * t : 128 * t + 128] = jnp.where(hot, 1.0, 0.0).astype(BF16)

    def mark_two(p, groups, owner):
        for h in range(2):
            hot = iota((128, 128), 0) == groups[h : h + 1, :] + C3L * owner
            hot_two[p, :, 128 * h : 128 * h + 128] = jnp.where(hot, 1.0, 0.0).astype(BF16)

    mark_two(0, coarser_groups[...], q)
    pair_products()
    local[8].wait()

    def split_tiles(t, carry):
        diags = []
        for r in (t, t + 8):
            for k in range(4):
                m = held_one[r, k]
                if k == 0:
                    diags.append(jnp.sum(jnp.where(eye_one, m, 0.0), axis=0, keepdims=True))
                    store_split(w_one.at[r], m)
                else:
                    m = jnp.transpose(m)
                    hi = m.astype(BF16)
                    w_far[r, 256 * k - 256 : 256 * k - 128, :] = hi
                    w_far[r, 256 * k - 128 : 256 * k, :] = (m - hi.astype(F32)).astype(BF16)
        low, high = (jnp.broadcast_to(d, (8, 128)) for d in diags)
        table[t] = 1.0 / jnp.where(upper(), low, high)
        return carry

    lax.fori_loop(0, 8, split_tiles, 0)
    inverse_one = table[...]
    pair_gains()

    fine_wait(0, 6)
    fine_fill(0, ext, 6)
    rows_all = range(8, EXT_ROWS - 8, 8)
    last_row = wide_size * GX - 1
    last_column = narrow_size * GY - 1
    lane_ext = iota((8, EXT_LANES), 1)
    column = q * GY + jnp.where(lane_ext < 192, lane_ext, lane_ext - EXT_LANES)
    for o in rows_all:
        row = w * GX + (o - TOP) + iota((8, EXT_LANES), 0)
        ext[4, o : o + 8, :] = jnp.where(row < last_row, ext[4, o : o + 8, :], 0.0)
        ext[5, o : o + 8, :] = jnp.where(column < last_column, ext[5, o : o + 8, :], 0.0)
    for o in rows_all:
        e = ext[4, o : o + 8, :]
        b = ext[4, o - 1 : o + 7, :]
        n = ext[5, o : o + 8, :]
        s = pltpu.roll(n, 1, 1)
        d = shift_value + e + b + n + s
        inv = 1.0 / d
        weight_e[o - 8 : o, :] = e * inv
        weight_w[o - 8 : o, :] = b * inv
        weight_n[o - 8 : o, :] = n * inv
        weight_s[o - 8 : o, :] = s * inv
        if TOP <= o < TOP + GX:
            diagonal[o - TOP : o - TOP + 8, :] = d[:, 0:128]
        for c in range(COLS):
            field_a[c, o : o + 8, :] = ext[c, o : o + 8, :] * inv

    def mixed(source, c, o):
        v = source[c, o : o + 8, :]
        a = weight_e[o - 8 : o, :] * source[c, o + 1 : o + 9, :]
        b = weight_w[o - 8 : o, :] * source[c, o - 1 : o + 7, :]
        n = weight_n[o - 8 : o, :] * pltpu.roll(v, EXT_LANES - 1, 1)
        s = weight_s[o - 8 : o, :] * pltpu.roll(v, 1, 1)
        return v, (a + b) + (n + s)

    rows_in = range(TOP, TOP + GX, 8)
    rest = 1.0 - jacobi_weight
    for o in rows_all:
        for c in range(COLS):
            v, m = mixed(field_a, c, o)
            field_b[c, o : o + 8, :] = rest * v + jacobi_weight * m
    for o in rows_all:
        for c in range(COLS):
            v, m = mixed(field_b, c, o)
            field_c[c, o : o + 8, :] = rest * v + jacobi_weight * m
    for o in rows_in:
        i = o - TOP
        for c in range(COLS):
            v, m = mixed(field_c, c, o)
            r = ((1.0 - smooth_weight) * v + smooth_weight * m)[:, 0:128] * diagonal[i : i + 8, :]
            both = field_a[c, o : o + 8, 0:128] + field_b[c, o : o + 8, 0:128]
            second[c, i : i + 8, :] = jacobi_weight * both
            hi = rounded(r)
            lo = r - hi
            for h in range(2):
                high_rows[pl.ds(8 * i + 4 * h + c, 8, stride=8), :] = hi
                low_rows[pl.ds(8 * i + 4 * h + c, 8, stride=8), :] = lo

    segment[...] = jnp.zeros((64, 256), F32)
    half = jnp.where(upper(), 0, 4)
    chunk = 16

    def gather_up(step, carry):
        lhs = []
        for j in range(chunk):
            i = step * chunk + j
            index = jnp.broadcast_to(groups_seg[pl.ds(i, 1), :], (8, 128))
            at = pl.multiple_of(8 * i, 8)
            v_hi = high_rows[pl.ds(at, 8), :]
            v_lo = low_rows[pl.ds(at, 8), :]
            masks = [index == half + t for t in range(4)]
            rows = [jnp.where(m, v_hi, 0.0) for m in masks] + [jnp.where(m, v_lo, 0.0) for m in masks]
            lhs.append(jnp.concatenate(rows, axis=0).astype(BF16))
        span = pl.ds(pl.multiple_of(step * (chunk * GY), chunk * GY), chunk * GY)
        segment[...] += dot_nn(jnp.concatenate(lhs, axis=1), hot_fine[span, :])
        return carry

    lax.fori_loop(0, GX // chunk, gather_up, 0)
    folded = segment[0:32, :] + segment[32:64, :]
    right_one = jnp.stack(
        [folded[8 * (t // 2) : 8 * (t // 2) + 8, 128 * (t % 2) : 128 * (t % 2) + 128] for t in range(8)]
    )

    def coarse_copy(sent, box, sends, receives, k, d, landing):
        return pltpu.make_async_remote_copy(
            src_ref=sent.at[k],
            dst_ref=box.at[k, landing],
            send_sem=sends.at[k, d],
            recv_sem=receives.at[k, landing],
            device_id=place(STEPS[d]),
            device_id_type=MESH_ID,
        )

    def coarse_send(bufs, k):
        for d in range(4):

            @pl.when(exists(STEPS[d]))
            def _():
                coarse_copy(*bufs, k, d, FACING[d]).start()

    def coarse_wait(bufs, k, sides=range(4)):
        for d in sides:

            @pl.when(exists(STEPS[d]))
            def _():
                coarse_copy(*bufs, k, d, d).wait_recv()
                coarse_copy(*bufs, k, d, FACING[d]).wait_send()

    bufs_one = (sent_one, box_one, send_one, recv_one)
    bufs_two = (sent_two, box_two, send_two, recv_two)

    def put_one(p, t, v):
        a, b = split_pair(v)
        picks_one[NT1 * p + t] = a
        picks_one[NT1 * p + t + 8] = b

    def apply_one(k, field, meanwhile=None):
        sent_one[k] = field
        coarse_send(bufs_one, k)
        for t in range(8):
            put_one(0, t, field[t])
        own = []
        for r in range(NT1):
            a = picks_one[r].astype(BF16)
            own.append(dot_nt(jnp.concatenate([a, a], axis=1), w_one[r]))
        own = [jnp.where(upper(), fold(own[t]), fold(own[t + 8])) for t in range(8)]
        if meanwhile is not None:
            meanwhile()
        for d in (SOUTH, NORTH, WEST, EAST):
            coarse_wait(bufs_one, k, (d,))
            there = exists(STEPS[d])
            for t in range(8):
                put_one(d + 1, t, jnp.where(there, box_one[k, d, t], 0.0))
        outs = []
        for r in range(NT1):
            parts = []
            for j in range(3):
                a = picks_one[spots_one[3 * r + j]].astype(BF16)
                parts += [a, a]
            outs.append(dot_nn(jnp.concatenate(parts, axis=1), w_far[r]))
        return jnp.stack(
            [own[t] + jnp.where(upper(), fold(outs[t]), fold(outs[t + 8])) for t in range(8)]
        )

    def put_two(p, v):
        for h, a in enumerate(split_pair(v)):
            turned = pltpu.roll(a, 64, 1)
            picks_two[NT2 * p + 2 * h] = jnp.where(left(), a, turned)
            picks_two[NT2 * p + 2 * h + 1] = jnp.where(left(), turned, a)

    def apply_two(k, field, meanwhile=None):
        sent_two[k] = field
        coarse_send(bufs_two, k)
        put_two(0, field)
        if meanwhile is not None:
            meanwhile()
        coarse_wait(bufs_two, k)
        for d in range(4):
            put_two(d + 1, jnp.where(exists(STEPS[d]), box_two[k, d], 0.0))
        return product_two()

    def product_two():
        outs = []
        for r in range(NT2):
            parts = [picks_two[r]] + [picks_two[spots_two[3 * r + j]] for j in range(3)]
            lhs = jnp.concatenate([a.astype(BF16) for a in parts], axis=1)
            outs.append(fold(dot_nt(lhs, w_two[r])))
        return jnp.where(
            upper(), jnp.where(left(), outs[0], outs[1]), jnp.where(left(), outs[2], outs[3])
        )

    def down(apply_op, inv, right, windows):
        s0 = inv * right
        r1 = right - jacobi_weight * apply_op(0, s0, windows[0])
        s1 = inv * r1
        r2 = r1 - jacobi_weight * apply_op(1, s1, windows[1])
        s2 = inv * r2
        r3 = r2 - smooth_weight * apply_op(2, s2, windows[2])
        return r3, r2, jacobi_weight * (s0 + s1)

    def up(apply_op, inv, spread, applied, r2, x2):
        fix = spread - smooth_weight * (inv * applied)
        r3 = r2 - apply_op(4, fix)
        s3 = inv * r3
        r4 = r3 - jacobi_weight * apply_op(5, s3)
        return x2 + fix + jacobi_weight * s3 + jacobi_weight * (inv * r4)

    def joined(a, b):
        a, b = split_twin(a).astype(BF16), split_twin(b).astype(BF16)
        return jnp.concatenate([a, a, b, b], axis=1)

    def sweep(count, maps, box, total):
        y = box[0, 0]
        enter_y[0] = jnp.zeros((8, 128), F32)
        lifted = [box[0, 1]]
        for p in range(1, count):
            enter_y[p] = y
            lifted.append(box[p, 1] + times(y, maps[p, 2]))
            if total or p < count - 1:
                y = box[p, 0] + times(y, maps[p, 0])
        x = lifted[count - 1]
        enter_x[count - 1] = jnp.zeros((8, 128), F32)
        for p in reversed(range(count - 1)):
            enter_x[p] = x
            if total or p > 0:
                x = lifted[p] + times(x, maps[p, 1])
        return y, x

    def chain_solve(piece):
        slot = core * narrow_size + q
        box_rhs[slot] = piece

        def rhs_copy(i, j, landing):
            mate = (w - core + lax.rem(core + i, CORES), lax.rem(q + j, narrow_size))
            return peer_copy(
                box_rhs.at[slot], box_rhs, rhs_send, rhs_recv, i * narrow_size + j, landing, mate
            )

        for i, j in group[1:]:
            rhs_copy(i, j, slot).start()
        z_splits()
        for i, j in group[1:]:
            other = lax.rem(core + i, CORES) * narrow_size + lax.rem(q + j, narrow_size)
            rhs_copy(i, j, other).wait_recv()
            rhs_copy(i, j, slot).wait_send()
        sums = []
        for i in range(CORES):
            total = box_rhs[i * narrow_size]
            for j in range(1, narrow_size):
                total = total + box_rhs[i * narrow_size + j]
            sums.append(total)
        both = fold(dot_nt(joined(*sums), pair_split[...]))
        ahead, behind = both[:, 0:128], both[:, 128:256]
        box_z[zs, 0] = ahead
        box_z[zs, 1] = behind
        z_start()
        z_finish()
        y, x = sweep(CHIPS_Z, z_split, box_z, True)
        box_x[xs, 0] = y
        box_x[xs, 1] = x
        x_start()
        y_in, x_in = enter_y[zs], enter_x[zs]
        x_splits()
        x_finish()
        sweep(segs, x_split, box_x, False)
        y_far, x_far = enter_y[xs], enter_x[xs]
        y_in = y_in + times(y_far, enter_split[0])
        x_in = x_in + times(y_far, enter_split[1]) + times(x_far, enter_split[2])
        both = fold(dot_nt(joined(y_in, x_in), pair_out[...]))
        x_first, x_last = behind + both[:, 0:128], ahead + both[:, 128:256]
        x_before = y_in + times(x_first, west_split[...])
        inner = core == 0
        return (
            jnp.where(inner, x_first, x_last),
            jnp.where(inner, x_before, x_first),
            jnp.where(inner, x_last, x_in),
        )

    def halves(pair):
        return jnp.concatenate([a.astype(BF16) for a in pair], axis=1)

    def pack_two(o):
        o = fold(o)
        return jnp.where(upper(), o[:, 0:128], o[:, 128:256])

    def restrict_one(field):
        pairs = [split_pair(field[t]) for t in range(8)]
        tiles = [p[0] for p in pairs] + [p[1] for p in pairs]
        return pack_two(dot_nt(halves(tiles), hot_one[...]))

    def prolong_one(coarse):
        o = fold(dot_nn(halves(split_pair(coarse)), hot_one[...]))
        parts = [o[:, 128 * t : 128 * t + 128] for t in range(NT1)]
        return jnp.stack([jnp.where(upper(), parts[t], parts[t + 8]) for t in range(8)])

    r_one, r2_one, x2_one = down(apply_one, inverse_one, right_one, (zmap_across, None, None))
    right_two = restrict_one(r_one)
    r_two, r2_two, x2_two = down(apply_two, inverse_two, right_two, (zmap_relay, z_composites, None))
    piece = fold(dot_nt(halves(split_pair(r_two)), hot_two[0]))
    answers = chain_solve(piece)

    def spread_two(p, answer):
        return pack_two(dot_nn(split_twin(answer).astype(BF16), hot_two[p]))

    spread = spread_two(0, answers[0])
    put_two(0, spread)
    for d, answer in enumerate((answers[1], answers[2], answers[0], answers[0])):
        put_two(d + 1, jnp.where(exists(STEPS[d]), spread_two(d + 1, answer), 0.0))
    answer_two = up(apply_two, inverse_two, spread, product_two(), r2_two, x2_two)
    spread = prolong_one(answer_two)
    answer_one = up(apply_one, inverse_one, spread, apply_one(3, spread), r2_one, x2_one)
    table[...] = answer_one

    def spread_rows(k, carry):
        at = pl.multiple_of(8 * k, 8)
        hi_index = groups_hi[pl.ds(at, 8), :]
        lo_index = groups_lo[pl.ds(at, 8), :]
        for c in range(COLS):
            total = jnp.zeros((8, 128), F32)
            for t in range(NT1):
                j = 4 * (t // 8) + c
                row = jnp.broadcast_to(table[t % 8, j : j + 1, :], (8, 128))
                value = jnp.take_along_axis(row, lo_index, axis=1, mode="promise_in_bounds")
                total = jnp.where(hi_index == t, value, total)
            field_a[c, pl.ds(pl.multiple_of(TOP + at, 8), 8), 0:128] = total
        return carry

    lax.fori_loop(0, GX // 8, spread_rows, 0, unroll=4)
    fine_start(1, field_a, 4)
    fine_send_all(1, 4)
    fine_wait(1, 4)
    fine_fill(1, field_a, 4)
    for o in rows_all:
        for c in range(COLS):
            v, m = mixed(field_a, c, o)
            field_b[c, o : o + 8, :] = (1.0 - smooth_weight) * v + smooth_weight * m
    for o in rows_all:
        for c in range(COLS):
            v, m = mixed(field_b, c, o)
            field_a[c, o : o + 8, :] = field_c[c, o : o + 8, :] - v + m
    for o in rows_in:
        i = o - TOP
        for c in range(COLS):
            v, m = mixed(field_a, c, o)
            x3 = second[c, i : i + 8, :] + field_b[c, o : o + 8, 0:128]
            s4 = rest * v + jacobi_weight * m
            out[c, i : i + 8, :] = x3 + jacobi_weight * (v + s4)[:, 0:128]


def solution(mesh):
    wide_size, narrow_size = mesh.shape["wide"], mesh.shape["narrow"]
    segs = wide_size // (CORES * CHIPS_Z)

    def body(
        block,
        east,
        north,
        fine_groups,
        tiles_one,
        columns_one,
        live_one,
        coarse_groups,
        tiles_two,
        columns_two,
        live_two,
        coarser_groups,
        chain_forward,
        chain_gain,
        chain_backward,
    ):
        hbm = pl.BlockSpec(memory_space=pl.ANY)
        vmem = pl.BlockSpec(memory_space=pltpu.VMEM)
        dma = pltpu.SemaphoreType.DMA
        big = pltpu.VMEM((COLS, EXT_ROWS, EXT_LANES), F32)
        weight = pltpu.VMEM((EXT_ROWS - 16, EXT_LANES), F32)
        square = pltpu.VMEM((GX, GY), F32)
        indices = pltpu.VMEM((GX, GY), jnp.int32)

        def kernel_fn(*refs):
            kernel(wide_size, narrow_size, *refs)

        return pl.pallas_call(
            kernel_fn,
            out_shape=jax.ShapeDtypeStruct((COLS, GX, GY), F32),
            in_specs=[hbm] * 15,
            out_specs=vmem,
            scratch_shapes=[
                pltpu.SMEM((3, NT1), jnp.int32),
                pltpu.SMEM((3, NT1), jnp.int32),
                pltpu.VMEM((16, 128), jnp.int32),
                pltpu.SMEM((NT2, 3), jnp.int32),
                pltpu.SMEM((NT2, 3), jnp.int32),
                pltpu.VMEM((2, 128), jnp.int32),
                pltpu.VMEM((6, EXT_ROWS, EXT_LANES), F32),
                indices,
                indices,
                pltpu.VMEM((NT1, 4, 128, 128), F32),
                pltpu.VMEM((NT2, 4, 64, 64), F32),
                pltpu.VMEM((2, 2, 6, 8, 128), F32),
                pltpu.VMEM((2, 6, 8, 128), F32),
                pltpu.VMEM((2, 8, 6, 8, 128), F32),
                weight,
                weight,
                weight,
                weight,
                weight,
                square,
                big,
                big,
                big,
                pltpu.VMEM((COLS, GX, GY), F32),
                pltpu.VMEM((8 * GX, GY), F32),
                pltpu.VMEM((8 * GX, GY), F32),
                pltpu.VMEM((64, 256), F32),
                pltpu.VMEM((8, 8, 128), F32),
                pltpu.VMEM((NT1, 128, 256), BF16),
                pltpu.VMEM((NT1, 768, 128), BF16),
                pltpu.VMEM((GX * GY, 256), BF16),
                indices,
                pltpu.VMEM((NT2, 128, 512), BF16),
                pltpu.VMEM((5 * NT1 + 1, 8, 128), F32),
                pltpu.VMEM((5 * NT2 + 1, 8, 128), F32),
                pltpu.SMEM((3 * NT1,), jnp.int32),
                pltpu.SMEM((3 * NT2,), jnp.int32),
                pltpu.VMEM((256, 2048), BF16),
                pltpu.VMEM((5, 128, 256), BF16),
                pltpu.VMEM((6, 8, 8, 128), F32),
                pltpu.VMEM((6, 8, 128), F32),
                pltpu.VMEM((6, 4, 8, 8, 128), F32),
                pltpu.VMEM((6, 4, 8, 128), F32),
                pltpu.VMEM((CORES, 3, 128, 128), F32),
                pltpu.VMEM((256, 512), BF16),
                pltpu.VMEM((256, 512), BF16),
                square,
                pltpu.VMEM((128, 256), BF16),
                pltpu.VMEM((4, 2, 128), jnp.int32),
                pltpu.VMEM((384, 128), F32),
                pltpu.VMEM((CHIPS_Z, 384, 128), F32),
                pltpu.VMEM((CHIPS_Z, 3, 128, 256), BF16),
                pltpu.VMEM((CHIPS_Z + 1, 128, 128), F32),
                pltpu.VMEM((CHIPS_Z + 1, 128, 128), F32),
                pltpu.VMEM((CHIPS_Z + 1, 128, 128), F32),
                pltpu.VMEM((segs, 3, 128, 128), F32),
                pltpu.VMEM((segs, 3, 128, 256), BF16),
                pltpu.VMEM((3, 128, 256), BF16),
                pltpu.VMEM((CORES * narrow_size, 8, 128), F32),
                pltpu.VMEM((CHIPS_Z, 2, 8, 128), F32),
                pltpu.VMEM((segs, 2, 8, 128), F32),
                pltpu.VMEM((CHIPS_Z, 8, 128), F32),
                pltpu.VMEM((CHIPS_Z, 8, 128), F32),
                dma((15,)),
                dma((2, 8)),
                dma((2, 8)),
                dma((6, 4)),
                dma((6, 4)),
                dma((6, 4)),
                dma((6, 4)),
                dma,
                dma,
                dma,
                dma,
                dma((4,)),
                dma((4,)),
                dma((narrow_size,)),
                dma((narrow_size,)),
                dma,
                dma,
                dma((CORES * narrow_size,)),
                dma((CORES * narrow_size,)),
                dma((CHIPS_Z,)),
                dma((CHIPS_Z,)),
                dma((2, segs)),
                dma((2, segs)),
                dma((CHIPS_Z,)),
                dma((CHIPS_Z,)),
                dma((segs,)),
                dma((segs,)),
            ],
            compiler_params=pltpu.CompilerParams(
                collective_id=0, has_side_effects=True, vmem_limit_bytes=56 * 1024 * 1024
            ),
            name="cycle",
        )(
            block,
            east,
            north,
            fine_groups,
            tiles_one,
            columns_one.T,
            live_one.T,
            coarse_groups.reshape(16, 128),
            tiles_two,
            columns_two,
            live_two,
            coarser_groups.reshape(2, 128),
            chain_forward,
            chain_gain,
            chain_backward,
        )

    both = ("wide", "narrow")
    placed = (
        P(None, "wide", "narrow"),
        P("wide", "narrow"),
        P("wide", "narrow"),
        P("wide", "narrow"),
        P(both, None, None, None),
        P(both, None),
        P(both, None),
        P(both),
        P(both, None, None, None),
        P(both, None),
        P(both, None),
        P(both),
        P("wide", None, None),
        P("wide", None, None),
        P("wide", None, None),
    )
    return jax.shard_map(
        body, mesh=mesh, in_specs=placed, out_specs=P(None, "wide", "narrow"), check_vma=False
    )
```

```python
import jax
import jax.numpy as jnp
from jax import lax
from jax.experimental import pallas as pl
from jax.experimental.pallas import tpu as pltpu
from jax.sharding import PartitionSpec as P

F32 = jnp.float32
BF16 = jnp.bfloat16
MESH_ID = pl.DeviceIdType.MESH
GX = 128
GY = 128
COLS = 4
NT1 = 16
NT2 = 4
C3L = 32
CORES = 2
CHIPS_Z = 8
TOP = 16
EXT_ROWS = 160
EXT_LANES = 256
WEST, EAST, SOUTH, NORTH = 0, 1, 2, 3
STEPS = ((-1, 0), (1, 0), (0, -1), (0, 1), (-1, -1), (-1, 1), (1, -1), (1, 1))
FACING = (1, 0, 3, 2, 7, 6, 5, 4)
shift_value = 0.1
jacobi_weight = 0.6
smooth_weight = 0.5


def iota(shape, dim):
    return lax.broadcasted_iota(jnp.int32, shape, dim)


def dot_nt(a, b):
    return lax.dot_general(a, b, (((1,), (1,)), ((), ())), preferred_element_type=F32)


def dot_nn(a, b):
    return lax.dot_general(a, b, (((1,), (0,)), ((), ())), preferred_element_type=F32)


def matmul(a, b):
    return jnp.dot(a, b, precision=lax.Precision.HIGHEST, preferred_element_type=F32)


def upper():
    return iota((8, 128), 0) < 4


def left():
    return iota((8, 128), 1) < 64


def rounded(v):
    return v.astype(BF16).astype(F32)


def fold(o):
    return o + pltpu.roll(o, 4, 0)


def split_twin(v):
    hi = rounded(v)
    return jnp.where(upper(), hi, v - hi)


def split_pair(v):
    hi = rounded(v)
    lo = v - hi
    first = jnp.where(upper(), hi, pltpu.roll(lo, 4, 0))
    second = jnp.where(upper(), pltpu.roll(hi, 4, 0), lo)
    return first, second


def store_split(ref, m):
    hi = m.astype(BF16)
    ref[:, 0:128] = hi
    ref[:, 128:256] = (m - hi.astype(F32)).astype(BF16)


def times(v, split_map):
    a = split_twin(v).astype(BF16)
    return fold(dot_nt(jnp.concatenate([a, a], axis=1), split_map))


def kernel(
    wide_size,
    narrow_size,
    block,
    east,
    north,
    fine_groups,
    tiles_one,
    columns_one_in,
    live_one_in,
    coarse_groups_in,
    tiles_two,
    columns_two_in,
    live_two_in,
    coarser_groups_in,
    chain_forward,
    chain_gain,
    chain_backward,
    out,
    columns_one,
    live_one,
    coarse_groups,
    columns_two,
    live_two,
    coarser_groups,
    ext,
    groups_hi,
    groups_lo,
    held_one,
    held_two,
    slabs,
    packs,
    fine_box,
    weight_e,
    weight_w,
    weight_n,
    weight_s,
    inverse,
    diagonal,
    field_a,
    field_b,
    field_c,
    second,
    high_rows,
    low_rows,
    segment,
    table,
    w_one,
    w_far,
    hot_fine,
    groups_seg,
    w_two,
    picks_one,
    picks_two,
    spots_one,
    spots_two,
    hot_one,
    hot_two,
    sent_one,
    sent_two,
    box_one,
    box_two,
    pair_maps,
    pair_split,
    pair_out,
    west_map,
    west_split,
    group_box,
    own_maps,
    z_maps,
    z_split,
    prefix_u,
    suffix_v,
    suffix_w,
    x_maps,
    x_split,
    enter_split,
    box_rhs,
    box_z,
    box_x,
    enter_y,
    enter_x,
    local_sem,
    fine_send,
    fine_recv,
    send_one,
    recv_one,
    send_two,
    recv_two,
    core_send,
    core_recv,
    west_send,
    west_recv,
    group_send,
    group_recv,
    ymap_send,
    ymap_recv,
    relay_send,
    relay_recv,
    rhs_send,
    rhs_recv,
    zmap_send,
    zmap_recv,
    xmap_send,
    xmap_recv,
    z_send,
    z_recv,
    x_send,
    x_recv,
):
    w = lax.axis_index("wide")
    q = lax.axis_index("narrow")
    seg_size = CORES * CHIPS_Z
    segs = wide_size // seg_size
    xs = w // seg_size
    zs = lax.rem(w, seg_size) // CORES
    core = lax.rem(w, CORES)

    def place(step):
        return w + step[0], q + step[1]

    def exists(step):
        a, b = place(step)
        return (a >= 0) & (a < wide_size) & (b >= 0) & (b < narrow_size)

    loads = (
        (block, ext.at[pl.ds(0, 4), pl.ds(TOP, GX), pl.ds(0, GY)]),
        (east, ext.at[4, pl.ds(TOP, GX), pl.ds(0, GY)]),
        (north, ext.at[5, pl.ds(TOP, GX), pl.ds(0, GY)]),
        (chain_forward.at[0], pair_maps.at[core, 0]),
        (chain_gain.at[0], pair_maps.at[core, 1]),
        (chain_backward.at[0], pair_maps.at[core, 2]),
        (fine_groups, groups_lo),
        (tiles_two, held_two),
        (tiles_one, held_one),
        (columns_one_in, columns_one),
        (live_one_in, live_one),
        (coarse_groups_in, coarse_groups),
        (columns_two_in, columns_two),
        (live_two_in, live_two),
        (coarser_groups_in, coarser_groups),
    )
    local = [pltpu.make_async_copy(a, b, local_sem.at[i]) for i, (a, b) in enumerate(loads)]
    barrier = pltpu.get_barrier_semaphore()
    for i in (4, 3, 5, 2, 6, 1, 7):
        mate = (xs * seg_size + lax.rem(zs + i, CHIPS_Z) * CORES + core, q)
        pl.semaphore_signal(barrier, inc=1, device_id=mate, device_id_type=MESH_ID)
    for i in range(1, segs):
        mate = (lax.rem(xs + i, segs) * seg_size + zs * CORES + core, q)
        pl.semaphore_signal(barrier, inc=1, device_id=mate, device_id_type=MESH_ID)
    awaited = jnp.int32(0)
    for step in STEPS:
        there = exists(step)
        a, b = place(step)

        @pl.when(there)
        def _():
            pl.semaphore_signal(barrier, inc=1, device_id=(a, b), device_id_type=MESH_ID)

        awaited = awaited + jnp.where(there, 1, 0)
    group = [(i, j) for i in range(CORES) for j in range(narrow_size)]
    for i, j in group[1:]:
        mate = (w - core + lax.rem(core + i, CORES), lax.rem(q + j, narrow_size))
        pl.semaphore_signal(barrier, inc=1, device_id=mate, device_id_type=MESH_ID)
    awaited = awaited + len(group) - 1 + CHIPS_Z - 1 + segs - 1

    for i in (0, 1, 2, 3, 4, 5, 14, 6, 9, 10, 11, 12, 13, 7, 8):
        local[i].start()

    def fine_start(turn, source, arrays):
        lane = iota((8, 128), 1) // 4
        for a in range(arrays):
            slabs[turn, 0, a] = source[a, TOP : TOP + 8, 0:128]
            slabs[turn, 1, a] = source[a, TOP + GX - 8 : TOP + GX, 0:128]
            packed = jnp.zeros((8, 128), F32)
            for g in range(GX // 8):
                v = source[a, TOP + 8 * g : TOP + 8 * g + 8, 0:128]
                packed = jnp.where(lane == g, v if g == 0 else pltpu.roll(v, 4 * g, 1), packed)
                packed = jnp.where(lane == 16 + g, pltpu.roll(v, (68 + 4 * g) % 128, 1), packed)
            packs[turn, a] = packed

    def fine_copy(turn, arrays, d, landing):
        span = pl.ds(0, arrays)
        source = slabs.at[turn, d, span] if d < 2 else packs.at[turn, span]
        return pltpu.make_async_remote_copy(
            src_ref=source,
            dst_ref=fine_box.at[turn, landing, span],
            send_sem=fine_send.at[turn, d],
            recv_sem=fine_recv.at[turn, landing],
            device_id=place(STEPS[d]),
            device_id_type=MESH_ID,
        )

    def fine_send_all(turn, arrays):
        for d, step in enumerate(STEPS):

            @pl.when(exists(step))
            def _():
                fine_copy(turn, arrays, d, FACING[d]).start()

    def fine_wait(turn, arrays):
        for d, step in enumerate(STEPS):

            @pl.when(exists(step))
            def _():
                fine_copy(turn, arrays, d, d).wait_recv()
                fine_copy(turn, arrays, d, FACING[d]).wait_send()

    def fine_fill(turn, target, arrays):
        lane = iota((8, 128), 1)
        there = [exists(step) for step in STEPS]

        def got(d, a):
            return jnp.where(there[d], fine_box[turn, d, a], 0.0)

        def beside(south_pack, south_group, north_pack, north_group):
            low = pltpu.roll(south_pack, (124 - 64 - 4 * south_group) % 128, 1)
            high = pltpu.roll(north_pack, (128 - 4 * north_group) % 128, 1)
            return jnp.where(lane < 4, high, jnp.where(lane >= 124, low, 0.0))

        for a in range(arrays):
            target[a, TOP - 8 : TOP, 0:128] = got(0, a)
            target[a, TOP + GX : TOP + GX + 8, 0:128] = got(1, a)
            south_pack, north_pack = got(2, a), got(3, a)
            for g in range(GX // 8):
                target[a, TOP + 8 * g : TOP + 8 * g + 8, 128:256] = beside(south_pack, g, north_pack, g)
            target[a, TOP - 8 : TOP, 128:256] = beside(got(4, a), 15, got(5, a), 15)
            target[a, TOP + GX : TOP + GX + 8, 128:256] = beside(got(6, a), 0, got(7, a), 0)

    local[0].wait()
    local[1].wait()
    local[2].wait()
    fine_start(0, ext, 6)
    pl.semaphore_wait(barrier, awaited)
    fine_send_all(0, 6)

    local[3].wait()
    local[4].wait()
    local[5].wait()

    def core_copy(landing):
        return pltpu.make_async_remote_copy(
            src_ref=pair_maps.at[core],
            dst_ref=pair_maps.at[landing],
            send_sem=core_send,
            recv_sem=core_recv,
            device_id=(w - core + (1 - core), q),
            device_id_type=MESH_ID,
        )

    def west_copy():
        return pltpu.make_async_remote_copy(
            src_ref=pair_maps.at[core, 2],
            dst_ref=west_map,
            send_sem=west_send,
            recv_sem=west_recv,
            device_id=(w + 1, q),
            device_id_type=MESH_ID,
        )

    def group_copy(d, landing):
        return pltpu.make_async_remote_copy(
            src_ref=coarser_groups,
            dst_ref=group_box.at[landing],
            send_sem=group_send.at[d],
            recv_sem=group_recv.at[landing],
            device_id=place(STEPS[d]),
            device_id_type=MESH_ID,
        )

    feeds_east = (core == CORES - 1) & (w < wide_size - 1)
    fed_from_west = (core == 0) & (w > 0)
    local[14].wait()
    core_copy(core).start()

    @pl.when(feeds_east)
    def _():
        west_copy().start()

    for d in range(4):

        @pl.when(exists(STEPS[d]))
        def _():
            group_copy(d, FACING[d]).start()


    eye_one = iota((128, 128), 0) == iota((128, 128), 1)

    def peer_copy(source, target, sends, receives, slot, landing, mate):
        return pltpu.make_async_remote_copy(
            src_ref=source,
            dst_ref=target.at[landing],
            send_sem=sends.at[slot],
            recv_sem=receives.at[landing],
            device_id=mate,
            device_id_type=MESH_ID,
        )

    def z_mate(i):
        z = lax.rem(zs + i, CHIPS_Z)
        return z, (xs * seg_size + z * CORES + core, q)

    def x_mate(i):
        x = lax.rem(xs + i, segs)
        return x, (x * seg_size + zs * CORES + core, q)

    def along(mates, count, box, sends, receives, mine):
        def start():
            for i in range(1, count):
                _, mate = mates(i)
                peer_copy(box.at[mine], box, sends, receives, i, mine, mate).start()

        def finish():
            for i in range(1, count):
                other, mate = mates(i)
                peer_copy(box.at[mine], box, sends, receives, i, other, mate).wait_recv()
                peer_copy(box.at[mine], box, sends, receives, i, mine, mate).wait_send()

        return start, finish

    z_start, z_finish = along(z_mate, CHIPS_Z, box_z, z_send, z_recv, zs)
    x_start, x_finish = along(x_mate, segs, box_x, x_send, x_recv, xs)
    z_order = (1, 7, 2, 6, 3, 5, 4)

    piece_rows = pl.ds(pl.multiple_of(192 * core + 48 * q, 16), 48)

    def zmap_copy(i, landing, mate):
        return pltpu.make_async_remote_copy(
            src_ref=own_maps.at[piece_rows],
            dst_ref=z_maps.at[landing, piece_rows],
            send_sem=zmap_send.at[i],
            recv_sem=zmap_recv.at[landing],
            device_id=mate,
            device_id_type=MESH_ID,
        )

    def ymap_copy(i, z, other):
        rows = pl.ds(pl.multiple_of(192 * core + 48 * other, 16), 48)
        return pltpu.make_async_remote_copy(
            src_ref=z_maps.at[z, rows],
            dst_ref=z_maps.at[z, rows],
            send_sem=ymap_send.at[i, z],
            recv_sem=ymap_recv.at[other, z],
            device_id=(w, lax.rem(q + i, narrow_size)),
            device_id_type=MESH_ID,
        )

    def relay_copy(side):
        half = pl.ds(pl.multiple_of(192 * side, 64), 192)
        return pltpu.make_async_remote_copy(
            src_ref=z_maps.at[:, half],
            dst_ref=z_maps.at[:, half],
            send_sem=relay_send,
            recv_sem=relay_recv,
            device_id=(w - core + (1 - core), q),
            device_id_type=MESH_ID,
        )

    def pair_products():
        core_copy(1 - core).wait_recv()
        core_copy(core).wait_send()
        f0, b0 = pair_maps[0, 0], pair_maps[0, 2]
        f1, b1 = pair_maps[1, 0], pair_maps[1, 2]
        both = matmul(f1, f0)
        own_maps[0:128] = both
        own_maps[128:256] = matmul(b0, b1)
        own_maps[256:384] = f0 + matmul(b0, both)
        z_maps[zs, piece_rows] = own_maps[piece_rows]
        for i in z_order:
            _, mate = z_mate(i)
            zmap_copy(i, zs, mate).start()

    def pair_gains():
        g0, b0 = pair_maps[0, 1], pair_maps[0, 2]
        f1, g1 = pair_maps[1, 0], pair_maps[1, 1]
        across = matmul(f1, g0)
        store_split(pair_split.at[0:128, 0:256], across)
        store_split(pair_split.at[0:128, 256:512], g1)
        store_split(pair_split.at[128:256, 0:256], g0 + matmul(b0, across))
        store_split(pair_split.at[128:256, 256:512], matmul(b0, g1))

    def ymap_start(z):
        for i in range(1, narrow_size):
            ymap_copy(i, z, q).start()

    def zmap_take(order):
        for i in order:
            other, mate = z_mate(i)
            zmap_copy(i, other, mate).wait_recv()
            zmap_copy(i, zs, mate).wait_send()
            ymap_start(other)

    def zmap_near():
        ymap_start(zs)
        zmap_take(z_order[:4])

    def zmap_far():
        zmap_take(z_order[4:])

    def zmap_relay():
        for i in range(1, narrow_size):
            for z in range(CHIPS_Z):
                ymap_copy(i, z, lax.rem(q + i, narrow_size)).wait_recv()
                ymap_copy(i, z, q).wait_send()
        relay_copy(core).start()

    def times_map(split_map, m):
        hi = m.astype(BF16)
        lo = (m - hi.astype(F32)).astype(BF16)
        lhs = jnp.concatenate([split_map, split_map[:, 0:128]], axis=1)
        return dot_nn(lhs, jnp.concatenate([hi, hi, lo], axis=0))

    def z_prefix():
        relay_copy(1 - core).wait_recv()
        relay_copy(core).wait_send()

        def split_one(p, carry):
            for j in range(3):
                store_split(z_split.at[p, j], z_maps[p, 128 * j : 128 * j + 128])
            return carry

        lax.fori_loop(0, CHIPS_Z, split_one, 0)
        one_map = jnp.where(eye_one, 1.0, 0.0)
        prefix_u[0] = one_map
        suffix_w[CHIPS_Z] = one_map

        def one(p, carry):
            prefix_u[p + 1] = times_map(z_split[p, 0], prefix_u[p])
            r = CHIPS_Z - 1 - p
            suffix_w[r] = times_map(z_split[r, 1], suffix_w[r + 1])
            return carry

        lax.fori_loop(0, CHIPS_Z, one, 0)
        x_maps[xs, 0] = prefix_u[CHIPS_Z]
        x_maps[xs, 1] = suffix_w[0]

    def xmap_copy(part, i, landing, mate):
        return pltpu.make_async_remote_copy(
            src_ref=x_maps.at[xs, part],
            dst_ref=x_maps.at[landing, part],
            send_sem=xmap_send.at[part, i],
            recv_sem=xmap_recv.at[part, landing],
            device_id=mate,
            device_id_type=MESH_ID,
        )

    def has_map(part, source, target):
        if part == 0:
            return (source > 0) & (source < segs - 1)
        if part == 1:
            return (source < segs - 1) & (target < source)
        return target < source

    def z_suffix():
        suffix_v[CHIPS_Z] = jnp.zeros((128, 128), F32)

        def one(i, carry):
            p = CHIPS_Z - 1 - i
            suffix_v[p] = times_map(z_split[p, 1], suffix_v[p + 1]) + times_map(
                z_split[p, 2], prefix_u[p]
            )
            return carry

        lax.fori_loop(0, CHIPS_Z, one, 0)
        x_maps[xs, 2] = suffix_v[0]
        for part in range(3):
            for i in range(1, segs):
                other, mate = x_mate(i)

                @pl.when(has_map(part, xs, other))
                def _():
                    xmap_copy(part, i, xs, mate).start()

    def z_composites():
        z_prefix()
        z_suffix()

    def z_splits():
        store_split(enter_split.at[0], prefix_u[zs])
        store_split(enter_split.at[1], suffix_v[zs + 1])
        store_split(enter_split.at[2], suffix_w[zs + 1])
        pair_out[0:128, 0:256] = z_split[zs, 2]
        pair_out[0:128, 256:512] = z_split[zs, 1]
        pair_out[128:256, 0:256] = z_split[zs, 0]
        store_split(pair_out.at[128:256, 256:512], pair_maps[1, 2])

        @pl.when(fed_from_west)
        def _():
            west_copy().wait_recv()

        @pl.when(feeds_east)
        def _():
            west_copy().wait_send()

        store_split(west_split, west_map[...])
        for d in range(4):

            @pl.when(exists(STEPS[d]))
            def _():
                group_copy(d, d).wait_recv()
                group_copy(d, FACING[d]).wait_send()

            mark_two(d + 1, group_box[d], q + STEPS[d][1])

    def x_splits():
        for part in range(3):
            for i in range(1, segs):
                other, mate = x_mate(i)

                @pl.when(has_map(part, other, xs))
                def _():
                    xmap_copy(part, i, other, mate).wait_recv()

                @pl.when(has_map(part, xs, other))
                def _():
                    xmap_copy(part, i, xs, mate).wait_send()

        for p in range(1, segs):
            for j in range(3):
                if j == 2 or p < segs - 1:
                    store_split(x_split.at[p, j], x_maps[p, j])

    local[6].wait()
    groups = groups_lo[...]
    groups_hi[...] = groups // 128
    groups_lo[...] = lax.rem(groups, 128)
    groups_seg[...] = groups // 256
    turned = jnp.transpose(lax.rem(groups, 256).astype(F32))
    wide_lane = iota((GY, 256), 1).astype(F32)
    for i in range(GX):
        hot = turned[:, i : i + 1] == wide_lane
        hot_fine[GY * i : GY * i + GY, :] = jnp.where(hot, 1.0, 0.0).astype(BF16)
    for i in range(9, 14):
        local[i].wait()
    for r in range(NT1):
        for k in range(3):
            spots_one[3 * r + k] = jnp.where(live_one[k, r] == 1, columns_one[k, r], 5 * NT1)
    for r in range(NT2):
        for k in range(3):
            spots_two[3 * r + k] = jnp.where(live_two[r, k] == 1, columns_two[r, k], 5 * NT2)
    picks_one[5 * NT1] = jnp.zeros((8, 128), F32)
    picks_two[5 * NT2] = jnp.zeros((8, 128), F32)
    local[7].wait()
    lane_two = iota((64, 128), 1)
    eye_two = iota((64, 128), 0) == lax.rem(lane_two, 64)
    diag_two = []
    for r in range(NT2):
        for k in range(4):
            m = held_two[r, k]
            m = jnp.concatenate([m, m], axis=1)
            if k == 0:
                diag_two.append(jnp.sum(jnp.where(eye_two, m, 0.0), axis=0, keepdims=True))
            hi = rounded(m)
            m = jnp.where(lane_two < 64, hi, m - hi).astype(BF16)
            w_two[r, 0:64, 128 * k : 128 * k + 128] = m
            w_two[r, 64:128, 128 * k : 128 * k + 128] = m
    wide_two = [jnp.broadcast_to(d, (8, 128)) for d in diag_two]
    inverse_two = 1.0 / jnp.where(
        upper(),
        jnp.where(left(), wide_two[0], wide_two[1]),
        jnp.where(left(), wide_two[2], wide_two[3]),
    )
    for t in range(NT1):
        hot = iota((256, 128), 0) == coarse_groups[t : t + 1, :]
        hot_one[:, 128 * t : 128 * t + 128] = jnp.where(hot, 1.0, 0.0).astype(BF16)

    def mark_two(p, groups, owner):
        for h in range(2):
            hot = iota((128, 128), 0) == groups[h : h + 1, :] + C3L * owner
            hot_two[p, :, 128 * h : 128 * h + 128] = jnp.where(hot, 1.0, 0.0).astype(BF16)

    mark_two(0, coarser_groups[...], q)
    pair_products()
    local[8].wait()

    def split_tiles(t, carry):
        diags = []
        for r in (t, t + 8):
            for k in range(4):
                m = held_one[r, k]
                if k == 0:
                    diags.append(jnp.sum(jnp.where(eye_one, m, 0.0), axis=0, keepdims=True))
                    store_split(w_one.at[r], m)
                else:
                    m = jnp.transpose(m)
                    hi = m.astype(BF16)
                    w_far[r, 256 * k - 256 : 256 * k - 128, :] = hi
                    w_far[r, 256 * k - 128 : 256 * k, :] = (m - hi.astype(F32)).astype(BF16)
        low, high = (jnp.broadcast_to(d, (8, 128)) for d in diags)
        table[t] = 1.0 / jnp.where(upper(), low, high)
        return carry

    lax.fori_loop(0, 8, split_tiles, 0)
    inverse_one = table[...]
    pair_gains()

    fine_wait(0, 6)
    fine_fill(0, ext, 6)
    rows_all = range(8, EXT_ROWS - 8, 8)
    last_row = wide_size * GX - 1
    last_column = narrow_size * GY - 1
    lane_ext = iota((8, EXT_LANES), 1)
    column = q * GY + jnp.where(lane_ext < 192, lane_ext, lane_ext - EXT_LANES)
    for o in rows_all:
        row = w * GX + (o - TOP) + iota((8, EXT_LANES), 0)
        ext[4, o : o + 8, :] = jnp.where(row < last_row, ext[4, o : o + 8, :], 0.0)
        ext[5, o : o + 8, :] = jnp.where(column < last_column, ext[5, o : o + 8, :], 0.0)
    for o in rows_all:
        e = ext[4, o : o + 8, :]
        b = ext[4, o - 1 : o + 7, :]
        n = ext[5, o : o + 8, :]
        s = pltpu.roll(n, 1, 1)
        d = shift_value + e + b + n + s
        inv = 1.0 / d
        weight_e[o - 8 : o, :] = e * inv
        weight_w[o - 8 : o, :] = b * inv
        weight_n[o - 8 : o, :] = n * inv
        weight_s[o - 8 : o, :] = s * inv
        if TOP <= o < TOP + GX:
            diagonal[o - TOP : o - TOP + 8, :] = d[:, 0:128]
        for c in range(COLS):
            field_a[c, o : o + 8, :] = ext[c, o : o + 8, :] * inv

    def mixed(source, c, o):
        v = source[c, o : o + 8, :]
        a = weight_e[o - 8 : o, :] * source[c, o + 1 : o + 9, :]
        b = weight_w[o - 8 : o, :] * source[c, o - 1 : o + 7, :]
        n = weight_n[o - 8 : o, :] * pltpu.roll(v, EXT_LANES - 1, 1)
        s = weight_s[o - 8 : o, :] * pltpu.roll(v, 1, 1)
        return v, (a + b) + (n + s)

    rows_in = range(TOP, TOP + GX, 8)
    rest = 1.0 - jacobi_weight
    for o in rows_all:
        for c in range(COLS):
            v, m = mixed(field_a, c, o)
            field_b[c, o : o + 8, :] = rest * v + jacobi_weight * m
    for o in rows_all:
        for c in range(COLS):
            v, m = mixed(field_b, c, o)
            field_c[c, o : o + 8, :] = rest * v + jacobi_weight * m
    for o in rows_in:
        i = o - TOP
        for c in range(COLS):
            v, m = mixed(field_c, c, o)
            r = ((1.0 - smooth_weight) * v + smooth_weight * m)[:, 0:128] * diagonal[i : i + 8, :]
            both = field_a[c, o : o + 8, 0:128] + field_b[c, o : o + 8, 0:128]
            second[c, i : i + 8, :] = jacobi_weight * both
            hi = rounded(r)
            lo = r - hi
            for h in range(2):
                high_rows[pl.ds(8 * i + 4 * h + c, 8, stride=8), :] = hi
                low_rows[pl.ds(8 * i + 4 * h + c, 8, stride=8), :] = lo

    segment[...] = jnp.zeros((64, 256), F32)
    half = jnp.where(upper(), 0, 4)
    chunk = 16

    def gather_up(step, carry):
        lhs = []
        for j in range(chunk):
            i = step * chunk + j
            index = jnp.broadcast_to(groups_seg[pl.ds(i, 1), :], (8, 128))
            at = pl.multiple_of(8 * i, 8)
            v_hi = high_rows[pl.ds(at, 8), :]
            v_lo = low_rows[pl.ds(at, 8), :]
            masks = [index == half + t for t in range(4)]
            rows = [jnp.where(m, v_hi, 0.0) for m in masks] + [jnp.where(m, v_lo, 0.0) for m in masks]
            lhs.append(jnp.concatenate(rows, axis=0).astype(BF16))
        span = pl.ds(pl.multiple_of(step * (chunk * GY), chunk * GY), chunk * GY)
        segment[...] += dot_nn(jnp.concatenate(lhs, axis=1), hot_fine[span, :])
        return carry

    lax.fori_loop(0, GX // chunk, gather_up, 0)
    folded = segment[0:32, :] + segment[32:64, :]
    right_one = jnp.stack(
        [folded[8 * (t // 2) : 8 * (t // 2) + 8, 128 * (t % 2) : 128 * (t % 2) + 128] for t in range(8)]
    )

    def coarse_copy(sent, box, sends, receives, k, d, landing):
        return pltpu.make_async_remote_copy(
            src_ref=sent.at[k],
            dst_ref=box.at[k, landing],
            send_sem=sends.at[k, d],
            recv_sem=receives.at[k, landing],
            device_id=place(STEPS[d]),
            device_id_type=MESH_ID,
        )

    def coarse_send(bufs, k):
        for d in range(4):

            @pl.when(exists(STEPS[d]))
            def _():
                coarse_copy(*bufs, k, d, FACING[d]).start()

    def coarse_wait(bufs, k, sides=range(4)):
        for d in sides:

            @pl.when(exists(STEPS[d]))
            def _():
                coarse_copy(*bufs, k, d, d).wait_recv()
                coarse_copy(*bufs, k, d, FACING[d]).wait_send()

    bufs_one = (sent_one, box_one, send_one, recv_one)
    bufs_two = (sent_two, box_two, send_two, recv_two)

    def put_one(p, t, v):
        a, b = split_pair(v)
        picks_one[NT1 * p + t] = a
        picks_one[NT1 * p + t + 8] = b

    def apply_one(k, field, meanwhile=None):
        sent_one[k] = field
        coarse_send(bufs_one, k)
        for t in range(8):
            put_one(0, t, field[t])
        own = []
        for r in range(NT1):
            a = picks_one[r].astype(BF16)
            own.append(dot_nt(jnp.concatenate([a, a], axis=1), w_one[r]))
        own = [jnp.where(upper(), fold(own[t]), fold(own[t + 8])) for t in range(8)]
        if meanwhile is not None:
            meanwhile()
        for d in (SOUTH, NORTH, WEST, EAST):
            coarse_wait(bufs_one, k, (d,))
            there = exists(STEPS[d])
            for t in range(8):
                put_one(d + 1, t, jnp.where(there, box_one[k, d, t], 0.0))
        outs = []
        for r in range(NT1):
            parts = []
            for j in range(3):
                a = picks_one[spots_one[3 * r + j]].astype(BF16)
                parts += [a, a]
            outs.append(dot_nn(jnp.concatenate(parts, axis=1), w_far[r]))
        return jnp.stack(
            [own[t] + jnp.where(upper(), fold(outs[t]), fold(outs[t + 8])) for t in range(8)]
        )

    def put_two(p, v):
        for h, a in enumerate(split_pair(v)):
            turned = pltpu.roll(a, 64, 1)
            picks_two[NT2 * p + 2 * h] = jnp.where(left(), a, turned)
            picks_two[NT2 * p + 2 * h + 1] = jnp.where(left(), turned, a)

    def apply_two(k, field, meanwhile=None):
        sent_two[k] = field
        coarse_send(bufs_two, k)
        put_two(0, field)
        if meanwhile is not None:
            meanwhile()
        coarse_wait(bufs_two, k)
        for d in range(4):
            put_two(d + 1, jnp.where(exists(STEPS[d]), box_two[k, d], 0.0))
        return product_two()

    def product_two():
        outs = []
        for r in range(NT2):
            parts = [picks_two[r]] + [picks_two[spots_two[3 * r + j]] for j in range(3)]
            lhs = jnp.concatenate([a.astype(BF16) for a in parts], axis=1)
            outs.append(fold(dot_nt(lhs, w_two[r])))
        return jnp.where(
            upper(), jnp.where(left(), outs[0], outs[1]), jnp.where(left(), outs[2], outs[3])
        )

    def down(apply_op, inv, right, windows):
        s0 = inv * right
        r1 = right - jacobi_weight * apply_op(0, s0, windows[0])
        s1 = inv * r1
        r2 = r1 - jacobi_weight * apply_op(1, s1, windows[1])
        s2 = inv * r2
        r3 = r2 - smooth_weight * apply_op(2, s2, windows[2])
        return r3, r2, jacobi_weight * (s0 + s1)

    def up(apply_op, inv, spread, applied, r2, x2):
        fix = spread - smooth_weight * (inv * applied)
        r3 = r2 - apply_op(4, fix)
        s3 = inv * r3
        r4 = r3 - jacobi_weight * apply_op(5, s3)
        return x2 + fix + jacobi_weight * s3 + jacobi_weight * (inv * r4)

    def joined(a, b):
        a, b = split_twin(a).astype(BF16), split_twin(b).astype(BF16)
        return jnp.concatenate([a, a, b, b], axis=1)

    def sweep(count, maps, box, total):
        y = box[0, 0]
        enter_y[0] = jnp.zeros((8, 128), F32)
        lifted = [box[0, 1]]
        for p in range(1, count):
            enter_y[p] = y
            lifted.append(box[p, 1] + times(y, maps[p, 2]))
            if total or p < count - 1:
                y = box[p, 0] + times(y, maps[p, 0])
        x = lifted[count - 1]
        enter_x[count - 1] = jnp.zeros((8, 128), F32)
        for p in reversed(range(count - 1)):
            enter_x[p] = x
            if total or p > 0:
                x = lifted[p] + times(x, maps[p, 1])
        return y, x

    def chain_solve(piece):
        slot = core * narrow_size + q
        box_rhs[slot] = piece

        def rhs_copy(i, j, landing):
            mate = (w - core + lax.rem(core + i, CORES), lax.rem(q + j, narrow_size))
            return peer_copy(
                box_rhs.at[slot], box_rhs, rhs_send, rhs_recv, i * narrow_size + j, landing, mate
            )

        for i, j in group[1:]:
            rhs_copy(i, j, slot).start()
        z_splits()
        for i, j in group[1:]:
            other = lax.rem(core + i, CORES) * narrow_size + lax.rem(q + j, narrow_size)
            rhs_copy(i, j, other).wait_recv()
            rhs_copy(i, j, slot).wait_send()
        sums = []
        for i in range(CORES):
            total = box_rhs[i * narrow_size]
            for j in range(1, narrow_size):
                total = total + box_rhs[i * narrow_size + j]
            sums.append(total)
        both = fold(dot_nt(joined(*sums), pair_split[...]))
        ahead, behind = both[:, 0:128], both[:, 128:256]
        box_z[zs, 0] = ahead
        box_z[zs, 1] = behind
        z_start()
        z_finish()
        y, x = sweep(CHIPS_Z, z_split, box_z, True)
        box_x[xs, 0] = y
        box_x[xs, 1] = x
        x_start()
        y_in, x_in = enter_y[zs], enter_x[zs]
        x_splits()
        x_finish()
        sweep(segs, x_split, box_x, False)
        y_far, x_far = enter_y[xs], enter_x[xs]
        y_in = y_in + times(y_far, enter_split[0])
        x_in = x_in + times(y_far, enter_split[1]) + times(x_far, enter_split[2])
        both = fold(dot_nt(joined(y_in, x_in), pair_out[...]))
        x_first, x_last = behind + both[:, 0:128], ahead + both[:, 128:256]
        x_before = y_in + times(x_first, west_split[...])
        inner = core == 0
        return (
            jnp.where(inner, x_first, x_last),
            jnp.where(inner, x_before, x_first),
            jnp.where(inner, x_last, x_in),
        )

    def halves(pair):
        return jnp.concatenate([a.astype(BF16) for a in pair], axis=1)

    def pack_two(o):
        o = fold(o)
        return jnp.where(upper(), o[:, 0:128], o[:, 128:256])

    def restrict_one(field):
        pairs = [split_pair(field[t]) for t in range(8)]
        tiles = [p[0] for p in pairs] + [p[1] for p in pairs]
        return pack_two(dot_nt(halves(tiles), hot_one[...]))

    def prolong_one(coarse):
        o = fold(dot_nn(halves(split_pair(coarse)), hot_one[...]))
        parts = [o[:, 128 * t : 128 * t + 128] for t in range(NT1)]
        return jnp.stack([jnp.where(upper(), parts[t], parts[t + 8]) for t in range(8)])

    r_one, r2_one, x2_one = down(apply_one, inverse_one, right_one, (zmap_near, zmap_far, None))
    right_two = restrict_one(r_one)
    r_two, r2_two, x2_two = down(apply_two, inverse_two, right_two, (zmap_relay, z_composites, None))
    piece = fold(dot_nt(halves(split_pair(r_two)), hot_two[0]))
    answers = chain_solve(piece)

    def spread_two(p, answer):
        return pack_two(dot_nn(split_twin(answer).astype(BF16), hot_two[p]))

    spread = spread_two(0, answers[0])
    put_two(0, spread)
    for d, answer in enumerate((answers[1], answers[2], answers[0], answers[0])):
        put_two(d + 1, jnp.where(exists(STEPS[d]), spread_two(d + 1, answer), 0.0))
    answer_two = up(apply_two, inverse_two, spread, product_two(), r2_two, x2_two)
    spread = prolong_one(answer_two)
    answer_one = up(apply_one, inverse_one, spread, apply_one(3, spread), r2_one, x2_one)
    table[...] = answer_one

    def spread_rows(k, carry):
        at = pl.multiple_of(8 * k, 8)
        hi_index = groups_hi[pl.ds(at, 8), :]
        lo_index = groups_lo[pl.ds(at, 8), :]
        for c in range(COLS):
            total = jnp.zeros((8, 128), F32)
            for t in range(NT1):
                j = 4 * (t // 8) + c
                row = jnp.broadcast_to(table[t % 8, j : j + 1, :], (8, 128))
                value = jnp.take_along_axis(row, lo_index, axis=1, mode="promise_in_bounds")
                total = jnp.where(hi_index == t, value, total)
            field_a[c, pl.ds(pl.multiple_of(TOP + at, 8), 8), 0:128] = total
        return carry

    lax.fori_loop(0, GX // 8, spread_rows, 0, unroll=4)
    fine_start(1, field_a, 4)
    fine_send_all(1, 4)
    fine_wait(1, 4)
    fine_fill(1, field_a, 4)
    for o in rows_all:
        for c in range(COLS):
            v, m = mixed(field_a, c, o)
            field_b[c, o : o + 8, :] = (1.0 - smooth_weight) * v + smooth_weight * m
    for o in rows_all:
        for c in range(COLS):
            v, m = mixed(field_b, c, o)
            field_a[c, o : o + 8, :] = field_c[c, o : o + 8, :] - v + m
    for o in rows_in:
        i = o - TOP
        for c in range(COLS):
            v, m = mixed(field_a, c, o)
            x3 = second[c, i : i + 8, :] + field_b[c, o : o + 8, 0:128]
            s4 = rest * v + jacobi_weight * m
            out[c, i : i + 8, :] = x3 + jacobi_weight * (v + s4)[:, 0:128]


def solution(mesh):
    wide_size, narrow_size = mesh.shape["wide"], mesh.shape["narrow"]
    segs = wide_size // (CORES * CHIPS_Z)

    def body(
        block,
        east,
        north,
        fine_groups,
        tiles_one,
        columns_one,
        live_one,
        coarse_groups,
        tiles_two,
        columns_two,
        live_two,
        coarser_groups,
        chain_forward,
        chain_gain,
        chain_backward,
    ):
        hbm = pl.BlockSpec(memory_space=pl.ANY)
        vmem = pl.BlockSpec(memory_space=pltpu.VMEM)
        dma = pltpu.SemaphoreType.DMA
        big = pltpu.VMEM((COLS, EXT_ROWS, EXT_LANES), F32)
        weight = pltpu.VMEM((EXT_ROWS - 16, EXT_LANES), F32)
        square = pltpu.VMEM((GX, GY), F32)
        indices = pltpu.VMEM((GX, GY), jnp.int32)

        def kernel_fn(*refs):
            kernel(wide_size, narrow_size, *refs)

        return pl.pallas_call(
            kernel_fn,
            out_shape=pltpu.VMEM((COLS, GX, GY), F32),
            in_specs=[hbm] * 15,
            out_specs=vmem,
            scratch_shapes=[
                pltpu.SMEM((3, NT1), jnp.int32),
                pltpu.SMEM((3, NT1), jnp.int32),
                pltpu.VMEM((16, 128), jnp.int32),
                pltpu.SMEM((NT2, 3), jnp.int32),
                pltpu.SMEM((NT2, 3), jnp.int32),
                pltpu.VMEM((2, 128), jnp.int32),
                pltpu.VMEM((6, EXT_ROWS, EXT_LANES), F32),
                indices,
                indices,
                pltpu.VMEM((NT1, 4, 128, 128), F32),
                pltpu.VMEM((NT2, 4, 64, 64), F32),
                pltpu.VMEM((2, 2, 6, 8, 128), F32),
                pltpu.VMEM((2, 6, 8, 128), F32),
                pltpu.VMEM((2, 8, 6, 8, 128), F32),
                weight,
                weight,
                weight,
                weight,
                weight,
                square,
                big,
                big,
                big,
                pltpu.VMEM((COLS, GX, GY), F32),
                pltpu.VMEM((8 * GX, GY), F32),
                pltpu.VMEM((8 * GX, GY), F32),
                pltpu.VMEM((64, 256), F32),
                pltpu.VMEM((8, 8, 128), F32),
                pltpu.VMEM((NT1, 128, 256), BF16),
                pltpu.VMEM((NT1, 768, 128), BF16),
                pltpu.VMEM((GX * GY, 256), BF16),
                indices,
                pltpu.VMEM((NT2, 128, 512), BF16),
                pltpu.VMEM((5 * NT1 + 1, 8, 128), F32),
                pltpu.VMEM((5 * NT2 + 1, 8, 128), F32),
                pltpu.SMEM((3 * NT1,), jnp.int32),
                pltpu.SMEM((3 * NT2,), jnp.int32),
                pltpu.VMEM((256, 2048), BF16),
                pltpu.VMEM((5, 128, 256), BF16),
                pltpu.VMEM((6, 8, 8, 128), F32),
                pltpu.VMEM((6, 8, 128), F32),
                pltpu.VMEM((6, 4, 8, 8, 128), F32),
                pltpu.VMEM((6, 4, 8, 128), F32),
                pltpu.VMEM((CORES, 3, 128, 128), F32),
                pltpu.VMEM((256, 512), BF16),
                pltpu.VMEM((256, 512), BF16),
                square,
                pltpu.VMEM((128, 256), BF16),
                pltpu.VMEM((4, 2, 128), jnp.int32),
                pltpu.VMEM((384, 128), F32),
                pltpu.VMEM((CHIPS_Z, 384, 128), F32),
                pltpu.VMEM((CHIPS_Z, 3, 128, 256), BF16),
                pltpu.VMEM((CHIPS_Z + 1, 128, 128), F32),
                pltpu.VMEM((CHIPS_Z + 1, 128, 128), F32),
                pltpu.VMEM((CHIPS_Z + 1, 128, 128), F32),
                pltpu.VMEM((segs, 3, 128, 128), F32),
                pltpu.VMEM((segs, 3, 128, 256), BF16),
                pltpu.VMEM((3, 128, 256), BF16),
                pltpu.VMEM((CORES * narrow_size, 8, 128), F32),
                pltpu.VMEM((CHIPS_Z, 2, 8, 128), F32),
                pltpu.VMEM((segs, 2, 8, 128), F32),
                pltpu.VMEM((CHIPS_Z, 8, 128), F32),
                pltpu.VMEM((CHIPS_Z, 8, 128), F32),
                dma((15,)),
                dma((2, 8)),
                dma((2, 8)),
                dma((6, 4)),
                dma((6, 4)),
                dma((6, 4)),
                dma((6, 4)),
                dma,
                dma,
                dma,
                dma,
                dma((4,)),
                dma((4,)),
                dma((narrow_size, CHIPS_Z)),
                dma((narrow_size, CHIPS_Z)),
                dma,
                dma,
                dma((CORES * narrow_size,)),
                dma((CORES * narrow_size,)),
                dma((CHIPS_Z,)),
                dma((CHIPS_Z,)),
                dma((3, segs)),
                dma((3, segs)),
                dma((CHIPS_Z,)),
                dma((CHIPS_Z,)),
                dma((segs,)),
                dma((segs,)),
            ],
            compiler_params=pltpu.CompilerParams(
                collective_id=0, has_side_effects=True, vmem_limit_bytes=56 * 1024 * 1024
            ),
            name="cycle",
        )(
            block,
            east,
            north,
            fine_groups,
            tiles_one,
            columns_one.T,
            live_one.T,
            coarse_groups.reshape(16, 128),
            tiles_two,
            columns_two,
            live_two,
            coarser_groups.reshape(2, 128),
            chain_forward,
            chain_gain,
            chain_backward,
        )

    both = ("wide", "narrow")
    placed = (
        P(None, "wide", "narrow"),
        P("wide", "narrow"),
        P("wide", "narrow"),
        P("wide", "narrow"),
        P(both, None, None, None),
        P(both, None),
        P(both, None),
        P(both),
        P(both, None, None, None),
        P(both, None),
        P(both, None),
        P(both),
        P("wide", None, None),
        P("wide", None, None),
        P("wide", None, None),
    )
    return jax.shard_map(
        body, mesh=mesh, in_specs=placed, out_specs=P(None, "wide", "narrow"), check_vma=False
    )
```

```python
import jax
import jax.numpy as jnp
from jax import lax
from jax.experimental import pallas as pl
from jax.experimental.pallas import tpu as pltpu
from jax.sharding import PartitionSpec as P

F32 = jnp.float32
BF16 = jnp.bfloat16
MESH_ID = pl.DeviceIdType.MESH
GX = 128
GY = 128
COLS = 4
NT1 = 16
NT2 = 4
C3L = 32
CORES = 2
CHIPS_Z = 8
TOP = 16
EXT_ROWS = 160
EXT_LANES = 256
WEST, EAST, SOUTH, NORTH = 0, 1, 2, 3
STEPS = ((-1, 0), (1, 0), (0, -1), (0, 1), (-1, -1), (-1, 1), (1, -1), (1, 1))
FACING = (1, 0, 3, 2, 7, 6, 5, 4)
shift_value = 0.1
jacobi_weight = 0.6
smooth_weight = 0.5


def iota(shape, dim):
    return lax.broadcasted_iota(jnp.int32, shape, dim)


def dot_nt(a, b):
    return lax.dot_general(a, b, (((1,), (1,)), ((), ())), preferred_element_type=F32)


def dot_nn(a, b):
    return lax.dot_general(a, b, (((1,), (0,)), ((), ())), preferred_element_type=F32)


def matmul(a, b):
    return jnp.dot(a, b, precision=lax.Precision.HIGHEST, preferred_element_type=F32)


def upper():
    return iota((8, 128), 0) < 4


def left():
    return iota((8, 128), 1) < 64


def rounded(v):
    return v.astype(BF16).astype(F32)


def fold(o):
    return o + pltpu.roll(o, 4, 0)


def split_twin(v):
    hi = rounded(v)
    return jnp.where(upper(), hi, v - hi)


def split_pair(v):
    hi = rounded(v)
    lo = v - hi
    first = jnp.where(upper(), hi, pltpu.roll(lo, 4, 0))
    second = jnp.where(upper(), pltpu.roll(hi, 4, 0), lo)
    return first, second


def store_split(ref, m):
    hi = m.astype(BF16)
    ref[:, 0:128] = hi
    ref[:, 128:256] = (m - hi.astype(F32)).astype(BF16)


def times(v, split_map):
    a = split_twin(v).astype(BF16)
    return fold(dot_nt(jnp.concatenate([a, a], axis=1), split_map))


def kernel(
    wide_size,
    narrow_size,
    block,
    east,
    north,
    fine_groups,
    tiles_one,
    columns_one_in,
    live_one_in,
    coarse_groups_in,
    tiles_two,
    columns_two_in,
    live_two_in,
    coarser_groups_in,
    chain_forward,
    chain_gain,
    chain_backward,
    out,
    columns_one,
    live_one,
    coarse_groups,
    columns_two,
    live_two,
    coarser_groups,
    ext,
    groups_hi,
    groups_lo,
    held_one,
    held_two,
    slabs,
    packs,
    fine_box,
    weight_e,
    weight_w,
    weight_n,
    weight_s,
    inverse,
    diagonal,
    field_a,
    field_b,
    field_c,
    second,
    high_rows,
    low_rows,
    segment,
    table,
    w_one,
    w_far,
    hot_fine,
    groups_seg,
    w_two,
    picks_one,
    picks_two,
    spots_one,
    spots_two,
    hot_one,
    hot_two,
    sent_one,
    sent_two,
    box_one,
    box_two,
    pair_maps,
    pair_split,
    pair_out,
    west_map,
    west_split,
    group_box,
    own_maps,
    z_maps,
    z_split,
    prefix_u,
    suffix_v,
    suffix_w,
    x_maps,
    x_split,
    enter_split,
    box_rhs,
    box_z,
    box_x,
    enter_y,
    enter_x,
    local_sem,
    fine_send,
    fine_recv,
    send_one,
    recv_one,
    send_two,
    recv_two,
    core_send,
    core_recv,
    west_send,
    west_recv,
    group_send,
    group_recv,
    ymap_send,
    ymap_recv,
    relay_send,
    relay_recv,
    rhs_send,
    rhs_recv,
    zmap_send,
    zmap_recv,
    xmap_send,
    xmap_recv,
    z_send,
    z_recv,
    x_send,
    x_recv,
):
    w = lax.axis_index("wide")
    q = lax.axis_index("narrow")
    seg_size = CORES * CHIPS_Z
    segs = wide_size // seg_size
    xs = w // seg_size
    zs = lax.rem(w, seg_size) // CORES
    core = lax.rem(w, CORES)

    def place(step):
        return w + step[0], q + step[1]

    def exists(step):
        a, b = place(step)
        return (a >= 0) & (a < wide_size) & (b >= 0) & (b < narrow_size)

    loads = (
        (block, ext.at[pl.ds(0, 4), pl.ds(TOP, GX), pl.ds(0, GY)]),
        (east, ext.at[4, pl.ds(TOP, GX), pl.ds(0, GY)]),
        (north, ext.at[5, pl.ds(TOP, GX), pl.ds(0, GY)]),
        (chain_forward.at[0], pair_maps.at[core, 0]),
        (chain_gain.at[0], pair_maps.at[core, 1]),
        (chain_backward.at[0], pair_maps.at[core, 2]),
        (fine_groups, groups_lo),
        (tiles_two, held_two),
        (tiles_one, held_one),
        (columns_one_in, columns_one),
        (live_one_in, live_one),
        (coarse_groups_in, coarse_groups),
        (columns_two_in, columns_two),
        (live_two_in, live_two),
        (coarser_groups_in, coarser_groups),
    )
    local = [pltpu.make_async_copy(a, b, local_sem.at[i]) for i, (a, b) in enumerate(loads)]
    barrier = pltpu.get_barrier_semaphore()
    for i in (4, 3, 5, 2, 6, 1, 7):
        mate = (xs * seg_size + lax.rem(zs + i, CHIPS_Z) * CORES + core, q)
        pl.semaphore_signal(barrier, inc=1, device_id=mate, device_id_type=MESH_ID)
    for i in range(1, segs):
        mate = (lax.rem(xs + i, segs) * seg_size + zs * CORES + core, q)
        pl.semaphore_signal(barrier, inc=1, device_id=mate, device_id_type=MESH_ID)
    awaited = jnp.int32(0)
    for step in STEPS:
        there = exists(step)
        a, b = place(step)

        @pl.when(there)
        def _():
            pl.semaphore_signal(barrier, inc=1, device_id=(a, b), device_id_type=MESH_ID)

        awaited = awaited + jnp.where(there, 1, 0)
    group = [(i, j) for i in range(CORES) for j in range(narrow_size)]
    for i, j in group[1:]:
        mate = (w - core + lax.rem(core + i, CORES), lax.rem(q + j, narrow_size))
        pl.semaphore_signal(barrier, inc=1, device_id=mate, device_id_type=MESH_ID)
    awaited = awaited + len(group) - 1 + CHIPS_Z - 1 + segs - 1

    for i in (0, 1, 2, 3, 4, 5, 14, 6, 9, 10, 11, 12, 13, 7, 8):
        local[i].start()

    def fine_start(turn, source, arrays):
        lane = iota((8, 128), 1) // 4
        for a in range(arrays):
            slabs[turn, 0, a] = source[a, TOP : TOP + 8, 0:128]
            slabs[turn, 1, a] = source[a, TOP + GX - 8 : TOP + GX, 0:128]
            packed = jnp.zeros((8, 128), F32)
            for g in range(GX // 8):
                v = source[a, TOP + 8 * g : TOP + 8 * g + 8, 0:128]
                packed = jnp.where(lane == g, v if g == 0 else pltpu.roll(v, 4 * g, 1), packed)
                packed = jnp.where(lane == 16 + g, pltpu.roll(v, (68 + 4 * g) % 128, 1), packed)
            packs[turn, a] = packed

    def fine_copy(turn, arrays, d, landing):
        span = pl.ds(0, arrays)
        source = slabs.at[turn, d, span] if d < 2 else packs.at[turn, span]
        return pltpu.make_async_remote_copy(
            src_ref=source,
            dst_ref=fine_box.at[turn, landing, span],
            send_sem=fine_send.at[turn, d],
            recv_sem=fine_recv.at[turn, landing],
            device_id=place(STEPS[d]),
            device_id_type=MESH_ID,
        )

    def fine_send_all(turn, arrays):
        for d, step in enumerate(STEPS):

            @pl.when(exists(step))
            def _():
                fine_copy(turn, arrays, d, FACING[d]).start()

    def fine_wait(turn, arrays):
        for d, step in enumerate(STEPS):

            @pl.when(exists(step))
            def _():
                fine_copy(turn, arrays, d, d).wait_recv()
                fine_copy(turn, arrays, d, FACING[d]).wait_send()

    def fine_fill(turn, target, arrays):
        lane = iota((8, 128), 1)
        there = [exists(step) for step in STEPS]

        def got(d, a):
            return jnp.where(there[d], fine_box[turn, d, a], 0.0)

        def beside(south_pack, south_group, north_pack, north_group):
            low = pltpu.roll(south_pack, (124 - 64 - 4 * south_group) % 128, 1)
            high = pltpu.roll(north_pack, (128 - 4 * north_group) % 128, 1)
            return jnp.where(lane < 4, high, jnp.where(lane >= 124, low, 0.0))

        for a in range(arrays):
            target[a, TOP - 8 : TOP, 0:128] = got(0, a)
            target[a, TOP + GX : TOP + GX + 8, 0:128] = got(1, a)
            south_pack, north_pack = got(2, a), got(3, a)
            for g in range(GX // 8):
                target[a, TOP + 8 * g : TOP + 8 * g + 8, 128:256] = beside(south_pack, g, north_pack, g)
            target[a, TOP - 8 : TOP, 128:256] = beside(got(4, a), 15, got(5, a), 15)
            target[a, TOP + GX : TOP + GX + 8, 128:256] = beside(got(6, a), 0, got(7, a), 0)

    local[0].wait()
    local[1].wait()
    local[2].wait()
    fine_start(0, ext, 6)
    pl.semaphore_wait(barrier, awaited)
    fine_send_all(0, 6)

    local[3].wait()
    local[4].wait()
    local[5].wait()

    def core_copy(landing):
        return pltpu.make_async_remote_copy(
            src_ref=pair_maps.at[core],
            dst_ref=pair_maps.at[landing],
            send_sem=core_send,
            recv_sem=core_recv,
            device_id=(w - core + (1 - core), q),
            device_id_type=MESH_ID,
        )

    def west_copy():
        return pltpu.make_async_remote_copy(
            src_ref=pair_maps.at[core, 2],
            dst_ref=west_map,
            send_sem=west_send,
            recv_sem=west_recv,
            device_id=(w + 1, q),
            device_id_type=MESH_ID,
        )

    def group_copy(d, landing):
        return pltpu.make_async_remote_copy(
            src_ref=coarser_groups,
            dst_ref=group_box.at[landing],
            send_sem=group_send.at[d],
            recv_sem=group_recv.at[landing],
            device_id=place(STEPS[d]),
            device_id_type=MESH_ID,
        )

    feeds_east = (core == CORES - 1) & (w < wide_size - 1)
    fed_from_west = (core == 0) & (w > 0)
    local[14].wait()
    core_copy(core).start()

    @pl.when(feeds_east)
    def _():
        west_copy().start()

    for d in range(4):

        @pl.when(exists(STEPS[d]))
        def _():
            group_copy(d, FACING[d]).start()


    eye_one = iota((128, 128), 0) == iota((128, 128), 1)

    def peer_copy(source, target, sends, receives, slot, landing, mate):
        return pltpu.make_async_remote_copy(
            src_ref=source,
            dst_ref=target.at[landing],
            send_sem=sends.at[slot],
            recv_sem=receives.at[landing],
            device_id=mate,
            device_id_type=MESH_ID,
        )

    def z_mate(i):
        z = lax.rem(zs + i, CHIPS_Z)
        return z, (xs * seg_size + z * CORES + core, q)

    def x_mate(i):
        x = lax.rem(xs + i, segs)
        return x, (x * seg_size + zs * CORES + core, q)

    def along(mates, count, box, sends, receives, mine):
        def start():
            for i in range(1, count):
                _, mate = mates(i)
                peer_copy(box.at[mine], box, sends, receives, i, mine, mate).start()

        def finish():
            for i in range(1, count):
                other, mate = mates(i)
                peer_copy(box.at[mine], box, sends, receives, i, other, mate).wait_recv()
                peer_copy(box.at[mine], box, sends, receives, i, mine, mate).wait_send()

        return start, finish

    z_start, z_finish = along(z_mate, CHIPS_Z, box_z, z_send, z_recv, zs)
    x_start, x_finish = along(x_mate, segs, box_x, x_send, x_recv, xs)
    z_order = (1, 7, 2, 6, 3, 5, 4)

    piece_rows = pl.ds(pl.multiple_of(192 * core + 48 * q, 16), 48)

    def zmap_copy(i, landing, mate):
        return pltpu.make_async_remote_copy(
            src_ref=own_maps.at[piece_rows],
            dst_ref=z_maps.at[landing, piece_rows],
            send_sem=zmap_send.at[i],
            recv_sem=zmap_recv.at[landing],
            device_id=mate,
            device_id_type=MESH_ID,
        )

    def ymap_copy(i, z, other):
        rows = pl.ds(pl.multiple_of(192 * core + 48 * other, 16), 48)
        return pltpu.make_async_remote_copy(
            src_ref=z_maps.at[z, rows],
            dst_ref=z_maps.at[z, rows],
            send_sem=ymap_send.at[i, z],
            recv_sem=ymap_recv.at[other, z],
            device_id=(w, lax.rem(q + i, narrow_size)),
            device_id_type=MESH_ID,
        )

    def relay_copy(side):
        half = pl.ds(pl.multiple_of(192 * side, 64), 192)
        return pltpu.make_async_remote_copy(
            src_ref=z_maps.at[:, half],
            dst_ref=z_maps.at[:, half],
            send_sem=relay_send,
            recv_sem=relay_recv,
            device_id=(w - core + (1 - core), q),
            device_id_type=MESH_ID,
        )

    def pair_products():
        core_copy(1 - core).wait_recv()
        core_copy(core).wait_send()
        f0, b0 = pair_maps[0, 0], pair_maps[0, 2]
        f1, b1 = pair_maps[1, 0], pair_maps[1, 2]
        both = matmul(f1, f0)
        own_maps[0:128] = both
        own_maps[128:256] = matmul(b0, b1)
        own_maps[256:384] = f0 + matmul(b0, both)
        z_maps[zs, piece_rows] = own_maps[piece_rows]
        for i in z_order:
            _, mate = z_mate(i)
            zmap_copy(i, zs, mate).start()

    def pair_gains():
        g0, b0 = pair_maps[0, 1], pair_maps[0, 2]
        f1, g1 = pair_maps[1, 0], pair_maps[1, 1]
        across = matmul(f1, g0)
        store_split(pair_split.at[0:128, 0:256], across)
        store_split(pair_split.at[0:128, 256:512], g1)
        store_split(pair_split.at[128:256, 0:256], g0 + matmul(b0, across))
        store_split(pair_split.at[128:256, 256:512], matmul(b0, g1))

    def ymap_start(z):
        for i in range(1, narrow_size):
            ymap_copy(i, z, q).start()

    def zmap_take(order):
        for i in order:
            other, mate = z_mate(i)
            zmap_copy(i, other, mate).wait_recv()
            zmap_copy(i, zs, mate).wait_send()
            ymap_start(other)

    def zmap_near():
        ymap_start(zs)
        zmap_take(z_order[:4])

    def zmap_far():
        zmap_take(z_order[4:])

    def zmap_relay():
        for i in range(1, narrow_size):
            for z in range(CHIPS_Z):
                ymap_copy(i, z, lax.rem(q + i, narrow_size)).wait_recv()
                ymap_copy(i, z, q).wait_send()
        relay_copy(core).start()

    def times_map(split_map, m):
        hi = m.astype(BF16)
        lo = (m - hi.astype(F32)).astype(BF16)
        lhs = jnp.concatenate([split_map, split_map[:, 0:128]], axis=1)
        return dot_nn(lhs, jnp.concatenate([hi, hi, lo], axis=0))

    def z_prefix():
        relay_copy(1 - core).wait_recv()
        relay_copy(core).wait_send()

        def split_one(p, carry):
            for j in range(3):
                store_split(z_split.at[p, j], z_maps[p, 128 * j : 128 * j + 128])
            return carry

        lax.fori_loop(0, CHIPS_Z, split_one, 0)
        one_map = jnp.where(eye_one, 1.0, 0.0)
        prefix_u[0] = one_map
        suffix_w[CHIPS_Z] = one_map

        def one(p, carry):
            prefix_u[p + 1] = times_map(z_split[p, 0], prefix_u[p])
            r = CHIPS_Z - 1 - p
            suffix_w[r] = times_map(z_split[r, 1], suffix_w[r + 1])
            return carry

        lax.fori_loop(0, CHIPS_Z, one, 0)
        x_maps[xs, 0] = prefix_u[CHIPS_Z]
        x_maps[xs, 1] = suffix_w[0]

    def xmap_copy(part, i, landing, mate):
        return pltpu.make_async_remote_copy(
            src_ref=x_maps.at[xs, part],
            dst_ref=x_maps.at[landing, part],
            send_sem=xmap_send.at[part, i],
            recv_sem=xmap_recv.at[part, landing],
            device_id=mate,
            device_id_type=MESH_ID,
        )

    def has_map(part, source, target):
        if part == 0:
            return (source > 0) & (source < segs - 1)
        if part == 1:
            return (source < segs - 1) & (target < source)
        return target < source

    def z_suffix():
        suffix_v[CHIPS_Z] = jnp.zeros((128, 128), F32)

        def one(i, carry):
            p = CHIPS_Z - 1 - i
            suffix_v[p] = times_map(z_split[p, 1], suffix_v[p + 1]) + times_map(
                z_split[p, 2], prefix_u[p]
            )
            return carry

        lax.fori_loop(0, CHIPS_Z, one, 0)
        x_maps[xs, 2] = suffix_v[0]
        for part in range(3):
            for i in range(1, segs):
                other, mate = x_mate(i)

                @pl.when(has_map(part, xs, other))
                def _():
                    xmap_copy(part, i, xs, mate).start()

    def z_composites():
        z_prefix()
        z_suffix()

    def z_splits():
        store_split(enter_split.at[0], prefix_u[zs])
        store_split(enter_split.at[1], suffix_v[zs + 1])
        store_split(enter_split.at[2], suffix_w[zs + 1])
        pair_out[0:128, 0:256] = z_split[zs, 2]
        pair_out[0:128, 256:512] = z_split[zs, 1]
        pair_out[128:256, 0:256] = z_split[zs, 0]
        store_split(pair_out.at[128:256, 256:512], pair_maps[1, 2])

        @pl.when(fed_from_west)
        def _():
            west_copy().wait_recv()

        @pl.when(feeds_east)
        def _():
            west_copy().wait_send()

        store_split(west_split, west_map[...])
        for d in range(4):

            @pl.when(exists(STEPS[d]))
            def _():
                group_copy(d, d).wait_recv()
                group_copy(d, FACING[d]).wait_send()

            mark_two(d + 1, group_box[d], q + STEPS[d][1])

    def x_splits():
        for part in range(3):
            for i in range(1, segs):
                other, mate = x_mate(i)

                @pl.when(has_map(part, other, xs))
                def _():
                    xmap_copy(part, i, other, mate).wait_recv()

                @pl.when(has_map(part, xs, other))
                def _():
                    xmap_copy(part, i, xs, mate).wait_send()

        for p in range(1, segs):
            for j in range(3):
                if j == 2 or p < segs - 1:
                    store_split(x_split.at[p, j], x_maps[p, j])

    local[6].wait()
    groups = groups_lo[...]
    groups_hi[...] = groups // 128
    groups_lo[...] = lax.rem(groups, 128)
    groups_seg[...] = groups // 256
    turned = jnp.transpose(lax.rem(groups, 256).astype(F32))
    wide_lane = iota((GY, 256), 1).astype(F32)
    for i in range(GX):
        hot = turned[:, i : i + 1] == wide_lane
        hot_fine[GY * i : GY * i + GY, :] = jnp.where(hot, 1.0, 0.0).astype(BF16)
    for i in range(9, 14):
        local[i].wait()
    for r in range(NT1):
        for k in range(3):
            spots_one[3 * r + k] = jnp.where(live_one[k, r] == 1, columns_one[k, r], 5 * NT1)
    for r in range(NT2):
        for k in range(3):
            spots_two[3 * r + k] = jnp.where(live_two[r, k] == 1, columns_two[r, k], 5 * NT2)
    picks_one[5 * NT1] = jnp.zeros((8, 128), F32)
    picks_two[5 * NT2] = jnp.zeros((8, 128), F32)
    local[7].wait()
    lane_two = iota((64, 128), 1)
    eye_two = iota((64, 128), 0) == lax.rem(lane_two, 64)
    diag_two = []
    for r in range(NT2):
        for k in range(4):
            m = held_two[r, k]
            m = jnp.concatenate([m, m], axis=1)
            if k == 0:
                diag_two.append(jnp.sum(jnp.where(eye_two, m, 0.0), axis=0, keepdims=True))
            hi = rounded(m)
            m = jnp.where(lane_two < 64, hi, m - hi).astype(BF16)
            w_two[r, 0:64, 128 * k : 128 * k + 128] = m
            w_two[r, 64:128, 128 * k : 128 * k + 128] = m
    wide_two = [jnp.broadcast_to(d, (8, 128)) for d in diag_two]
    inverse_two = 1.0 / jnp.where(
        upper(),
        jnp.where(left(), wide_two[0], wide_two[1]),
        jnp.where(left(), wide_two[2], wide_two[3]),
    )
    for t in range(NT1):
        hot = iota((256, 128), 0) == coarse_groups[t : t + 1, :]
        hot_one[:, 128 * t : 128 * t + 128] = jnp.where(hot, 1.0, 0.0).astype(BF16)

    def mark_two(p, groups, owner):
        for h in range(2):
            hot = iota((128, 128), 0) == groups[h : h + 1, :] + C3L * owner
            hot_two[p, :, 128 * h : 128 * h + 128] = jnp.where(hot, 1.0, 0.0).astype(BF16)

    mark_two(0, coarser_groups[...], q)
    pair_products()
    local[8].wait()

    def split_tiles(t, carry):
        diags = []
        for r in (t, t + 8):
            for k in range(4):
                m = held_one[r, k]
                if k == 0:
                    diags.append(jnp.sum(jnp.where(eye_one, m, 0.0), axis=0, keepdims=True))
                    store_split(w_one.at[r], m)
                else:
                    m = jnp.transpose(m)
                    hi = m.astype(BF16)
                    w_far[r, 128 * k - 128 : 128 * k, 0:128] = hi
                    w_far[r, 128 * k - 128 : 128 * k, 128:256] = (m - hi.astype(F32)).astype(BF16)
        low, high = (jnp.broadcast_to(d, (8, 128)) for d in diags)
        table[t] = 1.0 / jnp.where(upper(), low, high)
        return carry

    lax.fori_loop(0, 8, split_tiles, 0)
    inverse_one = table[...]
    pair_gains()

    fine_wait(0, 6)
    fine_fill(0, ext, 6)
    rows_all = range(8, EXT_ROWS - 8, 8)
    last_row = wide_size * GX - 1
    last_column = narrow_size * GY - 1
    lane_ext = iota((8, EXT_LANES), 1)
    column = q * GY + jnp.where(lane_ext < 192, lane_ext, lane_ext - EXT_LANES)
    for o in rows_all:
        row = w * GX + (o - TOP) + iota((8, EXT_LANES), 0)
        ext[4, o : o + 8, :] = jnp.where(row < last_row, ext[4, o : o + 8, :], 0.0)
        ext[5, o : o + 8, :] = jnp.where(column < last_column, ext[5, o : o + 8, :], 0.0)
    for o in rows_all:
        e = ext[4, o : o + 8, :]
        b = ext[4, o - 1 : o + 7, :]
        n = ext[5, o : o + 8, :]
        s = pltpu.roll(n, 1, 1)
        d = shift_value + e + b + n + s
        inv = 1.0 / d
        weight_e[o - 8 : o, :] = e * inv
        weight_w[o - 8 : o, :] = b * inv
        weight_n[o - 8 : o, :] = n * inv
        weight_s[o - 8 : o, :] = s * inv
        if TOP <= o < TOP + GX:
            diagonal[o - TOP : o - TOP + 8, :] = d[:, 0:128]
        for c in range(COLS):
            field_a[c, o : o + 8, :] = ext[c, o : o + 8, :] * inv

    def mixed(source, c, o):
        v = source[c, o : o + 8, :]
        a = weight_e[o - 8 : o, :] * source[c, o + 1 : o + 9, :]
        b = weight_w[o - 8 : o, :] * source[c, o - 1 : o + 7, :]
        n = weight_n[o - 8 : o, :] * pltpu.roll(v, EXT_LANES - 1, 1)
        s = weight_s[o - 8 : o, :] * pltpu.roll(v, 1, 1)
        return v, (a + b) + (n + s)

    rows_in = range(TOP, TOP + GX, 8)
    rest = 1.0 - jacobi_weight
    for o in rows_all:
        for c in range(COLS):
            v, m = mixed(field_a, c, o)
            field_b[c, o : o + 8, :] = rest * v + jacobi_weight * m
    for o in rows_all:
        for c in range(COLS):
            v, m = mixed(field_b, c, o)
            field_c[c, o : o + 8, :] = rest * v + jacobi_weight * m
    for o in rows_in:
        i = o - TOP
        for c in range(COLS):
            v, m = mixed(field_c, c, o)
            r = ((1.0 - smooth_weight) * v + smooth_weight * m)[:, 0:128] * diagonal[i : i + 8, :]
            both = field_a[c, o : o + 8, 0:128] + field_b[c, o : o + 8, 0:128]
            second[c, i : i + 8, :] = jacobi_weight * both
            hi = rounded(r)
            lo = r - hi
            for h in range(2):
                high_rows[pl.ds(8 * i + 4 * h + c, 8, stride=8), :] = hi
                low_rows[pl.ds(8 * i + 4 * h + c, 8, stride=8), :] = lo

    segment[...] = jnp.zeros((64, 256), F32)
    half = jnp.where(upper(), 0, 4)
    chunk = 16

    def gather_up(step, carry):
        lhs = []
        for j in range(chunk):
            i = step * chunk + j
            index = jnp.broadcast_to(groups_seg[pl.ds(i, 1), :], (8, 128))
            at = pl.multiple_of(8 * i, 8)
            v_hi = high_rows[pl.ds(at, 8), :]
            v_lo = low_rows[pl.ds(at, 8), :]
            masks = [index == half + t for t in range(4)]
            rows = [jnp.where(m, v_hi, 0.0) for m in masks] + [jnp.where(m, v_lo, 0.0) for m in masks]
            lhs.append(jnp.concatenate(rows, axis=0).astype(BF16))
        span = pl.ds(pl.multiple_of(step * (chunk * GY), chunk * GY), chunk * GY)
        segment[...] += dot_nn(jnp.concatenate(lhs, axis=1), hot_fine[span, :])
        return carry

    lax.fori_loop(0, GX // chunk, gather_up, 0, unroll=4)
    folded = segment[0:32, :] + segment[32:64, :]
    right_one = jnp.stack(
        [folded[8 * (t // 2) : 8 * (t // 2) + 8, 128 * (t % 2) : 128 * (t % 2) + 128] for t in range(8)]
    )

    def coarse_copy(sent, box, sends, receives, k, d, landing):
        return pltpu.make_async_remote_copy(
            src_ref=sent.at[k],
            dst_ref=box.at[k, landing],
            send_sem=sends.at[k, d],
            recv_sem=receives.at[k, landing],
            device_id=place(STEPS[d]),
            device_id_type=MESH_ID,
        )

    def coarse_send(bufs, k):
        for d in range(4):

            @pl.when(exists(STEPS[d]))
            def _():
                coarse_copy(*bufs, k, d, FACING[d]).start()

    def coarse_wait(bufs, k, sides=range(4)):
        for d in sides:

            @pl.when(exists(STEPS[d]))
            def _():
                coarse_copy(*bufs, k, d, d).wait_recv()
                coarse_copy(*bufs, k, d, FACING[d]).wait_send()

    bufs_one = (sent_one, box_one, send_one, recv_one)
    bufs_two = (sent_two, box_two, send_two, recv_two)

    def put_one(p, t, v):
        a, b = split_pair(v)
        picks_one[NT1 * p + t] = a
        picks_one[NT1 * p + t + 8] = b

    def apply_one(k, field, meanwhile=None):
        sent_one[k] = field
        coarse_send(bufs_one, k)
        for t in range(8):
            put_one(0, t, field[t])
        own = []
        for r in range(NT1):
            a = picks_one[r].astype(BF16)
            own.append(dot_nt(jnp.concatenate([a, a], axis=1), w_one[r]))
        own = [jnp.where(upper(), fold(own[t]), fold(own[t + 8])) for t in range(8)]
        if meanwhile is not None:
            meanwhile()
        for d in (SOUTH, NORTH, WEST, EAST):
            coarse_wait(bufs_one, k, (d,))
            there = exists(STEPS[d])
            for t in range(8):
                put_one(d + 1, t, jnp.where(there, box_one[k, d, t], 0.0))
        outs = []
        for r in range(NT1):
            parts = []
            for j in range(3):
                parts.append(picks_one[spots_one[3 * r + j]].astype(BF16))
            both = dot_nn(jnp.concatenate(parts, axis=1), w_far[r])
            outs.append(both[:, 0:128] + both[:, 128:256])
        return jnp.stack(
            [own[t] + jnp.where(upper(), fold(outs[t]), fold(outs[t + 8])) for t in range(8)]
        )

    def put_two(p, v):
        for h, a in enumerate(split_pair(v)):
            turned = pltpu.roll(a, 64, 1)
            picks_two[NT2 * p + 2 * h] = jnp.where(left(), a, turned)
            picks_two[NT2 * p + 2 * h + 1] = jnp.where(left(), turned, a)

    def apply_two(k, field, meanwhile=None):
        sent_two[k] = field
        coarse_send(bufs_two, k)
        put_two(0, field)
        if meanwhile is not None:
            meanwhile()
        coarse_wait(bufs_two, k)
        for d in range(4):
            put_two(d + 1, jnp.where(exists(STEPS[d]), box_two[k, d], 0.0))
        return product_two()

    def product_two():
        outs = []
        for r in range(NT2):
            parts = [picks_two[r]] + [picks_two[spots_two[3 * r + j]] for j in range(3)]
            lhs = jnp.concatenate([a.astype(BF16) for a in parts], axis=1)
            outs.append(fold(dot_nt(lhs, w_two[r])))
        return jnp.where(
            upper(), jnp.where(left(), outs[0], outs[1]), jnp.where(left(), outs[2], outs[3])
        )

    def down(apply_op, inv, right, windows):
        s0 = inv * right
        r1 = right - jacobi_weight * apply_op(0, s0, windows[0])
        s1 = inv * r1
        r2 = r1 - jacobi_weight * apply_op(1, s1, windows[1])
        s2 = inv * r2
        r3 = r2 - smooth_weight * apply_op(2, s2, windows[2])
        return r3, r2, jacobi_weight * (s0 + s1)

    def up(apply_op, inv, spread, applied, r2, x2):
        fix = spread - smooth_weight * (inv * applied)
        r3 = r2 - apply_op(4, fix)
        s3 = inv * r3
        r4 = r3 - jacobi_weight * apply_op(5, s3)
        return x2 + fix + jacobi_weight * s3 + jacobi_weight * (inv * r4)

    def joined(a, b):
        a, b = split_twin(a).astype(BF16), split_twin(b).astype(BF16)
        return jnp.concatenate([a, a, b, b], axis=1)

    def sweep(count, maps, box, total):
        y = box[0, 0]
        enter_y[0] = jnp.zeros((8, 128), F32)
        lifted = [box[0, 1]]
        for p in range(1, count):
            enter_y[p] = y
            lifted.append(box[p, 1] + times(y, maps[p, 2]))
            if total or p < count - 1:
                y = box[p, 0] + times(y, maps[p, 0])
        x = lifted[count - 1]
        enter_x[count - 1] = jnp.zeros((8, 128), F32)
        for p in reversed(range(count - 1)):
            enter_x[p] = x
            if total or p > 0:
                x = lifted[p] + times(x, maps[p, 1])
        return y, x

    def chain_solve(piece):
        slot = core * narrow_size + q
        box_rhs[slot] = piece

        def rhs_copy(i, j, landing):
            mate = (w - core + lax.rem(core + i, CORES), lax.rem(q + j, narrow_size))
            return peer_copy(
                box_rhs.at[slot], box_rhs, rhs_send, rhs_recv, i * narrow_size + j, landing, mate
            )

        for i, j in group[1:]:
            rhs_copy(i, j, slot).start()
        z_splits()
        for i, j in group[1:]:
            other = lax.rem(core + i, CORES) * narrow_size + lax.rem(q + j, narrow_size)
            rhs_copy(i, j, other).wait_recv()
            rhs_copy(i, j, slot).wait_send()
        sums = []
        for i in range(CORES):
            total = box_rhs[i * narrow_size]
            for j in range(1, narrow_size):
                total = total + box_rhs[i * narrow_size + j]
            sums.append(total)
        both = fold(dot_nt(joined(*sums), pair_split[...]))
        ahead, behind = both[:, 0:128], both[:, 128:256]
        box_z[zs, 0] = ahead
        box_z[zs, 1] = behind
        z_start()
        z_finish()
        y, x = sweep(CHIPS_Z, z_split, box_z, True)
        box_x[xs, 0] = y
        box_x[xs, 1] = x
        x_start()
        y_in, x_in = enter_y[zs], enter_x[zs]
        x_splits()
        x_finish()
        sweep(segs, x_split, box_x, False)
        y_far, x_far = enter_y[xs], enter_x[xs]
        y_in = y_in + times(y_far, enter_split[0])
        x_in = x_in + times(y_far, enter_split[1]) + times(x_far, enter_split[2])
        both = fold(dot_nt(joined(y_in, x_in), pair_out[...]))
        x_first, x_last = behind + both[:, 0:128], ahead + both[:, 128:256]
        x_before = y_in + times(x_first, west_split[...])
        inner = core == 0
        return (
            jnp.where(inner, x_first, x_last),
            jnp.where(inner, x_before, x_first),
            jnp.where(inner, x_last, x_in),
        )

    def halves(pair):
        return jnp.concatenate([a.astype(BF16) for a in pair], axis=1)

    def pack_two(o):
        o = fold(o)
        return jnp.where(upper(), o[:, 0:128], o[:, 128:256])

    def restrict_one(field):
        pairs = [split_pair(field[t]) for t in range(8)]
        tiles = [p[0] for p in pairs] + [p[1] for p in pairs]
        return pack_two(dot_nt(halves(tiles), hot_one[...]))

    def prolong_one(coarse):
        o = fold(dot_nn(halves(split_pair(coarse)), hot_one[...]))
        parts = [o[:, 128 * t : 128 * t + 128] for t in range(NT1)]
        return jnp.stack([jnp.where(upper(), parts[t], parts[t + 8]) for t in range(8)])

    r_one, r2_one, x2_one = down(apply_one, inverse_one, right_one, (zmap_near, zmap_far, None))
    right_two = restrict_one(r_one)
    r_two, r2_two, x2_two = down(apply_two, inverse_two, right_two, (zmap_relay, z_composites, None))
    piece = fold(dot_nt(halves(split_pair(r_two)), hot_two[0]))
    answers = chain_solve(piece)

    def spread_two(p, answer):
        return pack_two(dot_nn(split_twin(answer).astype(BF16), hot_two[p]))

    spread = spread_two(0, answers[0])
    put_two(0, spread)
    for d, answer in enumerate((answers[1], answers[2], answers[0], answers[0])):
        put_two(d + 1, jnp.where(exists(STEPS[d]), spread_two(d + 1, answer), 0.0))
    answer_two = up(apply_two, inverse_two, spread, product_two(), r2_two, x2_two)
    spread = prolong_one(answer_two)
    answer_one = up(apply_one, inverse_one, spread, apply_one(3, spread), r2_one, x2_one)
    table[...] = answer_one

    def spread_rows(k, carry):
        at = pl.multiple_of(8 * k, 8)
        hi_index = groups_hi[pl.ds(at, 8), :]
        lo_index = groups_lo[pl.ds(at, 8), :]
        for c in range(COLS):
            total = jnp.zeros((8, 128), F32)
            for t in range(NT1):
                j = 4 * (t // 8) + c
                row = jnp.broadcast_to(table[t % 8, j : j + 1, :], (8, 128))
                value = jnp.take_along_axis(row, lo_index, axis=1, mode="promise_in_bounds")
                total = jnp.where(hi_index == t, value, total)
            field_a[c, pl.ds(pl.multiple_of(TOP + at, 8), 8), 0:128] = total
        return carry

    lax.fori_loop(0, GX // 8, spread_rows, 0, unroll=4)
    fine_start(1, field_a, 4)
    fine_send_all(1, 4)
    fine_wait(1, 4)
    fine_fill(1, field_a, 4)
    for o in rows_all:
        for c in range(COLS):
            v, m = mixed(field_a, c, o)
            field_b[c, o : o + 8, :] = (1.0 - smooth_weight) * v + smooth_weight * m
    for o in rows_all:
        for c in range(COLS):
            v, m = mixed(field_b, c, o)
            field_a[c, o : o + 8, :] = field_c[c, o : o + 8, :] - v + m
    for o in rows_in:
        i = o - TOP
        for c in range(COLS):
            v, m = mixed(field_a, c, o)
            x3 = second[c, i : i + 8, :] + field_b[c, o : o + 8, 0:128]
            s4 = rest * v + jacobi_weight * m
            out[c, i : i + 8, :] = x3 + jacobi_weight * (v + s4)[:, 0:128]


def solution(mesh):
    wide_size, narrow_size = mesh.shape["wide"], mesh.shape["narrow"]
    segs = wide_size // (CORES * CHIPS_Z)

    def body(
        block,
        east,
        north,
        fine_groups,
        tiles_one,
        columns_one,
        live_one,
        coarse_groups,
        tiles_two,
        columns_two,
        live_two,
        coarser_groups,
        chain_forward,
        chain_gain,
        chain_backward,
    ):
        hbm = pl.BlockSpec(memory_space=pl.ANY)
        vmem = pl.BlockSpec(memory_space=pltpu.VMEM)
        dma = pltpu.SemaphoreType.DMA
        big = pltpu.VMEM((COLS, EXT_ROWS, EXT_LANES), F32)
        weight = pltpu.VMEM((EXT_ROWS - 16, EXT_LANES), F32)
        square = pltpu.VMEM((GX, GY), F32)
        indices = pltpu.VMEM((GX, GY), jnp.int32)

        def kernel_fn(*refs):
            kernel(wide_size, narrow_size, *refs)

        return pl.pallas_call(
            kernel_fn,
            out_shape=pltpu.VMEM((COLS, GX, GY), F32),
            in_specs=[hbm] * 15,
            out_specs=vmem,
            scratch_shapes=[
                pltpu.SMEM((3, NT1), jnp.int32),
                pltpu.SMEM((3, NT1), jnp.int32),
                pltpu.VMEM((16, 128), jnp.int32),
                pltpu.SMEM((NT2, 3), jnp.int32),
                pltpu.SMEM((NT2, 3), jnp.int32),
                pltpu.VMEM((2, 128), jnp.int32),
                pltpu.VMEM((6, EXT_ROWS, EXT_LANES), F32),
                indices,
                indices,
                pltpu.VMEM((NT1, 4, 128, 128), F32),
                pltpu.VMEM((NT2, 4, 64, 64), F32),
                pltpu.VMEM((2, 2, 6, 8, 128), F32),
                pltpu.VMEM((2, 6, 8, 128), F32),
                pltpu.VMEM((2, 8, 6, 8, 128), F32),
                weight,
                weight,
                weight,
                weight,
                weight,
                square,
                big,
                big,
                big,
                pltpu.VMEM((COLS, GX, GY), F32),
                pltpu.VMEM((8 * GX, GY), F32),
                pltpu.VMEM((8 * GX, GY), F32),
                pltpu.VMEM((64, 256), F32),
                pltpu.VMEM((8, 8, 128), F32),
                pltpu.VMEM((NT1, 128, 256), BF16),
                pltpu.VMEM((NT1, 384, 256), BF16),
                pltpu.VMEM((GX * GY, 256), BF16),
                indices,
                pltpu.VMEM((NT2, 128, 512), BF16),
                pltpu.VMEM((5 * NT1 + 1, 8, 128), F32),
                pltpu.VMEM((5 * NT2 + 1, 8, 128), F32),
                pltpu.SMEM((3 * NT1,), jnp.int32),
                pltpu.SMEM((3 * NT2,), jnp.int32),
                pltpu.VMEM((256, 2048), BF16),
                pltpu.VMEM((5, 128, 256), BF16),
                pltpu.VMEM((6, 8, 8, 128), F32),
                pltpu.VMEM((6, 8, 128), F32),
                pltpu.VMEM((6, 4, 8, 8, 128), F32),
                pltpu.VMEM((6, 4, 8, 128), F32),
                pltpu.VMEM((CORES, 3, 128, 128), F32),
                pltpu.VMEM((256, 512), BF16),
                pltpu.VMEM((256, 512), BF16),
                square,
                pltpu.VMEM((128, 256), BF16),
                pltpu.VMEM((4, 2, 128), jnp.int32),
                pltpu.VMEM((384, 128), F32),
                pltpu.VMEM((CHIPS_Z, 384, 128), F32),
                pltpu.VMEM((CHIPS_Z, 3, 128, 256), BF16),
                pltpu.VMEM((CHIPS_Z + 1, 128, 128), F32),
                pltpu.VMEM((CHIPS_Z + 1, 128, 128), F32),
                pltpu.VMEM((CHIPS_Z + 1, 128, 128), F32),
                pltpu.VMEM((segs, 3, 128, 128), F32),
                pltpu.VMEM((segs, 3, 128, 256), BF16),
                pltpu.VMEM((3, 128, 256), BF16),
                pltpu.VMEM((CORES * narrow_size, 8, 128), F32),
                pltpu.VMEM((CHIPS_Z, 2, 8, 128), F32),
                pltpu.VMEM((segs, 2, 8, 128), F32),
                pltpu.VMEM((CHIPS_Z, 8, 128), F32),
                pltpu.VMEM((CHIPS_Z, 8, 128), F32),
                dma((15,)),
                dma((2, 8)),
                dma((2, 8)),
                dma((6, 4)),
                dma((6, 4)),
                dma((6, 4)),
                dma((6, 4)),
                dma,
                dma,
                dma,
                dma,
                dma((4,)),
                dma((4,)),
                dma((narrow_size, CHIPS_Z)),
                dma((narrow_size, CHIPS_Z)),
                dma,
                dma,
                dma((CORES * narrow_size,)),
                dma((CORES * narrow_size,)),
                dma((CHIPS_Z,)),
                dma((CHIPS_Z,)),
                dma((3, segs)),
                dma((3, segs)),
                dma((CHIPS_Z,)),
                dma((CHIPS_Z,)),
                dma((segs,)),
                dma((segs,)),
            ],
            compiler_params=pltpu.CompilerParams(
                collective_id=0, has_side_effects=True, vmem_limit_bytes=56 * 1024 * 1024
            ),
            name="cycle",
        )(
            block,
            east,
            north,
            fine_groups,
            tiles_one,
            columns_one.T,
            live_one.T,
            coarse_groups.reshape(16, 128),
            tiles_two,
            columns_two,
            live_two,
            coarser_groups.reshape(2, 128),
            chain_forward,
            chain_gain,
            chain_backward,
        )

    both = ("wide", "narrow")
    placed = (
        P(None, "wide", "narrow"),
        P("wide", "narrow"),
        P("wide", "narrow"),
        P("wide", "narrow"),
        P(both, None, None, None),
        P(both, None),
        P(both, None),
        P(both),
        P(both, None, None, None),
        P(both, None),
        P(both, None),
        P(both),
        P("wide", None, None),
        P("wide", None, None),
        P("wide", None, None),
    )
    return jax.shard_map(
        body, mesh=mesh, in_specs=placed, out_specs=P(None, "wide", "narrow"), check_vma=False
    )
```
